128 devices in a mesh: req: 64 (over y, z, x_hi, core), tp: 2 (over x_lo).
Axes of the slice: x: 4 (x_hi: 2, x_lo: 2; x = x_hi * 2 + x_lo), y: 4, z: 4, core: 2. Of those that a mesh axis runs over, the one named last changes fastest.
Arguments:
- residual: bfloat16 [8192, 2048], P('req'), may hold values from -6 to 6
- queries: bfloat16 [8192, 1024], P('req', 'tp'), may hold values from -6 to 6
- new_keys: bfloat16 [8192, 1024], P('req', 'tp'), may hold values from -6 to 6
- new_values: bfloat16 [8192, 1024], P('req', 'tp'), may hold values from -6 to 6
- request_ids: int32 [8192], P('req'), may hold values from 0 to 3, as said below
- page_store: bfloat16 [512, 2, 128, 1024], P('req', None, None, 'tp'), may hold values from -6 to 6
- page_sends: int32 [64, 64], P('req'), may hold values from 0 to 7
- page_users: int32 [64, 64], P('req'), may hold values from -1 to 3
- expert_ids: int32 [8192, 4], P('req'), may hold values from 0 to 63, all different within a row; in each aligned block of 128 rows (0 to 127, 128 to 255, ...) at most 12 rows name the same one
- expert_weights: float32 [8192, 4], P('req'), may hold values from 0.1 to 1
- output_weight: bfloat16 [1024, 2048], P('tp'), may hold values from -0.1875 to 0.1875
- norm_gain: float32 [2048], replicated, may hold values from 0.1 to 1.9
- gate_weight: bfloat16 [64, 2048, 1408], P('req', None, 'tp'), may hold values from -0.125 to 0.125
- up_weight: bfloat16 [64, 2048, 1408], P('req', None, 'tp'), may hold values from -0.125 to 0.125
- down_weight: bfloat16 [64, 1408, 2048], P('req', 'tp'), may hold values from -0.15625 to 0.15625
Outputs:
- layer_out: bfloat16 [8192, 2048], P('req', 'tp')
The draws below stay inside these ranges and needn't reach their ends.
Inputs may be any that keep to these rules, and one draw needn't show every extreme that they name: `request_ids`: within each device's 128 tokens the local requests 0 to 3 each appear, in order, in whole runs of 16 tokens that start at multiples of 16. `page_users`: -1 marks a fetched page that no local request uses. `expert_ids`: the 4 experts of a token differ; within the 128 rows of one device no expert is named more than 12 times.
All inputs are finite; a program needn't handle non-finite values.
Results may differ from the reference program's by a relative error of at most 0.0054.
Values may be sent and summed in bfloat16 or wider, within the bound.
No kernel may reach another device: no remote copies, remote signals or barrier semaphores. Data moves between devices by JAX's collectives and lax.ppermute only.
A program may use at most 192 MiB of HBM per device.

```python
import math
import jax
import jax.numpy as jnp
import numpy as np
from jax import lax

D = 2048
HD = 128
FFE = 1408
HEADS = 8
TOP = 4
PAGE = 128
REQ_DEV = 4
TOK_DEV = 128
POOL_DEV = 8
EXPERTS = 64
CAP = 12
TOKENS = 8192
POOL = 512
N_REQ = 64


def paired_rows(key):
    base_key = jax.random.fold_in(key, 7)
    shape = (TOKENS, HEADS * HD)
    first = jnp.clip(jax.random.normal(jax.random.fold_in(base_key, 1), shape, jnp.float32), -6.0, 6.0)
    second = jnp.clip(jax.random.normal(jax.random.fold_in(base_key, 2), shape, jnp.float32), -6.0, 6.0)
    return (first, second)


def draw_queries(key, part):
    first, second = paired_rows(key)
    return first.astype(jnp.bfloat16)


def draw_new_keys(key, part):
    first, second = paired_rows(key)
    return second.astype(jnp.bfloat16)


def draw_request_ids(key, part):
    device_count = TOKENS // TOK_DEV
    block_count = TOK_DEV // 16
    raw = jax.random.randint(jax.random.fold_in(key, 11), (device_count, block_count - 1), 0, 1 << 20)
    scores = raw * (block_count - 1) + jnp.arange(block_count - 1, dtype=jnp.int32)[None, :]
    chosen_pos = jnp.argsort(scores, axis=1)[:, :REQ_DEV - 1]
    row_pick = jnp.broadcast_to(jnp.arange(device_count, dtype=jnp.int32)[:, None], chosen_pos.shape)
    chosen = jnp.zeros((device_count, block_count - 1), jnp.int32).at[row_pick, chosen_pos].set(1)
    block_ids = jnp.concatenate([jnp.zeros((device_count, 1), jnp.int32), jnp.cumsum(chosen, axis=1)], axis=1)
    return jnp.repeat(block_ids, 16, axis=1).reshape(TOKENS).astype(jnp.int32)


def place_ends(array, rng, least, largest):
    index_at = [jax.random.randint(jax.random.fold_in(rng, axis), (), 0, length) for axis, length in enumerate(array.shape)]
    main_axis = array.shape.index(max(array.shape))
    next_to = index_at[:main_axis] + [(index_at[main_axis] + 1) % array.shape[main_axis]] + index_at[main_axis + 1:]
    return array.at[tuple(index_at)].set(least).at[tuple(next_to)].set(largest)


def steps_of(own_key, dims, shards, low, largest):
    level = 1.0
    for position, parts in shards:
        draws = jax.random.uniform(jax.random.fold_in(jax.random.fold_in(own_key, 6), position), (parts,), jnp.float32, low / len(shards), largest / len(shards))
        level = level * jnp.repeat(jnp.exp(draws), dims[position] // parts).reshape((-1,) + (1,) * (len(dims) - 1 - position))
    return level


def routed_block(stream_key, own, number, rows, number_of, top, most, skew):
    sequence = jax.random.permutation(stream_key, number_of)
    heavy_load, ordinary = shares(number_of, rows * top, most, skew, True), shares(number_of, rows * top, most, skew, False)
    places = jnp.arange(number_of)

    def named(sizes, rotation):
        used = int((sizes > 0).sum())
        fixed = max(1, used // 4)
        moved = fixed + (places - fixed + rotation * (used - fixed)) % max(1, number_of - fixed)
        return jnp.zeros((number_of,), jnp.int32).at[sequence[jnp.where(places < fixed, places, moved)]].set(jnp.asarray(sizes, jnp.int32))

    sizes = jnp.where(number % 4 == 0, named(heavy_load, number // 4), named(ordinary, number - number // 4 - 1))
    mixed = jax.random.permutation(jax.random.fold_in(own, 3), number_of)
    giver, receiver = mixed[0:number_of // 2 * 2:2], mixed[1:number_of // 2 * 2:2]
    slack = jnp.minimum(sizes[giver] - 1, most - sizes[receiver]) // 2
    slack = jnp.where((giver == sequence[0]) | (receiver == sequence[0]) | (sizes[receiver] == 0), 0, jnp.maximum(slack, 0))
    moved = jax.random.randint(jax.random.fold_in(own, 4), (number_of // 2,), 0, 1 << 20) % (slack + 1)
    sizes = sizes.at[giver].add(-moved).at[receiver].add(moved)
    items = jnp.searchsorted(jnp.cumsum(sizes), jnp.arange(rows * top), side="right").astype(jnp.int32)
    listing = items.reshape(top, rows).T
    listing = listing[jax.random.permutation(jax.random.fold_in(own, 1), rows)]
    rotation = jax.random.randint(jax.random.fold_in(own, 2), (rows, 1), 0, top)
    return jnp.take_along_axis(listing, (jnp.arange(top)[None, :] + rotation) % top, axis=1)


def shares(number_of, total, limit, skew, full):
    portions = [(1 << 20) // math.isqrt(grade ** skew) + 1 for grade in range(1, number_of + 1)]
    largest = limit if full else min(limit, max(-(-total // number_of), total * portions[0] // sum(portions)))
    least = 1 if total - largest >= number_of - 1 else 0
    holding, spare = [largest] + [least] * (number_of - 1), total - largest - least * (number_of - 1)
    while spare > 0:
        movable = [i for i in range(1, number_of) if holding[i] < largest] or [i for i in range(1, number_of) if holding[i] < limit]
        whole, budget = sum([portions[i] for i in movable]), spare
        for i in movable:
            more = min(limit - holding[i], max(1, budget * portions[i] // whole), spare)
            holding[i] = holding[i] + more
            spare = spare - more
    return np.array(holding)


def scatter_about(stream_key, dims, deviation, bound, shards=(), held_as=jnp.bfloat16):
    values = deviation * jax.random.normal(stream_key, dims, jnp.float32)
    if shards:
        values = values * steps_of(stream_key, dims, shards, -0.22, 0.18)
    return jnp.clip(values, -bound, bound).astype(held_as)


def setup_inputs(seed: int = 0) -> dict:
    keys = jax.random.split(jax.random.key(seed), 16)
    residual = scatter_about(keys[0], (TOKENS, D), 1.0, 6.0, ((0, 64),))
    queries = draw_queries(jax.random.fold_in(keys[15], 71), 0)
    new_keys = draw_new_keys(jax.random.fold_in(keys[15], 71), 0)
    new_values = scatter_about(keys[3], (TOKENS, HEADS * HD), 1.0, 6.0, ((0, 64), (1, 2)))
    request_ids = draw_request_ids(jax.random.fold_in(keys[15], 71), 0)
    page_store = scatter_about(keys[5], (POOL, 2, PAGE, HEADS * HD), 1.0, 6.0, ((0, 64), (3, 2)))
    page_sends = place_ends(jax.random.randint(keys[6], (N_REQ, N_REQ), 0, POOL_DEV), jax.random.fold_in(keys[6], 1), 0, POOL_DEV - 1).astype(jnp.int32)
    page_users = place_ends(jax.random.randint(keys[7], (N_REQ, N_REQ), -1, REQ_DEV), jax.random.fold_in(keys[7], 1), -1, REQ_DEV - 1).astype(jnp.int32)
    expert_ids_keys = jax.random.split(jax.random.fold_in(keys[8], 1), TOKENS // TOK_DEV)
    expert_ids_turns = jax.random.permutation(jax.random.fold_in(keys[8], 3), TOKENS // TOK_DEV)
    expert_ids = jax.vmap(lambda own, number: routed_block(jax.random.fold_in(keys[8], 2), own, number, TOK_DEV, EXPERTS, TOP, CAP, 2))(expert_ids_keys, expert_ids_turns).reshape((TOKENS, TOP))
    expert_weights = jnp.clip(jnp.exp(math.log(1.0) - 2.3025851 * jax.random.uniform(keys[9], (TOKENS, TOP), jnp.float32) ** steps_of(keys[9], (TOKENS, TOP), ((0, 64),), -0.2, 0.2)), 0.1, 1.0)
    output_weight = scatter_about(keys[10], (HEADS * HD, D), (HEADS * HD) ** -0.5, 0.1875, ((0, 2),))
    norm_gain = jnp.clip(1.0 + 0.18 * jax.random.normal(keys[11], (D,), jnp.float32), 0.1, 1.9)
    gate_weight = scatter_about(keys[12], (EXPERTS, D, FFE), D ** -0.5, 0.125, ((0, 64), (2, 2)))
    up_weight = scatter_about(keys[13], (EXPERTS, D, FFE), D ** -0.5, 0.125, ((0, 64), (2, 2)))
    down_weight = scatter_about(keys[14], (EXPERTS, FFE, D), FFE ** -0.5, 0.15625, ((0, 64), (1, 2)))
    return {"residual": residual, "queries": queries, "new_keys": new_keys, "new_values": new_values, "request_ids": request_ids, "page_store": page_store, "page_sends": page_sends, "page_users": page_users, "expert_ids": expert_ids, "expert_weights": expert_weights, "output_weight": output_weight, "norm_gain": norm_gain, "gate_weight": gate_weight, "up_weight": up_weight, "down_weight": down_weight}


norm_eps = 1e-06

def attend_device(device, queries, new_keys, new_values, request_ids, page_store, page_sends, page_users):
    row_start = device * TOK_DEV
    query_rows = lax.dynamic_slice_in_dim(queries, row_start, TOK_DEV, 0)
    key_rows = lax.dynamic_slice_in_dim(new_keys, row_start, TOK_DEV, 0)
    value_rows = lax.dynamic_slice_in_dim(new_values, row_start, TOK_DEV, 0)
    own_ids = lax.dynamic_slice_in_dim(request_ids, row_start, TOK_DEV, 0)
    page_index = jnp.arange(N_REQ, dtype=jnp.int32) * POOL_DEV + page_sends[:, device]
    fetched = page_store[page_index]
    all_keys = jnp.concatenate([fetched[:, 0].reshape(N_REQ * PAGE, HEADS * HD), key_rows], 0).reshape(-1, HEADS, HD)
    all_values = jnp.concatenate([fetched[:, 1].reshape(N_REQ * PAGE, HEADS * HD), value_rows], 0).reshape(-1, HEADS, HD)
    slot_users = page_users[device]
    key_request = jnp.concatenate([jnp.repeat(slot_users, PAGE), own_ids])
    key_place = jnp.concatenate([jnp.full((N_REQ * PAGE,), -1, jnp.int32), jnp.arange(TOK_DEV, dtype=jnp.int32)])
    query_place = jnp.arange(TOK_DEV, dtype=jnp.int32)
    allowed = (key_request[None, :] == own_ids[:, None]) & (key_place[None, :] <= query_place[:, None])
    query_heads = query_rows.reshape(TOK_DEV, HEADS, HD)
    scores = jnp.einsum('qhd,khd->hqk', query_heads.astype(jnp.float32), all_keys.astype(jnp.float32))
    scores = scores * (1.0 / math.sqrt(HD))
    masked = jnp.where(allowed[None], scores, -1e+30)
    top_score = lax.optimization_barrier(jnp.max(masked, axis=2, keepdims=True))
    shifted = jnp.where(allowed[None], jnp.exp(masked - top_score), 0.0)
    totals = lax.optimization_barrier(jnp.sum(shifted, axis=2, keepdims=True))
    attn_probs = (shifted / totals).astype(jnp.bfloat16)
    attended = jnp.einsum('hqk,khd->qhd', attn_probs.astype(jnp.float32), all_values.astype(jnp.float32))
    return attended.astype(jnp.bfloat16).reshape(TOK_DEV, HEADS * HD)

def reference(residual, queries, new_keys, new_values, request_ids, page_store, page_sends, page_users, expert_ids, expert_weights, output_weight, norm_gain, gate_weight, up_weight, down_weight):

    def one_device(device):
        return attend_device(device, queries, new_keys, new_values, request_ids, page_store, page_sends, page_users)
    attended = lax.map(one_device, jnp.arange(N_REQ, dtype=jnp.int32)).reshape(TOKENS, HEADS * HD)
    mixed_rows = residual.astype(jnp.float32) + jnp.dot(attended, output_weight, preferred_element_type=jnp.float32)
    scale_row = lax.rsqrt(lax.optimization_barrier(jnp.mean(mixed_rows * mixed_rows, axis=1, keepdims=True)) + norm_eps)
    normed = (mixed_rows * scale_row * norm_gain).astype(jnp.bfloat16)
    expert_flat = expert_ids.reshape(N_REQ, TOK_DEV * TOP)
    onehot = (expert_flat[:, :, None] == jnp.arange(EXPERTS, dtype=jnp.int32)).astype(jnp.int32)
    before = jnp.cumsum(onehot, axis=1) - onehot
    slot_index = lax.optimization_barrier(jnp.sum(before * onehot, axis=2))
    pick_index = jnp.arange(N_REQ * TOK_DEV * TOP, dtype=jnp.int32).reshape(N_REQ, TOK_DEV * TOP)
    device_index = jnp.broadcast_to(jnp.arange(N_REQ, dtype=jnp.int32)[:, None], (N_REQ, TOK_DEV * TOP))
    slot_table = jnp.full((EXPERTS, N_REQ, CAP), -1, jnp.int32).at[expert_flat, device_index, slot_index].set(pick_index)
    weights_flat = expert_weights.reshape(-1)

    def expert_step(running, expert):
        pick_rows = slot_table[expert].reshape(-1)
        is_valid = pick_rows >= 0
        safe_picks = jnp.maximum(pick_rows, 0)
        token_rows = safe_picks // TOP
        input_rows = jnp.where(is_valid[:, None], normed[token_rows], jnp.zeros((), jnp.bfloat16))
        gate_act = jnp.dot(input_rows, gate_weight[expert], preferred_element_type=jnp.float32)
        up_act = jnp.dot(input_rows, up_weight[expert], preferred_element_type=jnp.float32)
        hidden = (jax.nn.silu(gate_act) * up_act).astype(jnp.bfloat16)
        result = jnp.dot(hidden, down_weight[expert], preferred_element_type=jnp.float32)
        scaled = result * jnp.where(is_valid, weights_flat[safe_picks], 0.0)[:, None]
        return (running.at[token_rows].add(scaled), None)
    moe_sum, unused = lax.scan(expert_step, jnp.zeros((TOKENS, D), jnp.float32), jnp.arange(EXPERTS, dtype=jnp.int32))
    return (mixed_rows + moe_sum).astype(jnp.bfloat16)
```

```python
import math

import jax
import jax.numpy as jnp
import numpy as np
from jax import lax
from jax.experimental import pallas as pl
from jax.experimental.pallas import tpu as pltpu
from jax.sharding import PartitionSpec as P

HD = 128
TOP = 4
HEADS = 4
PAGE = 128
TOK = 128
REQS = 4
WIN = 80
CAP = 12
STAT = HEADS * WIN
BLOCK = STAT + 8
GROUPS = WIN // 8
QROWS = TOK + 8
NORM_EPS = 1e-06
SCALE = 1.0 / math.sqrt(HD)
NEG = -1e30
F32 = jnp.float32
BF16 = jnp.bfloat16

NY, NZ, NX, NC = 4, 4, 2, 2
NREQ = NY * NZ * NX * NC


def req_index(y, z, x, c):
    return ((y * NZ + z) * NX + x) * NC + c


def all_coords():
    return [
        (y, z, x, c) for y in range(NY) for z in range(NZ) for x in range(NX) for c in range(NC)
    ]


def perm_x():
    return [(req_index(y, z, x, c), req_index(y, z, 1 - x, c)) for y, z, x, c in all_coords()]


def perm_core():
    return [(req_index(y, z, x, c), req_index(y, z, x, 1 - c)) for y, z, x, c in all_coords()]


def perm_ring(stage, step):
    pairs = []
    for y, z, x, c in all_coords():
        if (c + stage) % 2 == 0:
            to = req_index((y + step) % NY, z, x, c)
        else:
            to = req_index(y, (z + step) % NZ, x, c)
        pairs.append((req_index(y, z, x, c), to))
    return pairs


def source_table():
    table = np.zeros((NREQ, NREQ), np.int32)
    for y, z, x, c in all_coords():
        row = []
        for swap in range(2):
            core = c ^ swap
            for d1 in range(4):
                for d0 in range(4):
                    for dx in range(2):
                        dy, dz = (d0, d1) if core == 0 else (d1, d0)
                        row.append(req_index((y - dy) % NY, (z - dz) % NZ, x ^ dx, core))
        table[req_index(y, z, x, c)] = row
    return table


def gather_blocks(block):
    pair = jnp.stack([block, lax.ppermute(block, "req", perm_x())])
    line = jnp.stack(
        [pair] + [lax.ppermute(pair, "req", perm_ring(0, step)) for step in (1, 2, 3)]
    ).reshape(8, *block.shape)
    own = [line] + [lax.ppermute(line, "req", perm_ring(1, step)) for step in (1, 2, 3)]
    other = [lax.ppermute(piece, "req", perm_core()) for piece in own]
    return own + other


def attend(query_of, key_of, value_of, mask=None):
    outs, sums = [], []
    for head in range(HEADS):
        scores = lax.dot_general(
            query_of(head), key_of(head), (((1,), (0,)), ((), ())), preferred_element_type=F32
        )
        if mask is not None:
            scores = jnp.where(mask, scores, NEG)
        top = jnp.max(scores, axis=1, keepdims=True)
        probs = jnp.exp((scores - top) * SCALE).astype(BF16)
        both = jnp.dot(probs, value_of(head), preferred_element_type=F32)
        total = both[:, HD:]
        outs.append(both[:, :HD] / total)
        sums.append(top * SCALE + jnp.log(total))
    return outs, sums


def pack_sums(sums):
    lane = lax.broadcasted_iota(jnp.int32, (WIN, 128), 1)
    head = lane % 4
    mixed = jnp.where(head == 0, sums[0], sums[1])
    mixed = jnp.where(head == 2, sums[2], mixed)
    mixed = jnp.where(head == 3, sums[3], mixed)
    group = (lax.broadcasted_iota(jnp.int32, (8, 128), 1) % 40) // 4
    tile = mixed[0:8]
    for g in range(1, GROUPS):
        tile = jnp.where(group == g, mixed[8 * g : 8 * g + 8], tile)
    return tile


def split_sums(tile):
    lane = lax.broadcasted_iota(jnp.int32, (8, 128), 1)
    first = tile.astype(BF16).astype(F32)
    rest = tile - first
    second = rest.astype(BF16).astype(F32)
    third = rest - second
    return jnp.where(lane < 40, first, jnp.where(lane < 80, second, third)).astype(BF16)


def page_kernel(src, page_of, win_of, *refs):
    pieces, (pages, out, keys_t, values_1) = refs[:8], refs[8:]
    ones = jnp.ones((PAGE, HD), BF16)
    for page in range(8):
        for head in range(HEADS):
            cols = slice(head * HD, (head + 1) * HD)
            keys_t[page, head] = pages[page, 0, :, cols].T
            values_1[page, head, :, :HD] = pages[page, 1, :, cols]
            values_1[page, head, :, HD:] = ones
    for index, piece in enumerate(pieces):

        def step(i, carry, index=index, piece=piece):
            b = index * 8 + i
            page = page_of[b]
            first = pl.multiple_of(win_of[b] * 16, 16)
            to = src[b]
            outs, sums = attend(
                lambda h: piece[i, pl.ds(first, WIN), h * HD : (h + 1) * HD],
                lambda h: keys_t[page, h],
                lambda h: values_1[page, h],
            )
            for head in range(HEADS):
                out[to, head * WIN : (head + 1) * WIN, :] = outs[head].astype(BF16)
            out[to, STAT:BLOCK, :] = split_sums(pack_sums(sums))
            return carry

        lax.fori_loop(0, 8, step, 0)


def smem():
    return pl.BlockSpec(memory_space=pltpu.SMEM)


def vmem():
    return pl.BlockSpec(memory_space=pltpu.VMEM)


def partial_attention(src, page_of, win_of, pieces, pages):
    return pl.pallas_call(
        page_kernel,
        out_shape=jax.ShapeDtypeStruct((NREQ, BLOCK, HD), BF16),
        in_specs=[smem()] * 3 + [vmem()] * 9,
        out_specs=vmem(),
        scratch_shapes=[
            pltpu.VMEM((8, HEADS, HD, PAGE), BF16),
            pltpu.VMEM((8, HEADS, PAGE, 2 * HD), BF16),
        ],
        compiler_params=pltpu.CompilerParams(vmem_limit_bytes=48 << 20),
        cost_estimate=pl.CostEstimate(
            flops=NREQ * HEADS * 6 * WIN * HD * HD, bytes_accessed=18 << 20, transcendentals=3 << 20
        ),
        name="page_attention",
    )(src, page_of, win_of, *pieces, pages)


def spread(tile, head, k):
    halves = []
    for g in (2 * k, 2 * k + 1):
        lane = g * 4 + head
        halves.append(jnp.broadcast_to(tile[:, lane : lane + 1], (8, 128)))
    return jnp.concatenate(halves, axis=0)


def merge_kernel(
    users, win_of, first_of, end_of, arrived, queries, keys, values, out, acc, tiles, top, low, rows
):
    lane = lax.broadcasted_iota(jnp.int32, (8, 128), 1)
    row_of = ((lane % 40) // 4) * 8 + lax.broadcasted_iota(jnp.int32, (8, 128), 0)

    def window(user):
        return jnp.minimum(first_of[user], TOK - WIN)

    def held(user):
        token = row_of + window(user)
        return (token >= first_of[user]) & (token < end_of[user])

    def rows_of(head, k):
        return slice(head * WIN + 16 * k, head * WIN + 16 * k + 16)

    ones = jnp.ones((TOK, HD), BF16)
    keys_t = [keys[:, h * HD : (h + 1) * HD].T for h in range(HEADS)]
    values_1 = [
        jnp.concatenate([values[:, h * HD : (h + 1) * HD], ones], axis=1) for h in range(HEADS)
    ]
    own = []
    for user in range(REQS):
        first = pl.multiple_of(window(user), 16)
        token = lax.broadcasted_iota(jnp.int32, (WIN, TOK), 0) + first
        key = lax.broadcasted_iota(jnp.int32, (WIN, TOK), 1)
        outs, sums = attend(
            lambda h: queries[pl.ds(first, WIN), h * HD : (h + 1) * HD],
            lambda h: keys_t[h],
            lambda h: values_1[h],
            (key <= token) & (key >= first_of[user]),
        )
        for head in range(HEADS):
            acc[user, head * WIN : (head + 1) * WIN, :] = outs[head]
        tile = pack_sums(sums)
        own.append(tile)
        top[user] = tile

    def collect(p, carry):
        user = users[p]

        @pl.when(user >= 0)
        def _():
            tile = arrived[p, STAT:BLOCK, :].astype(F32)
            tile = (tile + pltpu.roll(tile, 88, 1)) + pltpu.roll(tile, 48, 1)
            tiles[p] = tile
            top[user] = jnp.maximum(top[user], tile)

        return carry

    lax.fori_loop(0, NREQ, collect, 0)

    for user in range(REQS):
        share = jnp.where(held(user), jnp.exp(own[user] - top[user]), 0.0)
        low[user] = share
        for head in range(HEADS):
            for k in range(WIN // 16):
                acc[user, rows_of(head, k), :] *= spread(share, head, k)

    def add(p, carry):
        user = users[p]

        @pl.when(user >= 0)
        def _():
            share = jnp.where(held(user), jnp.exp(tiles[p] - top[user]), 0.0)
            low[user] += share
            for head in range(HEADS):
                for k in range(WIN // 16):
                    part = arrived[p, rows_of(head, k), :].astype(F32)
                    acc[user, rows_of(head, k), :] += part * spread(share, head, k)

        return carry

    lax.fori_loop(0, NREQ, add, 0)

    rows[...] = jnp.zeros_like(rows)
    for user in range(REQS):
        inside = held(user)
        factor = jnp.where(inside, 1.0 / jnp.where(inside, low[user], 1.0), 0.0)
        first = window(user)
        for head in range(HEADS):
            for k in range(WIN // 16):
                at = pl.ds(pl.multiple_of(first + 16 * k, 16), 16)
                rows[head, at, :] += acc[user, rows_of(head, k), :] * spread(factor, head, k)
    for head in range(HEADS):
        out[:, head * HD : (head + 1) * HD] = rows[head].astype(BF16)


def merge_attention(users, win_of, first_of, end_of, arrived, queries, keys, values):
    return pl.pallas_call(
        merge_kernel,
        out_shape=jax.ShapeDtypeStruct((TOK, HEADS * HD), BF16),
        in_specs=[smem()] * 4 + [vmem()] * 4,
        out_specs=vmem(),
        scratch_shapes=[
            pltpu.VMEM((REQS, STAT, HD), F32),
            pltpu.VMEM((NREQ, 8, 128), F32),
            pltpu.VMEM((REQS, 8, 128), F32),
            pltpu.VMEM((REQS, 8, 128), F32),
            pltpu.VMEM((HEADS, TOK, HD), F32),
        ],
        compiler_params=pltpu.CompilerParams(vmem_limit_bytes=32 << 20),
        cost_estimate=pl.CostEstimate(
            flops=64 << 20, bytes_accessed=6 << 20, transcendentals=1 << 18
        ),
        name="merge_attention",
    )(users, win_of, first_of, end_of, arrived, queries, keys, values)


def project_kernel(att, att_far, weight, weight_far, residual, gain, picks, mixed, sent, both):
    half = residual.shape[1] // 2
    total = residual[...].astype(F32)
    total += jnp.dot(att[...], weight[...], preferred_element_type=F32)
    total += jnp.dot(att_far[...], weight_far[...], preferred_element_type=F32)
    mixed[...] = total
    scale = lax.rsqrt(jnp.mean(total * total, axis=1, keepdims=True) + NORM_EPS)
    normed = (total * scale * gain[...]).astype(BF16)
    both[:TOK] = normed[:, :half]
    both[TOK:] = normed[:, half:]
    step = 256
    for row in range(0, sent.shape[0], step):
        sent[row : row + step] = jnp.dot(
            picks[row : row + step], both[...], preferred_element_type=F32
        ).astype(BF16)


def project(att, att_far, weight, weight_far, residual, gain, picks):
    width = residual.shape[1]
    return pl.pallas_call(
        project_kernel,
        out_shape=(
            jax.ShapeDtypeStruct((TOK, width), F32),
            jax.ShapeDtypeStruct((picks.shape[0], width // 2), BF16),
        ),
        in_specs=[vmem()] * 7,
        out_specs=(vmem(), vmem()),
        scratch_shapes=[pltpu.VMEM((2 * TOK, width // 2), BF16)],
        compiler_params=pltpu.CompilerParams(vmem_limit_bytes=32 << 20),
        cost_estimate=pl.CostEstimate(
            flops=4 * TOK * 512 * width + 2 * picks.shape[0] * 256 * width // 2,
            bytes_accessed=10 << 20,
            transcendentals=TOK,
        ),
        name="project_dispatch",
    )(att, att_far, weight, weight_far, residual, gain, picks)


def expert_kernel(rows, gate, up, down, out):
    count = rows.shape[0]
    width = gate.shape[0]
    half, quarter = width // 2, width // 4
    wide = rows[...].astype(F32)
    upper = lax.broadcasted_iota(jnp.int32, (count // 2, 8, half), 1) < 4
    tail = wide[:, 16:24].reshape(count // 2, 2, 8, half)
    even, odd = tail[:, 0], tail[:, 1]
    tail_0 = jnp.where(upper, even, pltpu.roll(odd, 4, 1))
    tail_1 = jnp.where(upper, pltpu.roll(even, 4, 1), odd)
    left = jnp.concatenate(
        [wide[:, 0:8].reshape(count * 8, half), tail_0.reshape(count * 4, half)], axis=0
    )
    right = jnp.concatenate(
        [wide[:, 8:16].reshape(count * 8, half), tail_1.reshape(count * 4, half)], axis=0
    )
    tokens = jnp.concatenate([left.astype(BF16), right.astype(BF16)], axis=1)
    gate_act = jnp.dot(tokens, gate[...], preferred_element_type=F32)
    up_act = jnp.dot(tokens, up[...], preferred_element_type=F32)
    hidden = (gate_act / (1.0 + jnp.exp(-gate_act)) * up_act).astype(BF16)
    result = jnp.dot(hidden, down[...], preferred_element_type=F32)
    upper = lax.broadcasted_iota(jnp.int32, (count // 2, 8, quarter), 1) < 4
    for side in range(2):
        cols = [slice((2 * side + q) * quarter, (2 * side + q + 1) * quarter) for q in range(2)]
        main = [result[: count * 8, c].reshape(count, 8, quarter) for c in cols]
        tail = [result[count * 8 :, c].reshape(count // 2, 8, quarter) for c in cols]
        even = jnp.where(upper, tail[0], pltpu.roll(tail[1], 4, 1))
        odd = jnp.where(upper, pltpu.roll(tail[0], 4, 1), tail[1])
        last = jnp.stack([even, odd], axis=1).reshape(count, 8, quarter)
        out[:, side] = jnp.concatenate(main + [last], axis=1).astype(BF16)


def run_expert(rows, gate, up, down, steps=2):
    count = rows.shape[0] // steps
    width, hidden = gate.shape
    once = pl.Buffered(1)
    return pl.pallas_call(
        expert_kernel,
        grid=(steps,),
        out_shape=jax.ShapeDtypeStruct((rows.shape[0], 2, 2 * CAP, width // 4), BF16),
        in_specs=[
            pl.BlockSpec((count, 2 * CAP, width // 2), lambda i: (i, 0, 0)),
            pl.BlockSpec((width, hidden), lambda i: (0, 0), pipeline_mode=once),
            pl.BlockSpec((width, hidden), lambda i: (0, 0), pipeline_mode=once),
            pl.BlockSpec((hidden, width), lambda i: (0, 0), pipeline_mode=once),
        ],
        out_specs=pl.BlockSpec((count, 2, 2 * CAP, width // 4), lambda i: (i, 0, 0, 0)),
        compiler_params=pltpu.CompilerParams(vmem_limit_bytes=56 << 20),
        cost_estimate=pl.CostEstimate(
            flops=6 * rows.shape[0] * CAP * width * hidden,
            bytes_accessed=15 << 20,
            transcendentals=rows.shape[0] * CAP * hidden,
        ),
        name="expert",
    )(rows, gate, up, down)


def combine_kernel(mixed, shares, shares_low, rows, out):
    total = jnp.dot(shares[...], rows[...], preferred_element_type=F32)
    total += jnp.dot(shares_low[...], rows[...], preferred_element_type=F32)
    width = rows.shape[1]
    out[:, :width] = (mixed[:, :width] + total[:TOK]).astype(BF16)
    out[:, width:] = (mixed[:, width:] + total[TOK:]).astype(BF16)


def combine(mixed, shares, shares_low, rows):
    return pl.pallas_call(
        combine_kernel,
        out_shape=jax.ShapeDtypeStruct(mixed.shape, BF16),
        in_specs=[vmem()] * 4,
        out_specs=vmem(),
        compiler_params=pltpu.CompilerParams(vmem_limit_bytes=32 << 20),
        cost_estimate=pl.CostEstimate(
            flops=4 * shares.shape[0] * rows.shape[0] * rows.shape[1],
            bytes_accessed=8 << 20,
            transcendentals=0,
        ),
        name="combine",
    )(mixed, shares, shares_low, rows)


def slot_rows():
    slot = np.array(list(range(8)) * 2 + list(range(8, 12)) * 2, np.int32)
    part = np.array([0] * 8 + [1] * 8 + [0] * 4 + [1] * 4, np.int32)
    return slot, part


def routing(expert_ids, expert_weights):
    flat = expert_ids.reshape(-1)
    count = flat.shape[0]
    onehot = (flat[:, None] == jnp.arange(NREQ, dtype=jnp.int32)[None, :]).astype(BF16)
    earlier = (
        jnp.arange(count, dtype=jnp.int32)[None, :] < jnp.arange(count, dtype=jnp.int32)[:, None]
    ).astype(BF16)
    before = jnp.dot(earlier, onehot, preferred_element_type=F32)
    slot = jnp.sum(before * onehot.astype(F32), axis=1).astype(jnp.int32)
    place = (flat * CAP + slot).reshape(TOK, TOP)

    slot_at, part_at = slot_rows()
    row_place = (np.arange(NREQ, dtype=np.int32)[:, None] * CAP + slot_at[None, :]).reshape(-1)
    row_part = np.tile(part_at, NREQ)
    col_place = jnp.concatenate([place, place], axis=0)
    col_part = np.repeat(np.arange(2, dtype=np.int32), TOK)
    hit = jnp.zeros((row_place.shape[0], 2 * TOK), jnp.bool_)
    for k in range(TOP):
        hit = hit | (col_place[None, :, k] == row_place[:, None])
    picks = (hit & (row_part[:, None] == col_part[None, :])).astype(BF16)

    back_place = np.repeat(row_place.reshape(NREQ, 1, -1), 2, axis=1).reshape(-1)
    back_part = np.tile(part_at, 2 * NREQ)
    col_weight = jnp.concatenate([expert_weights, expert_weights], axis=0)
    shares = jnp.zeros((2 * TOK, back_place.shape[0]), F32)
    for k in range(TOP):
        shares = shares + jnp.where(
            col_place[:, k, None] == back_place[None, :], col_weight[:, k, None], 0.0
        )
    shares = jnp.where(back_part[None, :] == col_part[:, None], shares, 0.0)
    high = lax.reduce_precision(shares, 8, 7)
    return picks, high.astype(BF16), (shares - high).astype(BF16)


def shards(
    residual,
    queries,
    new_keys,
    new_values,
    request_ids,
    page_store,
    page_sends,
    page_users,
    expert_ids,
    expert_weights,
    output_weight,
    norm_gain,
    gate_weight,
    up_weight,
    down_weight,
):
    me = lax.axis_index("req")
    tp_index = lax.axis_index("tp")
    width = residual.shape[1]
    half = width // 2
    swap = [(0, 1), (1, 0)]

    users = page_users[0]
    counts = jnp.sum(
        (request_ids[:, None] == jnp.arange(REQS, dtype=jnp.int32)[None, :]).astype(jnp.int32), 0
    )
    end_of = jnp.cumsum(counts)
    first_of = end_of - counts
    win_of_user = jnp.minimum(first_of, TOK - WIN) // 16
    sent_win = jnp.sum(
        jnp.where(
            users[:, None] == jnp.arange(REQS, dtype=jnp.int32)[None, :], win_of_user[None, :], 0
        ),
        1,
    )
    note = jnp.zeros((8, queries.shape[1]), BF16).at[0, :NREQ].set(sent_win.astype(BF16))
    pieces = gather_blocks(jnp.concatenate([queries, note], axis=0))
    src = lax.dynamic_index_in_dim(jnp.asarray(source_table()), me, 0, keepdims=False)
    page_of = page_sends[0][src]
    notes = jnp.concatenate([piece[:, TOK, :NREQ] for piece in pieces], axis=0)
    win_of = lax.dynamic_index_in_dim(notes, me, 1, keepdims=False).astype(jnp.int32)

    parts = partial_attention(src, page_of, win_of, pieces, page_store)
    arrived = lax.all_to_all(parts, "req", 0, 0, tiled=True)
    attended = merge_attention(
        users, sent_win, first_of, end_of, arrived, queries, new_keys, new_values
    )
    weight_far = lax.ppermute(output_weight, "tp", swap)
    picks, shares, shares_low = routing(expert_ids, expert_weights)
    attended_far = lax.ppermute(attended, "tp", swap)
    mixed, sent = project(
        attended, attended_far, output_weight, weight_far, residual, norm_gain[None, :], picks
    )
    rows = lax.all_to_all(sent.reshape(NREQ, 2 * CAP, half), "req", 0, 0, tiled=True)
    result = run_expert(rows, gate_weight[0], up_weight[0], down_weight[0])
    returned = lax.all_to_all(
        result.reshape(2 * NREQ, 2 * CAP, width // 4), ("req", "tp"), 0, 0, tiled=True
    )
    mixed_half = lax.dynamic_slice_in_dim(mixed, tp_index * half, half, 1)
    return combine(mixed_half, shares, shares_low, returned.reshape(-1, width // 4))


def solution(mesh):
    placed = (
        P("req", None),
        P("req", "tp"),
        P("req", "tp"),
        P("req", "tp"),
        P("req"),
        P("req", None, None, "tp"),
        P("req", None),
        P("req", None),
        P("req", None),
        P("req", None),
        P("tp", None),
        P(),
        P("req", None, "tp"),
        P("req", None, "tp"),
        P("req", "tp", None),
    )
    return jax.shard_map(
        shards, mesh=mesh, in_specs=placed, out_specs=P("req", "tp"), check_vma=False
    )
```

```python
import math

import jax
import jax.numpy as jnp
import numpy as np
from jax import lax
from jax.experimental import pallas as pl
from jax.experimental.pallas import tpu as pltpu
from jax.sharding import PartitionSpec as P

HD = 128
TOP = 4
HEADS = 4
PAGE = 128
TOK = 128
CAP = 12
SLOTS = 6
ROWS = SLOTS * 16
STAT = HEADS * ROWS
BLOCK = STAT + 16
NORM_EPS = 1e-06
SCALE = 1.0 / math.sqrt(HD)
LOG2E = math.log2(math.e)
NEG = -1e30
F32 = jnp.float32
BF16 = jnp.bfloat16

NY, NZ, NX, NC = 4, 4, 2, 2
NREQ = NY * NZ * NX * NC
NCHIP = NY * NZ * NX


def req_index(y, z, x, c):
    return ((y * NZ + z) * NX + x) * NC + c


def all_coords():
    return [
        (y, z, x, c) for y in range(NY) for z in range(NZ) for x in range(NX) for c in range(NC)
    ]


def perm_x():
    return [(req_index(y, z, x, c), req_index(y, z, 1 - x, c)) for y, z, x, c in all_coords()]


def perm_core():
    return [(req_index(y, z, x, c), req_index(y, z, x, 1 - c)) for y, z, x, c in all_coords()]


def perm_ring(stage, step):
    pairs = []
    for y, z, x, c in all_coords():
        if (c + stage) % 2 == 0:
            to = req_index((y + step) % NY, z, x, c)
        else:
            to = req_index(y, (z + step) % NZ, x, c)
        pairs.append((req_index(y, z, x, c), to))
    return pairs


def chip_table():
    table = np.zeros((NREQ, NCHIP), np.int32)
    for y, z, x, c in all_coords():
        row = []
        for d1 in range(4):
            for d0 in range(4):
                for dx in range(2):
                    dy, dz = (d0, d1) if c == 0 else (d1, d0)
                    row.append(req_index((y - dy) % NY, (z - dz) % NZ, x ^ dx, 0) // NC)
        table[req_index(y, z, x, c)] = row
    return table


def core_groups():
    return [[chip * NC + core for chip in range(NCHIP)] for core in range(NC)]


def gather_blocks(block, weight):
    pair = jnp.stack([block, lax.ppermute(block, "req", perm_x())])
    pair, weight = lax.optimization_barrier((pair, weight))
    weight_far = lax.ppermute(weight, "tp", [(0, 1), (1, 0)])
    line = jnp.stack(
        [pair] + [lax.ppermute(pair, "req", perm_ring(0, step)) for step in (1, 2, 3)]
    ).reshape(8, *block.shape)
    return [line] + [
        lax.ppermute(line, "req", perm_ring(1, step)) for step in (1, 3, 2)
    ], weight_far


def attend(query, key_t, value_1, shift):
    scores = jnp.dot(query, key_t, preferred_element_type=F32)
    scores = shift(scores)
    top = jnp.max(scores, axis=1, keepdims=True)
    probs = jnp.exp2((scores - top) * (SCALE * LOG2E)).astype(BF16)
    both = jnp.dot(probs, value_1, preferred_element_type=F32)
    total = both[:, HD:]
    return both[:, :HD] / total, top * SCALE + jnp.log(total)


def by_head(rows):
    head = lax.broadcasted_iota(jnp.int32, (8, 128), 0) % HEADS
    tile = jnp.where(head == 0, rows[0], rows[1])
    tile = jnp.where(head == 2, rows[2], tile)
    return jnp.where(head == 3, rows[3], tile)


def keys_kernel(pages, out):
    for page in range(pages.shape[0]):
        for head in range(HEADS):
            out[page, head] = pages[page, 0, :, head * HD : (head + 1) * HD].T


def turn_keys(pages):
    count = pages.shape[0]
    return pl.pallas_call(
        keys_kernel,
        out_shape=jax.ShapeDtypeStruct((count, HEADS, HD, PAGE), BF16),
        in_specs=[vmem()],
        out_specs=vmem(),
        cost_estimate=pl.CostEstimate(
            flops=32 << 20, bytes_accessed=3 << 20, transcendentals=0
        ),
        compiler_params=pltpu.CompilerParams(vmem_limit_bytes=16 << 20),
        name="turn_keys",
    )(pages)


def page_kernel(chip_of, page_a, page_b, codes, blocks, keys_a, keys_b, pages_a, pages_b, *refs):
    out, held, sems = refs[-3:]
    row = lax.broadcasted_iota(jnp.int32, (16, 128), 0)
    offset = lax.broadcasted_iota(jnp.int32, (16, 128), 1) - row
    sub = lax.broadcasted_iota(jnp.int32, (8, 128), 0)
    ones = jnp.ones((PAGE, HD), BF16)

    def copy(i):
        return pltpu.make_async_copy(held.at[i], out.at[chip_of[i]], sems.at[i])

    def step(i, carry):
        pa, pb = page_a[i], page_b[i]
        code = [codes[i * SLOTS + j] for j in range(SLOTS)]
        first = [pl.multiple_of((c & 7) * 16, 16) for c in code]
        bias = jnp.concatenate(
            [
                jnp.concatenate(
                    [
                        jnp.full((16, PAGE), jnp.where((c & bit) != 0, 0.0, NEG), F32)
                        for bit in (8, 16)
                    ],
                    axis=1,
                )
                for c in code
            ],
            axis=0,
        )
        mine = [offset == jnp.where(c >= 8, (c & 7) * 16, -1024) for c in code]
        sums = []
        for head in range(HEADS):
            cols = slice(head * HD, (head + 1) * HD)
            query = jnp.concatenate(
                [blocks[i, pl.ds(first[j], 16), cols] for j in range(SLOTS)], axis=0
            )
            key_t = jnp.concatenate([keys_a[pa, head], keys_b[pb, head]], axis=1)
            value_1 = jnp.concatenate(
                [
                    jnp.concatenate([pages_a[pa, 1, :, cols], ones], axis=1),
                    jnp.concatenate([pages_b[pb, 1, :, cols], ones], axis=1),
                ],
                axis=0,
            )
            got, total = attend(query, key_t, value_1, lambda s: s + bias)
            held[i, head * ROWS : (head + 1) * ROWS, :] = got.astype(BF16)
            here = jnp.where(mine[0], total[:16], NEG)
            for j in range(1, SLOTS):
                here = jnp.maximum(here, jnp.where(mine[j], total[16 * j : 16 * j + 16], NEG))
            sums.append(jnp.max(here, axis=0, keepdims=True))
        tile = by_head(sums)
        high = tile.astype(BF16).astype(F32)
        rest = tile - high
        middle = rest.astype(BF16).astype(F32)
        upper = jnp.where(sub < HEADS, high, middle)
        lower = jnp.where(sub < HEADS, rest - middle, 0.0)
        held[i, STAT:BLOCK, :] = jnp.concatenate([upper, lower], axis=0).astype(BF16)
        copy(i).start()
        return carry

    count = blocks.shape[0]
    lax.fori_loop(0, count, step, 0, unroll=2)
    lax.fori_loop(0, count, lambda i, carry: (copy(i).wait(), carry)[1], 0)


def page_attention(chip_of, page_a, page_b, codes, blocks, keys_a, keys_b, pages_a, pages_b, last):
    count = blocks.shape[0]
    before = [] if last is None else [last]
    return pl.pallas_call(
        page_kernel,
        out_shape=jax.ShapeDtypeStruct((NCHIP, BLOCK, HD), BF16),
        in_specs=[smem()] * 4
        + [vmem()] * 5
        + [pl.BlockSpec(memory_space=pl.ANY)] * len(before),
        out_specs=pl.BlockSpec(memory_space=pl.ANY),
        input_output_aliases={9: 0} if before else {},
        scratch_shapes=[
            pltpu.VMEM((count, BLOCK, HD), BF16),
            pltpu.SemaphoreType.DMA((count,)),
        ],
        compiler_params=pltpu.CompilerParams(vmem_limit_bytes=24 << 20),
        cost_estimate=pl.CostEstimate(
            flops=count * HEADS * 12 * ROWS * HD * HD * 8,
            bytes_accessed=6 << 20,
            transcendentals=count * HEADS * ROWS * 2 * PAGE,
        ),
        name="page_attention",
    )(chip_of, page_a, page_b, codes, blocks, keys_a, keys_b, pages_a, pages_b, *before)


def smem():
    return pl.BlockSpec(memory_space=pltpu.SMEM)


def vmem():
    return pl.BlockSpec(memory_space=pltpu.VMEM)


def own_kernel(request_col, request_row, queries, keys, values, out, total):
    token = lax.broadcasted_iota(jnp.int32, (TOK, TOK), 0)
    key = lax.broadcasted_iota(jnp.int32, (TOK, TOK), 1)
    mask = (request_col[...] == request_row[...]) & (key <= token)
    ones = jnp.ones((TOK, HD), BF16)
    sums = []
    for head in range(HEADS):
        cols = slice(head * HD, (head + 1) * HD)
        got, low = attend(
            queries[:, cols],
            keys[:, cols].T,
            jnp.concatenate([values[:, cols], ones], axis=1),
            lambda s: jnp.where(mask, s, NEG),
        )
        out[head] = got
        sums.append(jnp.max(jnp.where(token == key, low, NEG), axis=0, keepdims=True))
    total[...] = by_head(sums)


def own_attention(request_ids, queries, keys, values):
    return pl.pallas_call(
        own_kernel,
        out_shape=(
            jax.ShapeDtypeStruct((HEADS, TOK, HD), F32),
            jax.ShapeDtypeStruct((8, TOK), F32),
        ),
        in_specs=[vmem()] * 5,
        out_specs=(vmem(), vmem()),
        compiler_params=pltpu.CompilerParams(vmem_limit_bytes=16 << 20),
        cost_estimate=pl.CostEstimate(
            flops=64 << 20, bytes_accessed=1 << 20, transcendentals=HEADS * TOK * TOK
        ),
        name="own_attention",
    )(request_ids[:, None], request_ids[None, :], queries, keys, values)


def merge_kernel(codes, arrived, own, own_sums, out, acc, tiles):
    row = lax.broadcasted_iota(jnp.int32, (16, TOK), 0)
    offset = lax.broadcasted_iota(jnp.int32, (16, TOK), 1) - row
    ones = jnp.ones((2 * TOK, HD), BF16)

    def halves(tile):
        high = tile.astype(BF16).astype(F32)
        return high, tile - high

    def on_rows(parts, masks):
        blocks = []
        for head in range(HEADS):
            for mask in masks:
                blocks.append(
                    jnp.concatenate(
                        [
                            jnp.where(mask, jnp.broadcast_to(p[head : head + 1], (16, TOK)), 0.0)
                            for p in parts
                        ],
                        axis=1,
                    )
                )
        picked = jnp.concatenate(blocks, axis=0).astype(BF16)
        return jnp.dot(picked, ones, preferred_element_type=F32)

    def collect(p, top):
        tile = arrived[p, STAT:BLOCK, :].astype(F32)
        tile = (tile[:8] + pltpu.roll(tile[:8], HEADS, 0)) + tile[8:]
        tiles[p] = tile
        return jnp.maximum(top, tile)

    top = lax.fori_loop(0, NCHIP, collect, own_sums[...], unroll=4)
    whole = [offset == 16 * g for g in range(TOK // 16)]
    share = jnp.exp(own_sums[...] - top)
    acc[...] = own[...] * on_rows(halves(share), whole).reshape(HEADS, TOK, HD)

    def add(p, low):
        share = jnp.exp(tiles[p] - top)
        code = [codes[p * SLOTS + j] for j in range(SLOTS)]
        masks = [offset == jnp.where(c >= 8, (c & 7) * 16, -1024) for c in code]
        factor = on_rows(halves(share), masks)
        for j in range(SLOTS):
            at = pl.ds(pl.multiple_of((code[j] & 7) * 16, 16), 16)
            for head in range(HEADS):
                start = head * ROWS + 16 * j
                part = arrived[p, start : start + 16, :].astype(F32)
                acc[head, at, :] += part * factor[start : start + 16]
        return low + share

    low = lax.fori_loop(0, NCHIP, add, share)
    factor = on_rows(halves(1.0 / low), whole)
    for head in range(HEADS):
        out[:, head * HD : (head + 1) * HD] = (
            acc[head] * factor[head * TOK : (head + 1) * TOK]
        ).astype(BF16)


def merge_attention(codes, arrived, own, own_sums):
    return pl.pallas_call(
        merge_kernel,
        out_shape=jax.ShapeDtypeStruct((TOK, HEADS * HD), BF16),
        in_specs=[smem()] + [vmem()] * 3,
        out_specs=vmem(),
        scratch_shapes=[
            pltpu.VMEM((HEADS, TOK, HD), F32),
            pltpu.VMEM((NCHIP, 8, TOK), F32),
        ],
        compiler_params=pltpu.CompilerParams(vmem_limit_bytes=24 << 20),
        cost_estimate=pl.CostEstimate(
            flops=64 << 20, bytes_accessed=4 << 20, transcendentals=1 << 18
        ),
        name="merge_attention",
    )(codes, arrived, own, own_sums)


def project_kernel(att, att_far, weight, weight_far, residual, gain, picks, mixed, sent, both):
    half = residual.shape[1] // 2
    total = residual[...].astype(F32)
    total += jnp.dot(att[...], weight[...], preferred_element_type=F32)
    total += jnp.dot(att_far[...], weight_far[...], preferred_element_type=F32)
    mixed[...] = total
    scale = lax.rsqrt(jnp.mean(total * total, axis=1, keepdims=True) + NORM_EPS)
    normed = (total * scale * gain[...]).astype(BF16)
    both[:TOK] = normed[:, :half]
    both[TOK:] = normed[:, half:]
    step = 256
    for row in range(0, sent.shape[0], step):
        sent[row : row + step] = jnp.dot(
            picks[row : row + step], both[...], preferred_element_type=F32
        ).astype(BF16)


def project(att, att_far, weight, weight_far, residual, gain, picks):
    width = residual.shape[1]
    return pl.pallas_call(
        project_kernel,
        out_shape=(
            jax.ShapeDtypeStruct((TOK, width), F32),
            jax.ShapeDtypeStruct((picks.shape[0], width // 2), BF16),
        ),
        in_specs=[vmem()] * 7,
        out_specs=(vmem(), vmem()),
        scratch_shapes=[pltpu.VMEM((2 * TOK, width // 2), BF16)],
        compiler_params=pltpu.CompilerParams(vmem_limit_bytes=32 << 20),
        cost_estimate=pl.CostEstimate(
            flops=4 * TOK * 512 * width + 2 * picks.shape[0] * 256 * width // 2,
            bytes_accessed=10 << 20,
            transcendentals=TOK,
        ),
        name="project_dispatch",
    )(att, att_far, weight, weight_far, residual, gain, picks)


def expert_kernel(rows, gate, up, down, out):
    count = rows.shape[0]
    width = gate.shape[0]
    half, quarter = width // 2, width // 4
    wide = rows[...].astype(F32)
    upper = lax.broadcasted_iota(jnp.int32, (count // 2, 8, half), 1) < 4
    tail = wide[:, 16:24].reshape(count // 2, 2, 8, half)
    even, odd = tail[:, 0], tail[:, 1]
    tail_0 = jnp.where(upper, even, pltpu.roll(odd, 4, 1))
    tail_1 = jnp.where(upper, pltpu.roll(even, 4, 1), odd)
    left = jnp.concatenate(
        [wide[:, 0:8].reshape(count * 8, half), tail_0.reshape(count * 4, half)], axis=0
    )
    right = jnp.concatenate(
        [wide[:, 8:16].reshape(count * 8, half), tail_1.reshape(count * 4, half)], axis=0
    )
    tokens = jnp.concatenate([left.astype(BF16), right.astype(BF16)], axis=1)
    gate_act = jnp.dot(tokens, gate[...], preferred_element_type=F32)
    up_act = jnp.dot(tokens, up[...], preferred_element_type=F32)
    hidden = (gate_act / (1.0 + jnp.exp(-gate_act)) * up_act).astype(BF16)
    result = jnp.dot(hidden, down[...], preferred_element_type=F32)
    upper = lax.broadcasted_iota(jnp.int32, (count // 2, 8, quarter), 1) < 4
    for side in range(2):
        cols = [slice((2 * side + q) * quarter, (2 * side + q + 1) * quarter) for q in range(2)]
        main = [result[: count * 8, c].reshape(count, 8, quarter) for c in cols]
        tail = [result[count * 8 :, c].reshape(count // 2, 8, quarter) for c in cols]
        even = jnp.where(upper, tail[0], pltpu.roll(tail[1], 4, 1))
        odd = jnp.where(upper, pltpu.roll(tail[0], 4, 1), tail[1])
        last = jnp.stack([even, odd], axis=1).reshape(count, 8, quarter)
        out[:, side] = jnp.concatenate(main + [last], axis=1).astype(BF16)


def run_expert(rows, gate, up, down, steps=2):
    count = rows.shape[0] // steps
    width, hidden = gate.shape
    once = pl.Buffered(1)
    return pl.pallas_call(
        expert_kernel,
        grid=(steps,),
        out_shape=jax.ShapeDtypeStruct((rows.shape[0], 2, 2 * CAP, width // 4), BF16),
        in_specs=[
            pl.BlockSpec((count, 2 * CAP, width // 2), lambda i: (i, 0, 0)),
            pl.BlockSpec((width, hidden), lambda i: (0, 0), pipeline_mode=once),
            pl.BlockSpec((width, hidden), lambda i: (0, 0), pipeline_mode=once),
            pl.BlockSpec((hidden, width), lambda i: (0, 0), pipeline_mode=once),
        ],
        out_specs=pl.BlockSpec((count, 2, 2 * CAP, width // 4), lambda i: (i, 0, 0, 0)),
        compiler_params=pltpu.CompilerParams(vmem_limit_bytes=56 << 20),
        cost_estimate=pl.CostEstimate(
            flops=6 * rows.shape[0] * CAP * width * hidden,
            bytes_accessed=15 << 20,
            transcendentals=rows.shape[0] * CAP * hidden,
        ),
        name="expert",
    )(rows, gate, up, down)


def combine_kernel(mixed, shares, shares_low, rows, out):
    total = jnp.dot(shares[...], rows[...], preferred_element_type=F32)
    total += jnp.dot(shares_low[...], rows[...], preferred_element_type=F32)
    width = rows.shape[1]
    out[:, :width] = (mixed[:, :width] + total[:TOK]).astype(BF16)
    out[:, width:] = (mixed[:, width:] + total[TOK:]).astype(BF16)


def combine(mixed, shares, shares_low, rows):
    return pl.pallas_call(
        combine_kernel,
        out_shape=jax.ShapeDtypeStruct(mixed.shape, BF16),
        in_specs=[vmem()] * 4,
        out_specs=vmem(),
        compiler_params=pltpu.CompilerParams(vmem_limit_bytes=32 << 20),
        cost_estimate=pl.CostEstimate(
            flops=4 * shares.shape[0] * rows.shape[0] * rows.shape[1],
            bytes_accessed=8 << 20,
            transcendentals=0,
        ),
        name="combine",
    )(mixed, shares, shares_low, rows)


def slot_rows():
    slot = np.array(list(range(8)) * 2 + list(range(8, 12)) * 2, np.int32)
    part = np.array([0] * 8 + [1] * 8 + [0] * 4 + [1] * 4, np.int32)
    return slot, part


def routing(expert_ids, expert_weights):
    flat = expert_ids.reshape(-1)
    count = flat.shape[0]
    onehot = (flat[:, None] == jnp.arange(NREQ, dtype=jnp.int32)[None, :]).astype(BF16)
    earlier = (
        jnp.arange(count, dtype=jnp.int32)[None, :] < jnp.arange(count, dtype=jnp.int32)[:, None]
    ).astype(BF16)
    before = jnp.dot(earlier, onehot, preferred_element_type=F32)
    slot = jnp.sum(before * onehot.astype(F32), axis=1).astype(jnp.int32)
    place = (flat * CAP + slot).reshape(TOK, TOP)

    slot_at, part_at = slot_rows()
    row_place = (np.arange(NREQ, dtype=np.int32)[:, None] * CAP + slot_at[None, :]).reshape(-1)
    row_part = np.tile(part_at, NREQ)
    col_place = jnp.concatenate([place, place], axis=0)
    col_part = np.repeat(np.arange(2, dtype=np.int32), TOK)
    hit = jnp.zeros((row_place.shape[0], 2 * TOK), jnp.bool_)
    for k in range(TOP):
        hit = hit | (col_place[None, :, k] == row_place[:, None])
    picks = (hit & (row_part[:, None] == col_part[None, :])).astype(BF16)

    back_place = np.repeat(row_place.reshape(NREQ, 1, -1), 2, axis=1).reshape(-1)
    back_part = np.tile(part_at, 2 * NREQ)
    col_weight = jnp.concatenate([expert_weights, expert_weights], axis=0)
    shares = jnp.zeros((2 * TOK, back_place.shape[0]), F32)
    for k in range(TOP):
        shares = shares + jnp.where(
            col_place[:, k, None] == back_place[None, :], col_weight[:, k, None], 0.0
        )
    shares = jnp.where(back_part[None, :] == col_part[:, None], shares, 0.0)
    high = lax.reduce_precision(shares, 8, 7)
    return picks, high.astype(BF16), (shares - high).astype(BF16)


def shards(
    residual,
    queries,
    new_keys,
    new_values,
    request_ids,
    page_store,
    page_sends,
    page_users,
    expert_ids,
    expert_weights,
    output_weight,
    norm_gain,
    gate_weight,
    up_weight,
    down_weight,
):
    me = lax.axis_index("req")
    tp_index = lax.axis_index("tp")
    width = residual.shape[1]
    half = width // 2
    swap = [(0, 1), (1, 0)]

    core = me % NC
    users = page_users[0].reshape(NCHIP, NC)
    user_a = jnp.where(core == 0, users[:, 0], users[:, 1])[:, None]
    user_b = jnp.where(core == 0, users[:, 1], users[:, 0])[:, None]
    group = jnp.arange(TOK // 16, dtype=jnp.int32)
    group_user = request_ids.reshape(TOK // 16, 16)[:, 0][None, :]
    hit_a, hit_b = group_user == user_a, group_user == user_b
    needed = (hit_a | hit_b).astype(jnp.int32)
    rank = jnp.sum(needed[:, None, :] * (group[None, :] < group[:, None]), axis=2)
    value = needed * (group[None, :] + 8 * hit_a + 16 * hit_b)
    slot = jnp.arange(SLOTS, dtype=jnp.int32)
    codes = jnp.sum(jnp.where(rank[:, None, :] == slot[None, :, None], value[:, None, :], 0), 2)

    note = jnp.zeros((8, queries.shape[1]), BF16)
    note = note.at[0, : NCHIP * SLOTS].set(codes.T.reshape(-1).astype(BF16))
    pieces, weight_far = gather_blocks(
        jnp.concatenate([queries, note], axis=0), output_weight
    )
    pages_far = lax.ppermute(page_store, "req", perm_core())
    sends_far = lax.ppermute(page_sends, "req", perm_core())
    keys_a, keys_b = turn_keys(page_store), turn_keys(pages_far)
    own, own_sums = own_attention(request_ids, queries, new_keys, new_values)

    table = chip_table()
    order = np.array([0, 1, 3, 2])
    chips = lax.dynamic_index_in_dim(
        jnp.asarray(table.reshape(NREQ, 4, 8)[:, order].reshape(NREQ, NCHIP)), me, 0, keepdims=False
    )
    page_a = page_sends[0][chips * NC + core]
    page_b = sends_far[0][chips * NC + core]
    parts = None
    for index, piece in enumerate(pieces):
        if index == 3:
            piece, weight_far = lax.optimization_barrier((piece, weight_far))
        asked = piece[:, TOK, : NCHIP * SLOTS].reshape(8, SLOTS, NCHIP)
        asked = lax.dynamic_index_in_dim(asked, me // NC, 2, keepdims=False)
        rows = slice(8 * index, 8 * index + 8)
        parts = page_attention(
            chips[rows],
            page_a[rows],
            page_b[rows],
            asked.astype(jnp.int32).reshape(-1),
            piece,
            keys_a,
            keys_b,
            page_store,
            pages_far,
            parts,
        )
    arrived = lax.all_to_all(
        parts, "req", 0, 0, tiled=True, axis_index_groups=core_groups()
    )
    attended = merge_attention(codes.reshape(-1), arrived, own, own_sums)
    picks, shares, shares_low = routing(expert_ids, expert_weights)
    attended_far = lax.ppermute(attended, "tp", swap)
    mixed, sent = project(
        attended, attended_far, output_weight, weight_far, residual, norm_gain[None, :], picks
    )
    rows = lax.all_to_all(sent.reshape(NREQ, 2 * CAP, half), "req", 0, 0, tiled=True)
    result = run_expert(rows, gate_weight[0], up_weight[0], down_weight[0])
    returned = lax.all_to_all(
        result.reshape(2 * NREQ, 2 * CAP, width // 4), ("req", "tp"), 0, 0, tiled=True
    )
    mixed_half = lax.dynamic_slice_in_dim(mixed, tp_index * half, half, 1)
    return combine(mixed_half, shares, shares_low, returned.reshape(-1, width // 4))


def solution(mesh):
    placed = (
        P("req", None),
        P("req", "tp"),
        P("req", "tp"),
        P("req", "tp"),
        P("req"),
        P("req", None, None, "tp"),
        P("req", None),
        P("req", None),
        P("req", None),
        P("req", None),
        P("tp", None),
        P(),
        P("req", None, "tp"),
        P("req", None, "tp"),
        P("req", "tp", None),
    )
    return jax.shard_map(
        shards, mesh=mesh, in_specs=placed, out_specs=P("req", "tp"), check_vma=False
    )
```

```python
import math

import jax
import jax.numpy as jnp
import numpy as np
from jax import lax
from jax.experimental import pallas as pl
from jax.experimental.pallas import tpu as pltpu
from jax.sharding import PartitionSpec as P

HD = 128
TOP = 4
HEADS = 4
PAGE = 128
TOK = 128
CAP = 12
SLOTS = 6
ROWS = SLOTS * 16
STAT = HEADS * ROWS
BLOCK = STAT + 16
MERGE_PARTS = 2
NORM_EPS = 1e-06
SCALE = 1.0 / math.sqrt(HD)
LOG2E = math.log2(math.e)
NEG = -1e30
F32 = jnp.float32
BF16 = jnp.bfloat16

NY, NZ, NX, NC = 4, 4, 2, 2
NREQ = NY * NZ * NX * NC
NCHIP = NY * NZ * NX


def req_index(y, z, x, c):
    return ((y * NZ + z) * NX + x) * NC + c


def all_coords():
    return [
        (y, z, x, c) for y in range(NY) for z in range(NZ) for x in range(NX) for c in range(NC)
    ]


def perm_x():
    return [(req_index(y, z, x, c), req_index(y, z, 1 - x, c)) for y, z, x, c in all_coords()]


def perm_core():
    return [(req_index(y, z, x, c), req_index(y, z, x, 1 - c)) for y, z, x, c in all_coords()]


def perm_ring(stage, step):
    pairs = []
    for y, z, x, c in all_coords():
        if (c + stage) % 2 == 0:
            to = req_index((y + step) % NY, z, x, c)
        else:
            to = req_index(y, (z + step) % NZ, x, c)
        pairs.append((req_index(y, z, x, c), to))
    return pairs


def chip_table():
    table = np.zeros((NREQ, NCHIP), np.int32)
    for y, z, x, c in all_coords():
        row = []
        for d1 in range(4):
            for d0 in range(4):
                for dx in range(2):
                    dy, dz = (d0, d1) if c == 0 else (d1, d0)
                    row.append(req_index((y - dy) % NY, (z - dz) % NZ, x ^ dx, 0) // NC)
        table[req_index(y, z, x, c)] = row
    return table


def core_groups():
    return [[chip * NC + core for chip in range(NCHIP)] for core in range(NC)]


def gather_blocks(block, weight, pages, sends):
    near = lax.ppermute(block, "req", perm_x())
    pages = lax.ppermute(pages, "req", perm_core())
    sends = lax.ppermute(sends, "req", perm_core())
    near, weight, pages, sends = lax.optimization_barrier((near, weight, pages, sends))
    pair = jnp.stack([block, near])
    weight_far = lax.ppermute(weight, "tp", [(0, 1), (1, 0)])
    line = jnp.stack(
        [pair] + [lax.ppermute(pair, "req", perm_ring(0, step)) for step in (1, 2, 3)]
    ).reshape(8, *block.shape)
    return [line] + [
        lax.ppermute(line, "req", perm_ring(1, step)) for step in (1, 3, 2)
    ], (weight_far, pages, sends)


def attend(query, key_t, value_1, shift):
    scores = jnp.dot(query, key_t, preferred_element_type=F32)
    scores = shift(scores)
    top = jnp.max(scores, axis=1, keepdims=True)
    probs = jnp.exp2((scores - top) * (SCALE * LOG2E)).astype(BF16)
    both = jnp.dot(probs, value_1, preferred_element_type=F32)
    total = both[:, HD:]
    return both[:, :HD] / total, top * SCALE + jnp.log(total)


def by_head(rows):
    head = lax.broadcasted_iota(jnp.int32, (8, 128), 0) % HEADS
    tile = jnp.where(head == 0, rows[0], rows[1])
    tile = jnp.where(head == 2, rows[2], tile)
    return jnp.where(head == 3, rows[3], tile)


def keys_kernel(pages, out):
    for page in range(pages.shape[0]):
        for head in range(HEADS):
            out[page, head] = pages[page, 0, :, head * HD : (head + 1) * HD].T


def turn_keys(pages):
    count = pages.shape[0]
    return pl.pallas_call(
        keys_kernel,
        out_shape=jax.ShapeDtypeStruct((count, HEADS, HD, PAGE), BF16),
        in_specs=[pl.BlockSpec(pages.shape, lambda i: (0, 0, 0, 0))],
        out_specs=pl.BlockSpec((count, HEADS, HD, PAGE), lambda i: (0, 0, 0, 0)),
        grid=(1,),
        cost_estimate=pl.CostEstimate(
            flops=32 << 20, bytes_accessed=3 << 20, transcendentals=0
        ),
        compiler_params=pltpu.CompilerParams(vmem_limit_bytes=62 << 20),
        name="turn_keys",
    )(pages)


def page_kernel(chip_of, page_a, page_b, codes, blocks_in, keys_a_in, keys_b_in, pages_a_in, pages_b_in, *refs):
    out, blocks, keys_a, keys_b, values_a, values_b, held, sems, load_sems = refs[-9:]
    loads = [
        pltpu.make_async_copy(source, target, load_sems.at[n])
        for n, (source, target) in enumerate(
            (
                (keys_a_in, keys_a),
                (keys_b_in, keys_b),
                (blocks_in, blocks),
                (pages_a_in.at[:, 1], values_a),
                (pages_b_in.at[:, 1], values_b),
            )
        )
    ]
    for load in loads:
        load.start()
    row = lax.broadcasted_iota(jnp.int32, (16, 128), 0)
    offset = lax.broadcasted_iota(jnp.int32, (16, 128), 1) - row
    sub = lax.broadcasted_iota(jnp.int32, (8, 128), 0)
    ones = jnp.ones((PAGE, HD), BF16)
    for load in loads:
        load.wait()

    def copy(i):
        return pltpu.make_async_copy(held.at[i], out.at[chip_of[i]], sems.at[i])

    def step(i, carry):
        pa, pb = page_a[i], page_b[i]
        code = [codes[i * SLOTS + j] for j in range(SLOTS)]
        first = [pl.multiple_of((c & 7) * 16, 16) for c in code]
        bias = jnp.concatenate(
            [
                jnp.concatenate(
                    [
                        jnp.full((16, PAGE), jnp.where((c & bit) != 0, 0.0, NEG), F32)
                        for bit in (8, 16)
                    ],
                    axis=1,
                )
                for c in code
            ],
            axis=0,
        )
        mine = [offset == jnp.where(c >= 8, (c & 7) * 16, -1024) for c in code]
        scores = []
        for head in range(HEADS):
            cols = slice(head * HD, (head + 1) * HD)
            query = jnp.concatenate(
                [blocks[i, pl.ds(first[j], 16), cols] for j in range(SLOTS)], axis=0
            )
            key_t = jnp.concatenate([keys_a[pa, head], keys_b[pb, head]], axis=1)
            scores.append(jnp.dot(query, key_t, preferred_element_type=F32) + bias)
        tops = [jnp.max(s, axis=1, keepdims=True) for s in scores]
        probs = [
            jnp.exp2((s - t) * (SCALE * LOG2E)).astype(BF16) for s, t in zip(scores, tops)
        ]
        boths = []
        for head in range(HEADS):
            cols = slice(head * HD, (head + 1) * HD)
            value_1 = jnp.concatenate(
                [
                    jnp.concatenate([values_a[pa, :, cols], ones], axis=1),
                    jnp.concatenate([values_b[pb, :, cols], ones], axis=1),
                ],
                axis=0,
            )
            boths.append(jnp.dot(probs[head], value_1, preferred_element_type=F32))
        sums = []
        for head in range(HEADS):
            total = boths[head][:, HD:]
            got = boths[head][:, :HD] / total
            held[i, head * ROWS : (head + 1) * ROWS, :] = got.astype(BF16)
            total = tops[head] * SCALE + jnp.log(total)
            here = jnp.where(mine[0], total[:16], NEG)
            for j in range(1, SLOTS):
                here = jnp.maximum(here, jnp.where(mine[j], total[16 * j : 16 * j + 16], NEG))
            sums.append(jnp.max(here, axis=0, keepdims=True))
        tile = by_head(sums)
        high = tile.astype(BF16).astype(F32)
        rest = tile - high
        middle = rest.astype(BF16).astype(F32)
        upper = jnp.where(sub < HEADS, high, middle)
        lower = jnp.where(sub < HEADS, rest - middle, 0.0)
        held[i, STAT:BLOCK, :] = jnp.concatenate([upper, lower], axis=0).astype(BF16)
        copy(i).start()
        return carry

    count = blocks.shape[0]
    lax.fori_loop(0, count, step, 0, unroll=4)
    lax.fori_loop(0, count, lambda i, carry: (copy(i).wait(), carry)[1], 0)


def page_attention(chip_of, page_a, page_b, codes, blocks, keys_a, keys_b, pages_a, pages_b, last):
    count = blocks.shape[0]
    before = [] if last is None else [last]
    return pl.pallas_call(
        page_kernel,
        out_shape=jax.ShapeDtypeStruct((NCHIP, BLOCK, HD), BF16),
        in_specs=[smem()] * 4
        + [hbm()] * (5 + len(before)),
        out_specs=hbm(),
        input_output_aliases={9: 0} if before else {},
        scratch_shapes=[
            pltpu.VMEM(blocks.shape, BF16),
            pltpu.VMEM(keys_a.shape, BF16),
            pltpu.VMEM(keys_b.shape, BF16),
            pltpu.VMEM((pages_a.shape[0], PAGE, HEADS * HD), BF16),
            pltpu.VMEM((pages_b.shape[0], PAGE, HEADS * HD), BF16),
            pltpu.VMEM((count, BLOCK, HD), BF16),
            pltpu.SemaphoreType.DMA((count,)),
            pltpu.SemaphoreType.DMA((5,)),
        ],
        compiler_params=pltpu.CompilerParams(vmem_limit_bytes=62 << 20),
        cost_estimate=pl.CostEstimate(
            flops=count * HEADS * 12 * ROWS * HD * HD * 8,
            bytes_accessed=6 << 20,
            transcendentals=count * HEADS * ROWS * 2 * PAGE,
        ),
        name="page_attention",
    )(chip_of, page_a, page_b, codes, blocks, keys_a, keys_b, pages_a, pages_b, *before)


def smem():
    return pl.BlockSpec(memory_space=pltpu.SMEM)


def hbm():
    return pl.BlockSpec(memory_space=pltpu.HBM)


def vmem():
    return pl.BlockSpec(memory_space=pltpu.VMEM)


def own_kernel(request_col, request_row, queries, keys, values, out_hbm, total_hbm, out, total, sems):
    token = lax.broadcasted_iota(jnp.int32, (TOK, TOK), 0)
    key = lax.broadcasted_iota(jnp.int32, (TOK, TOK), 1)
    mask = (request_col[...] == request_row[...]) & (key <= token)
    ones = jnp.ones((TOK, HD), BF16)
    sums = []
    for head in range(HEADS):
        cols = slice(head * HD, (head + 1) * HD)
        got, low = attend(
            queries[:, cols],
            keys[:, cols].T,
            jnp.concatenate([values[:, cols], ones], axis=1),
            lambda s: jnp.where(mask, s, NEG),
        )
        out[head] = got
        sums.append(jnp.max(jnp.where(token == key, low, NEG), axis=0, keepdims=True))
    total[...] = by_head(sums)
    copies = [
        pltpu.make_async_copy(out, out_hbm, sems.at[0]),
        pltpu.make_async_copy(total, total_hbm, sems.at[1]),
    ]
    for copy in copies:
        copy.start()
    for copy in copies:
        copy.wait()


def own_attention(request_ids, queries, keys, values):
    return pl.pallas_call(
        own_kernel,
        out_shape=(
            jax.ShapeDtypeStruct((HEADS, TOK, HD), F32),
            jax.ShapeDtypeStruct((8, TOK), F32),
        ),
        in_specs=[vmem()] * 5,
        out_specs=(hbm(), hbm()),
        scratch_shapes=[
            pltpu.VMEM((HEADS, TOK, HD), F32),
            pltpu.VMEM((8, TOK), F32),
            pltpu.SemaphoreType.DMA((2,)),
        ],
        compiler_params=pltpu.CompilerParams(vmem_limit_bytes=62 << 20),
        cost_estimate=pl.CostEstimate(
            flops=64 << 20, bytes_accessed=1 << 20, transcendentals=HEADS * TOK * TOK
        ),
        name="own_attention",
    )(request_ids[:, None], request_ids[None, :], queries, keys, values)


def merge_kernel(
    codes, arrived_in, own_in, own_sums_in, out, acc, tiles, arrived, own, own_sums, sems
):
    part = NCHIP // MERGE_PARTS
    loads = [
        pltpu.make_async_copy(own_sums_in, own_sums, sems.at[0]),
        pltpu.make_async_copy(own_in, own, sems.at[1]),
    ] + [
        pltpu.make_async_copy(
            arrived_in.at[pl.ds(i * part, part)], arrived.at[pl.ds(i * part, part)], sems.at[2 + i]
        )
        for i in range(MERGE_PARTS)
    ]
    for load in loads:
        load.start()
    row = lax.broadcasted_iota(jnp.int32, (16, TOK), 0)
    offset = lax.broadcasted_iota(jnp.int32, (16, TOK), 1) - row
    ones = jnp.ones((2 * TOK, HD), BF16)

    def halves(tile):
        high = tile.astype(BF16).astype(F32)
        return high, tile - high

    def on_rows(parts, masks):
        blocks = []
        for head in range(HEADS):
            for mask in masks:
                blocks.append(
                    jnp.concatenate(
                        [
                            jnp.where(mask, jnp.broadcast_to(p[head : head + 1], (16, TOK)), 0.0)
                            for p in parts
                        ],
                        axis=1,
                    )
                )
        picked = jnp.concatenate(blocks, axis=0).astype(BF16)
        return jnp.dot(picked, ones, preferred_element_type=F32)

    def collect(p, top):
        tile = arrived[p, STAT:BLOCK, :].astype(F32)
        tile = (tile[:8] + pltpu.roll(tile[:8], HEADS, 0)) + tile[8:]
        tiles[p] = tile
        return jnp.maximum(top, tile)

    loads[0].wait()
    top = own_sums[...]
    for i in range(MERGE_PARTS):
        loads[2 + i].wait()
        top = lax.fori_loop(i * part, (i + 1) * part, collect, top, unroll=4)
    loads[1].wait()
    whole = [offset == 16 * g for g in range(TOK // 16)]
    share = jnp.exp(own_sums[...] - top)
    acc[...] = own[...] * on_rows(halves(share), whole).reshape(HEADS, TOK, HD)

    def add(p, low):
        share = jnp.exp(tiles[p] - top)
        code = [codes[p * SLOTS + j] for j in range(SLOTS)]
        masks = [offset == jnp.where(c >= 8, (c & 7) * 16, -1024) for c in code]
        factor = on_rows(halves(share), masks)
        for j in range(SLOTS):
            at = pl.ds(pl.multiple_of((code[j] & 7) * 16, 16), 16)
            for head in range(HEADS):
                start = head * ROWS + 16 * j
                part = arrived[p, start : start + 16, :].astype(F32)
                acc[head, at, :] += part * factor[start : start + 16]
        return low + share

    low = lax.fori_loop(0, NCHIP, add, share, unroll=4)
    factor = on_rows(halves(1.0 / low), whole)
    for head in range(HEADS):
        out[:, head * HD : (head + 1) * HD] = (
            acc[head] * factor[head * TOK : (head + 1) * TOK]
        ).astype(BF16)


def merge_attention(codes, arrived, own, own_sums):
    return pl.pallas_call(
        merge_kernel,
        out_shape=jax.ShapeDtypeStruct((TOK, HEADS * HD), BF16),
        in_specs=[smem()] + [hbm()] * 3,
        out_specs=vmem(),
        scratch_shapes=[
            pltpu.VMEM((HEADS, TOK, HD), F32),
            pltpu.VMEM((NCHIP, 8, TOK), F32),
            pltpu.VMEM((NCHIP, BLOCK, HD), BF16),
            pltpu.VMEM((HEADS, TOK, HD), F32),
            pltpu.VMEM((8, TOK), F32),
            pltpu.SemaphoreType.DMA((2 + MERGE_PARTS,)),
        ],
        compiler_params=pltpu.CompilerParams(vmem_limit_bytes=62 << 20),
        cost_estimate=pl.CostEstimate(
            flops=64 << 20, bytes_accessed=4 << 20, transcendentals=1 << 18
        ),
        name="merge_attention",
    )(codes, arrived, own, own_sums)


def project_kernel(
    side, att, att_far, weight, weight_far, residual, gain, picks, mixed, sent, both, kept, rows, sems
):
    half = residual.shape[1] // 2
    steps, step = rows.shape[0], rows.shape[1]
    total = residual[...].astype(F32)
    total += jnp.dot(att[...], weight[...], preferred_element_type=F32)
    total += jnp.dot(att_far[...], weight_far[...], preferred_element_type=F32)
    kept[...] = jnp.where(side[0] == 0, total[:, :half], total[:, half:])
    keep = pltpu.make_async_copy(kept, mixed, sems.at[steps])
    keep.start()
    scale = lax.rsqrt(jnp.mean(total * total, axis=1, keepdims=True) + NORM_EPS)
    normed = (total * scale * gain[...]).astype(BF16)
    both[:TOK] = normed[:, :half]
    both[TOK:] = normed[:, half:]
    copies = []
    for i in range(steps):
        rows[i] = jnp.dot(
            picks[i * step : (i + 1) * step], both[...], preferred_element_type=F32
        ).astype(BF16)
        copies.append(
            pltpu.make_async_copy(rows.at[i], sent.at[pl.ds(i * step, step)], sems.at[i])
        )
        copies[-1].start()
    keep.wait()
    for copy in copies:
        copy.wait()


def project(side, att, att_far, weight, weight_far, residual, gain, picks, steps=4):
    width = residual.shape[1]
    step = picks.shape[0] // steps
    return pl.pallas_call(
        project_kernel,
        out_shape=(
            jax.ShapeDtypeStruct((TOK, width // 2), F32),
            jax.ShapeDtypeStruct((picks.shape[0], width // 2), BF16),
        ),
        in_specs=[smem()] + [vmem()] * 7,
        out_specs=(hbm(), hbm()),
        scratch_shapes=[
            pltpu.VMEM((2 * TOK, width // 2), BF16),
            pltpu.VMEM((TOK, width // 2), F32),
            pltpu.VMEM((steps, step, width // 2), BF16),
            pltpu.SemaphoreType.DMA((steps + 1,)),
        ],
        compiler_params=pltpu.CompilerParams(vmem_limit_bytes=62 << 20),
        cost_estimate=pl.CostEstimate(
            flops=4 * TOK * 512 * width + 2 * picks.shape[0] * 256 * width // 2,
            bytes_accessed=10 << 20,
            transcendentals=TOK,
        ),
        name="project_dispatch",
    )(side, att, att_far, weight, weight_far, residual, gain, picks)


def expert_kernel(rows, gate, up, down, out, rows_v, gate_v, up_v, down_v, out_v, sems, back):
    steps, count = rows_v.shape[0], rows_v.shape[1]
    width = gate.shape[0]
    half, quarter = width // 2, width // 4

    def fetch(i):
        return pltpu.make_async_copy(rows.at[pl.ds(i * count, count)], rows_v.at[i], sems.at[i])

    def send(i):
        return pltpu.make_async_copy(out_v.at[i], out.at[pl.ds(i * count, count)], back.at[i])

    loads = [
        pltpu.make_async_copy(src, dst, sems.at[steps + n])
        for n, (src, dst) in enumerate(((gate, gate_v), (up, up_v), (down, down_v)))
    ]
    fetch(0).start()
    for load in loads:
        load.start()
    for i in range(1, steps):
        fetch(i).start()
    low_half = lax.broadcasted_iota(jnp.int32, (count // 2, 8, half), 1) < 4
    low_quarter = lax.broadcasted_iota(jnp.int32, (count // 2, 8, quarter), 1) < 4
    def step(i, carry):
        fetch(i).wait()
        wide = rows_v[i].astype(F32)
        tail = wide[:, 16:24].reshape(count // 2, 2, 8, half)
        even, odd = tail[:, 0], tail[:, 1]
        tail_0 = jnp.where(low_half, even, pltpu.roll(odd, 4, 1))
        tail_1 = jnp.where(low_half, pltpu.roll(even, 4, 1), odd)
        left = jnp.concatenate(
            [wide[:, 0:8].reshape(count * 8, half), tail_0.reshape(count * 4, half)], axis=0
        )
        right = jnp.concatenate(
            [wide[:, 8:16].reshape(count * 8, half), tail_1.reshape(count * 4, half)], axis=0
        )
        tokens = jnp.concatenate([left.astype(BF16), right.astype(BF16)], axis=1)
        pl.when(i == 0)(loads[0].wait)
        gate_act = jnp.dot(tokens, gate_v[...], preferred_element_type=F32)
        pl.when(i == 0)(loads[1].wait)
        up_act = jnp.dot(tokens, up_v[...], preferred_element_type=F32)
        hidden = (gate_act / (1.0 + jnp.exp(-gate_act)) * up_act).astype(BF16)
        pl.when(i == 0)(loads[2].wait)
        result = jnp.dot(hidden, down_v[...], preferred_element_type=F32)
        for side in range(2):
            cols = [slice((2 * side + q) * quarter, (2 * side + q + 1) * quarter) for q in range(2)]
            main = [result[: count * 8, c].reshape(count, 8, quarter) for c in cols]
            tail = [result[count * 8 :, c].reshape(count // 2, 8, quarter) for c in cols]
            even = jnp.where(low_quarter, tail[0], pltpu.roll(tail[1], 4, 1))
            odd = jnp.where(low_quarter, pltpu.roll(tail[0], 4, 1), tail[1])
            last = jnp.stack([even, odd], axis=1).reshape(count, 8, quarter)
            out_v[i, :, side] = jnp.concatenate(main + [last], axis=1).astype(BF16)
        send(i).start()
        return carry

    lax.fori_loop(0, steps, step, 0)
    for i in range(steps):
        send(i).wait()


def run_expert(rows, gate, up, down, steps=4):
    count = rows.shape[0] // steps
    width, hidden = gate.shape
    return pl.pallas_call(
        expert_kernel,
        out_shape=jax.ShapeDtypeStruct((rows.shape[0], 2, 2 * CAP, width // 4), BF16),
        in_specs=[hbm()] * 4,
        out_specs=hbm(),
        scratch_shapes=[
            pltpu.VMEM((steps, count, 2 * CAP, width // 2), BF16),
            pltpu.VMEM((width, hidden), BF16),
            pltpu.VMEM((width, hidden), BF16),
            pltpu.VMEM((hidden, width), BF16),
            pltpu.VMEM((steps, count, 2, 2 * CAP, width // 4), BF16),
            pltpu.SemaphoreType.DMA((steps + 3,)),
            pltpu.SemaphoreType.DMA((steps,)),
        ],
        compiler_params=pltpu.CompilerParams(vmem_limit_bytes=62 << 20),
        cost_estimate=pl.CostEstimate(
            flops=6 * rows.shape[0] * CAP * width * hidden,
            bytes_accessed=15 << 20,
            transcendentals=rows.shape[0] * CAP * hidden,
        ),
        name="expert",
    )(rows, gate, up, down)


def combine_kernel(mixed, shares, rows, out, mixed_v, shares_v, rows_v, sems):
    parts, depth, width = rows_v.shape
    loads = [
        pltpu.make_async_copy(rows.at[pl.ds(i * depth, depth)], rows_v.at[i], sems.at[i])
        for i in range(parts)
    ]
    share_load = pltpu.make_async_copy(shares, shares_v, sems.at[parts])
    mixed_load = pltpu.make_async_copy(mixed, mixed_v, sems.at[parts + 1])
    share_load.start()
    for load in loads:
        load.start()
    mixed_load.start()
    share_load.wait()
    total = jnp.zeros((shares_v.shape[0], width), F32)
    for i in range(parts):
        loads[i].wait()
        total += jnp.dot(
            shares_v[:, i * depth : (i + 1) * depth], rows_v[i], preferred_element_type=F32
        )
    mixed_load.wait()
    out[:, :width] = (mixed_v[:, :width] + total[:TOK]).astype(BF16)
    out[:, width:] = (mixed_v[:, width:] + total[TOK:]).astype(BF16)


def combine(mixed, shares, rows, parts=4):
    return pl.pallas_call(
        combine_kernel,
        out_shape=jax.ShapeDtypeStruct(mixed.shape, BF16),
        in_specs=[hbm()] * 3,
        out_specs=vmem(),
        scratch_shapes=[
            pltpu.VMEM(mixed.shape, F32),
            pltpu.VMEM(shares.shape, BF16),
            pltpu.VMEM((parts, rows.shape[0] // parts, rows.shape[1]), BF16),
            pltpu.SemaphoreType.DMA((parts + 2,)),
        ],
        compiler_params=pltpu.CompilerParams(vmem_limit_bytes=62 << 20),
        cost_estimate=pl.CostEstimate(
            flops=2 * shares.shape[0] * rows.shape[0] * rows.shape[1],
            bytes_accessed=6 << 20,
            transcendentals=0,
        ),
        name="combine",
    )(mixed, shares, rows)


def slot_rows():
    slot = np.array(list(range(8)) * 2 + list(range(8, 12)) * 2, np.int32)
    part = np.array([0] * 8 + [1] * 8 + [0] * 4 + [1] * 4, np.int32)
    return slot, part


def routing(expert_ids, expert_weights):
    flat = expert_ids.reshape(-1)
    count = flat.shape[0]
    onehot = (flat[:, None] == jnp.arange(NREQ, dtype=jnp.int32)[None, :]).astype(BF16)
    earlier = (
        jnp.arange(count, dtype=jnp.int32)[None, :] < jnp.arange(count, dtype=jnp.int32)[:, None]
    ).astype(BF16)
    before = jnp.dot(earlier, onehot, preferred_element_type=F32)
    slot = jnp.sum(before * onehot.astype(F32), axis=1).astype(jnp.int32)
    place = (flat * CAP + slot).reshape(TOK, TOP)

    slot_at, part_at = slot_rows()
    row_place = (np.arange(NREQ, dtype=np.int32)[:, None] * CAP + slot_at[None, :]).reshape(-1)
    row_part = np.tile(part_at, NREQ)
    col_place = jnp.concatenate([place, place], axis=0)
    col_part = np.repeat(np.arange(2, dtype=np.int32), TOK)
    hit = jnp.zeros((row_place.shape[0], 2 * TOK), jnp.bool_)
    for k in range(TOP):
        hit = hit | (col_place[None, :, k] == row_place[:, None])
    picks = (hit & (row_part[:, None] == col_part[None, :])).astype(BF16)

    back_place = np.repeat(row_place.reshape(NREQ, 1, -1), 2, axis=1).reshape(-1)
    back_part = np.tile(part_at, 2 * NREQ)
    col_weight = jnp.concatenate([expert_weights, expert_weights], axis=0)
    shares = jnp.zeros((2 * TOK, back_place.shape[0]), F32)
    for k in range(TOP):
        shares = shares + jnp.where(
            col_place[:, k, None] == back_place[None, :], col_weight[:, k, None], 0.0
        )
    shares = jnp.where(back_part[None, :] == col_part[:, None], shares, 0.0)
    return picks, shares.astype(BF16)


def shards(
    residual,
    queries,
    new_keys,
    new_values,
    request_ids,
    page_store,
    page_sends,
    page_users,
    expert_ids,
    expert_weights,
    output_weight,
    norm_gain,
    gate_weight,
    up_weight,
    down_weight,
):
    me = lax.axis_index("req")
    width = residual.shape[1]
    half = width // 2
    swap = [(0, 1), (1, 0)]

    core = me % NC
    users = page_users[0].reshape(NCHIP, NC)
    user_a = jnp.where(core == 0, users[:, 0], users[:, 1])[:, None]
    user_b = jnp.where(core == 0, users[:, 1], users[:, 0])[:, None]
    group = jnp.arange(TOK // 16, dtype=jnp.int32)
    group_user = request_ids.reshape(TOK // 16, 16)[:, 0][None, :]
    hit_a, hit_b = group_user == user_a, group_user == user_b
    needed = (hit_a | hit_b).astype(jnp.int32)
    rank = jnp.sum(needed[:, None, :] * (group[None, :] < group[:, None]), axis=2)
    value = needed * (group[None, :] + 8 * hit_a + 16 * hit_b)
    slot = jnp.arange(SLOTS, dtype=jnp.int32)
    codes = jnp.sum(jnp.where(rank[:, None, :] == slot[None, :, None], value[:, None, :], 0), 2)

    note = jnp.zeros((8, queries.shape[1]), BF16)
    note = note.at[0, : NCHIP * SLOTS].set(codes.T.reshape(-1).astype(BF16))
    pieces, (weight_far, pages_far, sends_far) = gather_blocks(
        jnp.concatenate([queries, note], axis=0), output_weight, page_store, page_sends
    )
    keys_a, keys_b = turn_keys(page_store), turn_keys(pages_far)
    own, own_sums = own_attention(request_ids, queries, new_keys, new_values)

    table = chip_table()
    order = np.array([0, 1, 3, 2])
    chips = lax.dynamic_index_in_dim(
        jnp.asarray(table.reshape(NREQ, 4, 8)[:, order].reshape(NREQ, NCHIP)), me, 0, keepdims=False
    )
    page_a = page_sends[0][chips * NC + core]
    page_b = sends_far[0][chips * NC + core]
    parts = None
    for index, piece in enumerate(pieces):
        if index == 3:
            piece, weight_far = lax.optimization_barrier((piece, weight_far))
        asked = piece[:, TOK, : NCHIP * SLOTS].reshape(8, SLOTS, NCHIP)
        asked = lax.dynamic_index_in_dim(asked, me // NC, 2, keepdims=False)
        rows = slice(8 * index, 8 * index + 8)
        parts = page_attention(
            chips[rows],
            page_a[rows],
            page_b[rows],
            asked.astype(jnp.int32).reshape(-1),
            piece,
            keys_a,
            keys_b,
            page_store,
            pages_far,
            parts,
        )
    arrived = lax.all_to_all(
        parts, "req", 0, 0, tiled=True, axis_index_groups=core_groups()
    )
    attended = merge_attention(codes.reshape(-1), arrived, own, own_sums)
    picks, shares = routing(expert_ids, expert_weights)
    attended_far = lax.ppermute(attended, "tp", swap)
    mixed, sent = project(
        lax.axis_index("tp")[None],
        attended,
        attended_far,
        output_weight,
        weight_far,
        residual,
        norm_gain[None, :],
        picks,
    )
    rows = lax.all_to_all(sent.reshape(NREQ, 2 * CAP, half), "req", 0, 0, tiled=True)
    result = run_expert(rows, gate_weight[0], up_weight[0], down_weight[0])
    returned = lax.all_to_all(
        result.reshape(2 * NREQ, 2 * CAP, width // 4), ("req", "tp"), 0, 0, tiled=True
    )
    return combine(mixed, shares, returned.reshape(-1, width // 4))


def solution(mesh):
    placed = (
        P("req", None),
        P("req", "tp"),
        P("req", "tp"),
        P("req", "tp"),
        P("req"),
        P("req", None, None, "tp"),
        P("req", None),
        P("req", None),
        P("req", None),
        P("req", None),
        P("tp", None),
        P(),
        P("req", None, "tp"),
        P("req", None, "tp"),
        P("req", "tp", None),
    )
    return jax.shard_map(
        shards, mesh=mesh, in_specs=placed, out_specs=P("req", "tp"), check_vma=False
    )
```

```python
import math

import jax
import jax.numpy as jnp
import numpy as np
from jax import lax
from jax.experimental import pallas as pl
from jax.experimental.pallas import tpu as pltpu
from jax.sharding import PartitionSpec as P

HD = 128
TOP = 4
HEADS = 4
PAGE = 128
TOK = 128
CAP = 12
SLOTS = 6
ROWS = SLOTS * 16
STAT = HEADS * ROWS
BLOCK = STAT + 16
MERGE_PARTS = 2
NORM_EPS = 1e-06
SCALE = 1.0 / math.sqrt(HD)
LOG2E = math.log2(math.e)
NEG = -1e30
F32 = jnp.float32
BF16 = jnp.bfloat16

NY, NZ, NX, NC = 4, 4, 2, 2
NREQ = NY * NZ * NX * NC
NCHIP = NY * NZ * NX


def req_index(y, z, x, c):
    return ((y * NZ + z) * NX + x) * NC + c


def all_coords():
    return [
        (y, z, x, c) for y in range(NY) for z in range(NZ) for x in range(NX) for c in range(NC)
    ]


def perm_x():
    return [(req_index(y, z, x, c), req_index(y, z, 1 - x, c)) for y, z, x, c in all_coords()]


def perm_core():
    return [(req_index(y, z, x, c), req_index(y, z, x, 1 - c)) for y, z, x, c in all_coords()]


def perm_ring(stage, step):
    pairs = []
    for y, z, x, c in all_coords():
        if (c + stage) % 2 == 0:
            to = req_index((y + step) % NY, z, x, c)
        else:
            to = req_index(y, (z + step) % NZ, x, c)
        pairs.append((req_index(y, z, x, c), to))
    return pairs


def chip_table():
    table = np.zeros((NREQ, NCHIP), np.int32)
    for y, z, x, c in all_coords():
        row = []
        for d1 in range(4):
            for d0 in range(4):
                for dx in range(2):
                    dy, dz = (d0, d1) if c == 0 else (d1, d0)
                    row.append(req_index((y - dy) % NY, (z - dz) % NZ, x ^ dx, 0) // NC)
        table[req_index(y, z, x, c)] = row
    return table


def core_groups():
    return [[chip * NC + core for chip in range(NCHIP)] for core in range(NC)]


def gather_near(queries, note, pages, sends):
    near = lax.ppermute(queries, "req", perm_x())
    near_note = lax.ppermute(note, "req", perm_x())
    pages = lax.ppermute(pages, "req", perm_core())
    sends = lax.ppermute(sends, "req", perm_core())
    return near, near_note, pages, sends


def gather_line(pair):
    line = [pair] + [lax.ppermute(pair, "req", perm_ring(0, step)) for step in (1, 2, 3)]
    return jnp.stack(line).reshape(8, *pair.shape[1:])


def gather_rest(line):
    return [line] + [lax.ppermute(line, "req", perm_ring(1, step)) for step in (1, 3, 2)]


def attend(query, key_t, value_1, shift):
    scores = jnp.dot(query, key_t, preferred_element_type=F32)
    scores = shift(scores)
    top = jnp.max(scores, axis=1, keepdims=True)
    probs = jnp.exp2((scores - top) * (SCALE * LOG2E)).astype(BF16)
    both = jnp.dot(probs, value_1, preferred_element_type=F32)
    total = both[:, HD:]
    return both[:, :HD] / total, top * SCALE + jnp.log(total)


def by_head(rows):
    head = lax.broadcasted_iota(jnp.int32, (8, 128), 0) % HEADS
    tile = jnp.where(head == 0, rows[0], rows[1])
    tile = jnp.where(head == 2, rows[2], tile)
    return jnp.where(head == 3, rows[3], tile)


def keys_kernel(pages, out):
    def step(page, carry):
        for head in range(HEADS):
            out[page, head] = pages[page, 0, :, head * HD : (head + 1) * HD].T
        return carry

    lax.fori_loop(0, pages.shape[0], step, 0, unroll=2)


def turn_keys(pages):
    count = pages.shape[0]
    return pl.pallas_call(
        keys_kernel,
        out_shape=jax.ShapeDtypeStruct((count, HEADS, HD, PAGE), BF16),
        in_specs=[pl.BlockSpec((count, 1, PAGE, HEADS * HD), lambda i: (0, 0, 0, 0))],
        out_specs=pl.BlockSpec((count, HEADS, HD, PAGE), lambda i: (0, 0, 0, 0)),
        grid=(1,),
        cost_estimate=pl.CostEstimate(
            flops=32 << 20, bytes_accessed=3 << 20, transcendentals=0
        ),
        compiler_params=pltpu.CompilerParams(vmem_limit_bytes=62 << 20),
        name="turn_keys",
    )(pages)


def page_kernel(chip_of, page_a, page_b, codes, blocks_in, keys_a_in, keys_b_in, pages_a_in, pages_b_in, *refs):
    out, blocks, keys_a, keys_b, values_a, values_b, held, sems, load_sems = refs[-9:]
    loads = [
        pltpu.make_async_copy(source, target, load_sems.at[n])
        for n, (source, target) in enumerate(
            (
                (keys_a_in, keys_a),
                (keys_b_in, keys_b),
                (blocks_in, blocks),
                (pages_a_in.at[:, 1], values_a),
                (pages_b_in.at[:, 1], values_b),
            )
        )
    ]
    for load in loads:
        load.start()
    row = lax.broadcasted_iota(jnp.int32, (16, 128), 0)
    offset = lax.broadcasted_iota(jnp.int32, (16, 128), 1) - row
    sub = lax.broadcasted_iota(jnp.int32, (8, 128), 0)
    ones = jnp.ones((PAGE, HD), BF16)
    for load in loads:
        load.wait()

    def copy(i):
        return pltpu.make_async_copy(held.at[i], out.at[chip_of[i]], sems.at[i])

    def step(i, carry):
        pa, pb = page_a[i], page_b[i]
        code = [codes[i * SLOTS + j] for j in range(SLOTS)]
        first = [pl.multiple_of((c & 7) * 16, 16) for c in code]
        bias = jnp.concatenate(
            [
                jnp.concatenate(
                    [
                        jnp.full((16, PAGE), jnp.where((c & bit) != 0, 0.0, NEG), F32)
                        for bit in (8, 16)
                    ],
                    axis=1,
                )
                for c in code
            ],
            axis=0,
        )
        mine = [offset == jnp.where(c >= 8, (c & 7) * 16, -1024) for c in code]
        scores = []
        for head in range(HEADS):
            cols = slice(head * HD, (head + 1) * HD)
            query = jnp.concatenate(
                [blocks[i, pl.ds(first[j], 16), cols] for j in range(SLOTS)], axis=0
            )
            key_t = jnp.concatenate([keys_a[pa, head], keys_b[pb, head]], axis=1)
            scores.append(jnp.dot(query, key_t, preferred_element_type=F32) + bias)
        tops = [jnp.max(s, axis=1, keepdims=True) for s in scores]
        probs = [
            jnp.exp2((s - t) * (SCALE * LOG2E)).astype(BF16) for s, t in zip(scores, tops)
        ]
        boths = []
        for head in range(HEADS):
            cols = slice(head * HD, (head + 1) * HD)
            value_1 = jnp.concatenate(
                [
                    jnp.concatenate([values_a[pa, :, cols], ones], axis=1),
                    jnp.concatenate([values_b[pb, :, cols], ones], axis=1),
                ],
                axis=0,
            )
            boths.append(jnp.dot(probs[head], value_1, preferred_element_type=F32))
        sums = []
        for head in range(HEADS):
            total = boths[head][:, HD:]
            got = boths[head][:, :HD] / total
            held[i, head * ROWS : (head + 1) * ROWS, :] = got.astype(BF16)
            total = tops[head] * SCALE + jnp.log(total)
            here = jnp.where(mine[0], total[:16], NEG)
            for j in range(1, SLOTS):
                here = jnp.maximum(here, jnp.where(mine[j], total[16 * j : 16 * j + 16], NEG))
            sums.append(jnp.max(here, axis=0, keepdims=True))
        tile = by_head(sums)
        high = tile.astype(BF16).astype(F32)
        rest = tile - high
        middle = rest.astype(BF16).astype(F32)
        upper = jnp.where(sub < HEADS, high, middle)
        lower = jnp.where(sub < HEADS, rest - middle, 0.0)
        held[i, STAT:BLOCK, :] = jnp.concatenate([upper, lower], axis=0).astype(BF16)
        copy(i).start()
        return carry

    count = blocks.shape[0]
    lax.fori_loop(0, count, step, 0, unroll=4)
    lax.fori_loop(0, count, lambda i, carry: (copy(i).wait(), carry)[1], 0)


def page_attention(chip_of, page_a, page_b, codes, blocks, keys_a, keys_b, pages_a, pages_b, last):
    count = blocks.shape[0]
    before = [] if last is None else [last]
    return pl.pallas_call(
        page_kernel,
        out_shape=jax.ShapeDtypeStruct((NCHIP, BLOCK, HD), BF16),
        in_specs=[smem()] * 4
        + [hbm()] * (5 + len(before)),
        out_specs=hbm(),
        input_output_aliases={9: 0} if before else {},
        scratch_shapes=[
            pltpu.VMEM(blocks.shape, BF16),
            pltpu.VMEM(keys_a.shape, BF16),
            pltpu.VMEM(keys_b.shape, BF16),
            pltpu.VMEM((pages_a.shape[0], PAGE, HEADS * HD), BF16),
            pltpu.VMEM((pages_b.shape[0], PAGE, HEADS * HD), BF16),
            pltpu.VMEM((count, BLOCK, HD), BF16),
            pltpu.SemaphoreType.DMA((count,)),
            pltpu.SemaphoreType.DMA((5,)),
        ],
        compiler_params=pltpu.CompilerParams(vmem_limit_bytes=62 << 20),
        cost_estimate=pl.CostEstimate(
            flops=count * HEADS * 16 * ROWS * HD * HD,
            bytes_accessed=5 << 20,
            transcendentals=count * HEADS * ROWS * 2 * PAGE,
        ),
        name="page_attention",
    )(chip_of, page_a, page_b, codes, blocks, keys_a, keys_b, pages_a, pages_b, *before)


def smem():
    return pl.BlockSpec(memory_space=pltpu.SMEM)


def hbm():
    return pl.BlockSpec(memory_space=pltpu.HBM)


def vmem():
    return pl.BlockSpec(memory_space=pltpu.VMEM)


def own_kernel(request_col, request_row, queries, keys, values, out_hbm, total_hbm, out, total, sems):
    token = lax.broadcasted_iota(jnp.int32, (TOK, TOK), 0)
    key = lax.broadcasted_iota(jnp.int32, (TOK, TOK), 1)
    mask = (request_col[...] == request_row[...]) & (key <= token)
    ones = jnp.ones((TOK, HD), BF16)
    sums = []
    for head in range(HEADS):
        cols = slice(head * HD, (head + 1) * HD)
        got, low = attend(
            queries[:, cols],
            keys[:, cols].T,
            jnp.concatenate([values[:, cols], ones], axis=1),
            lambda s: jnp.where(mask, s, NEG),
        )
        out[head] = got
        sums.append(jnp.max(jnp.where(token == key, low, NEG), axis=0, keepdims=True))
    total[...] = by_head(sums)
    copies = [
        pltpu.make_async_copy(out, out_hbm, sems.at[0]),
        pltpu.make_async_copy(total, total_hbm, sems.at[1]),
    ]
    for copy in copies:
        copy.start()
    for copy in copies:
        copy.wait()


def own_attention(request_ids, queries, keys, values):
    return pl.pallas_call(
        own_kernel,
        out_shape=(
            jax.ShapeDtypeStruct((HEADS, TOK, HD), F32),
            jax.ShapeDtypeStruct((8, TOK), F32),
        ),
        in_specs=[vmem()] * 5,
        out_specs=(hbm(), hbm()),
        scratch_shapes=[
            pltpu.VMEM((HEADS, TOK, HD), F32),
            pltpu.VMEM((8, TOK), F32),
            pltpu.SemaphoreType.DMA((2,)),
        ],
        compiler_params=pltpu.CompilerParams(vmem_limit_bytes=62 << 20),
        cost_estimate=pl.CostEstimate(
            flops=64 << 20, bytes_accessed=1 << 20, transcendentals=HEADS * TOK * TOK
        ),
        name="own_attention",
    )(request_ids[:, None], request_ids[None, :], queries, keys, values)


def merge_kernel(
    codes, arrived_in, own_in, own_sums_in, out, acc, tiles, arrived, own, own_sums, sems
):
    part = NCHIP // MERGE_PARTS
    loads = [
        pltpu.make_async_copy(own_sums_in, own_sums, sems.at[0]),
        pltpu.make_async_copy(own_in, own, sems.at[1]),
    ] + [
        pltpu.make_async_copy(
            arrived_in.at[pl.ds(i * part, part)], arrived.at[pl.ds(i * part, part)], sems.at[2 + i]
        )
        for i in range(MERGE_PARTS)
    ]
    for load in loads:
        load.start()
    row = lax.broadcasted_iota(jnp.int32, (16, TOK), 0)
    offset = lax.broadcasted_iota(jnp.int32, (16, TOK), 1) - row
    ones = jnp.ones((2 * TOK, HD), BF16)

    def halves(tile):
        high = tile.astype(BF16).astype(F32)
        return high, tile - high

    def on_rows(parts, masks):
        blocks = []
        for head in range(HEADS):
            for mask in masks:
                blocks.append(
                    jnp.concatenate(
                        [
                            jnp.where(mask, jnp.broadcast_to(p[head : head + 1], (16, TOK)), 0.0)
                            for p in parts
                        ],
                        axis=1,
                    )
                )
        picked = jnp.concatenate(blocks, axis=0).astype(BF16)
        return jnp.dot(picked, ones, preferred_element_type=F32)

    def collect(p, top):
        tile = arrived[p, STAT:BLOCK, :].astype(F32)
        tile = (tile[:8] + pltpu.roll(tile[:8], HEADS, 0)) + tile[8:]
        tiles[p] = tile
        return jnp.maximum(top, tile)

    loads[0].wait()
    top = own_sums[...]
    for i in range(MERGE_PARTS):
        loads[2 + i].wait()
        top = lax.fori_loop(i * part, (i + 1) * part, collect, top, unroll=4)
    loads[1].wait()
    whole = [offset == 16 * g for g in range(TOK // 16)]
    share = jnp.exp(own_sums[...] - top)
    acc[...] = own[...] * on_rows(halves(share), whole).reshape(HEADS, TOK, HD)

    def add(p, low):
        share = jnp.exp(tiles[p] - top)
        code = [codes[p * SLOTS + j] for j in range(SLOTS)]
        masks = [offset == jnp.where(c >= 8, (c & 7) * 16, -1024) for c in code]
        factor = on_rows(halves(share), masks)
        for j in range(SLOTS):
            at = pl.ds(pl.multiple_of((code[j] & 7) * 16, 16), 16)
            for head in range(HEADS):
                start = head * ROWS + 16 * j
                part = arrived[p, start : start + 16, :].astype(F32)
                acc[head, at, :] += part * factor[start : start + 16]
        return low + share

    low = lax.fori_loop(0, NCHIP, add, share, unroll=4)
    factor = on_rows(halves(1.0 / low), whole)
    for head in range(HEADS):
        out[:, head * HD : (head + 1) * HD] = (
            acc[head] * factor[head * TOK : (head + 1) * TOK]
        ).astype(BF16)


def merge_attention(codes, arrived, own, own_sums):
    return pl.pallas_call(
        merge_kernel,
        out_shape=jax.ShapeDtypeStruct((TOK, HEADS * HD), BF16),
        in_specs=[smem()] + [hbm()] * 3,
        out_specs=vmem(),
        scratch_shapes=[
            pltpu.VMEM((HEADS, TOK, HD), F32),
            pltpu.VMEM((NCHIP, 8, TOK), F32),
            pltpu.VMEM((NCHIP, BLOCK, HD), BF16),
            pltpu.VMEM((HEADS, TOK, HD), F32),
            pltpu.VMEM((8, TOK), F32),
            pltpu.SemaphoreType.DMA((2 + MERGE_PARTS,)),
        ],
        compiler_params=pltpu.CompilerParams(vmem_limit_bytes=62 << 20),
        cost_estimate=pl.CostEstimate(
            flops=64 << 20, bytes_accessed=4 << 20, transcendentals=1 << 18
        ),
        name="merge_attention",
    )(codes, arrived, own, own_sums)


def project_kernel(
    side, att, att_far, weight, weight_far, residual, gain, picks, mixed, sent, both, kept, rows, sems
):
    half = residual.shape[1] // 2
    steps, step = rows.shape[0], rows.shape[1]
    total = residual[...].astype(F32)
    total += jnp.dot(att[...], weight[...], preferred_element_type=F32)
    total += jnp.dot(att_far[...], weight_far[...], preferred_element_type=F32)
    kept[...] = jnp.where(side[0] == 0, total[:, :half], total[:, half:])
    keep = pltpu.make_async_copy(kept, mixed, sems.at[steps])
    keep.start()
    scale = lax.rsqrt(jnp.mean(total * total, axis=1, keepdims=True) + NORM_EPS)
    normed = (total * scale * gain[...]).astype(BF16)
    both[:TOK] = normed[:, :half]
    both[TOK:] = normed[:, half:]
    copies = []
    for i in range(steps):
        rows[i] = jnp.dot(
            picks[i * step : (i + 1) * step], both[...], preferred_element_type=F32
        ).astype(BF16)
        copies.append(
            pltpu.make_async_copy(rows.at[i], sent.at[pl.ds(i * step, step)], sems.at[i])
        )
        copies[-1].start()
    keep.wait()
    for copy in copies:
        copy.wait()


def project(side, att, att_far, weight, weight_far, residual, gain, picks, steps=4):
    width = residual.shape[1]
    step = picks.shape[0] // steps
    return pl.pallas_call(
        project_kernel,
        out_shape=(
            jax.ShapeDtypeStruct((TOK, width // 2), F32),
            jax.ShapeDtypeStruct((picks.shape[0], width // 2), BF16),
        ),
        in_specs=[smem()] + [vmem()] * 7,
        out_specs=(hbm(), hbm()),
        scratch_shapes=[
            pltpu.VMEM((2 * TOK, width // 2), BF16),
            pltpu.VMEM((TOK, width // 2), F32),
            pltpu.VMEM((steps, step, width // 2), BF16),
            pltpu.SemaphoreType.DMA((steps + 1,)),
        ],
        compiler_params=pltpu.CompilerParams(vmem_limit_bytes=62 << 20),
        cost_estimate=pl.CostEstimate(
            flops=4 * TOK * 512 * width + 2 * picks.shape[0] * 256 * width // 2,
            bytes_accessed=10 << 20,
            transcendentals=TOK,
        ),
        name="project_dispatch",
    )(side, att, att_far, weight, weight_far, residual, gain, picks)


def expert_kernel(rows, gate, up, down, out, rows_v, gate_v, up_v, down_v, out_v, sems, back):
    steps, count = rows_v.shape[0], rows_v.shape[1]
    width = gate.shape[0]
    half, quarter = width // 2, width // 4

    def fetch(i):
        return pltpu.make_async_copy(rows.at[pl.ds(i * count, count)], rows_v.at[i], sems.at[i])

    def send(i):
        return pltpu.make_async_copy(out_v.at[i], out.at[pl.ds(i * count, count)], back.at[i])

    loads = [
        pltpu.make_async_copy(src, dst, sems.at[steps + n])
        for n, (src, dst) in enumerate(((gate, gate_v), (up, up_v), (down, down_v)))
    ]
    fetch(0).start()
    for load in loads:
        load.start()
    for i in range(1, steps):
        fetch(i).start()
    low_half = lax.broadcasted_iota(jnp.int32, (count // 2, 8, half), 1) < 4
    low_quarter = lax.broadcasted_iota(jnp.int32, (count // 2, 8, quarter), 1) < 4
    def step(i, carry):
        fetch(i).wait()
        wide = rows_v[i].astype(F32)
        tail = wide[:, 16:24].reshape(count // 2, 2, 8, half)
        even, odd = tail[:, 0], tail[:, 1]
        tail_0 = jnp.where(low_half, even, pltpu.roll(odd, 4, 1))
        tail_1 = jnp.where(low_half, pltpu.roll(even, 4, 1), odd)
        left = jnp.concatenate(
            [wide[:, 0:8].reshape(count * 8, half), tail_0.reshape(count * 4, half)], axis=0
        )
        right = jnp.concatenate(
            [wide[:, 8:16].reshape(count * 8, half), tail_1.reshape(count * 4, half)], axis=0
        )
        tokens = jnp.concatenate([left.astype(BF16), right.astype(BF16)], axis=1)
        if i == 0:
            loads[0].wait()
        gate_act = jnp.dot(tokens, gate_v[...], preferred_element_type=F32)
        if i == 0:
            loads[1].wait()
        up_act = jnp.dot(tokens, up_v[...], preferred_element_type=F32)
        hidden = (gate_act / (1.0 + jnp.exp(-gate_act)) * up_act).astype(BF16)
        if i == 0:
            loads[2].wait()
        result = jnp.dot(hidden, down_v[...], preferred_element_type=F32)
        for side in range(2):
            cols = [slice((2 * side + q) * quarter, (2 * side + q + 1) * quarter) for q in range(2)]
            main = [result[: count * 8, c].reshape(count, 8, quarter) for c in cols]
            tail = [result[count * 8 :, c].reshape(count // 2, 8, quarter) for c in cols]
            even = jnp.where(low_quarter, tail[0], pltpu.roll(tail[1], 4, 1))
            odd = jnp.where(low_quarter, pltpu.roll(tail[0], 4, 1), tail[1])
            last = jnp.stack([even, odd], axis=1).reshape(count, 8, quarter)
            out_v[i, :, side] = jnp.concatenate(main + [last], axis=1).astype(BF16)
        send(i).start()
        return carry

    for i in range(steps):
        step(i, 0)
    for i in range(steps):
        send(i).wait()


def run_expert(rows, gate, up, down, steps=2):
    count = rows.shape[0] // steps
    width, hidden = gate.shape
    return pl.pallas_call(
        expert_kernel,
        out_shape=jax.ShapeDtypeStruct((rows.shape[0], 2, 2 * CAP, width // 4), BF16),
        in_specs=[hbm()] * 4,
        out_specs=hbm(),
        scratch_shapes=[
            pltpu.VMEM((steps, count, 2 * CAP, width // 2), BF16),
            pltpu.VMEM((width, hidden), BF16),
            pltpu.VMEM((width, hidden), BF16),
            pltpu.VMEM((hidden, width), BF16),
            pltpu.VMEM((steps, count, 2, 2 * CAP, width // 4), BF16),
            pltpu.SemaphoreType.DMA((steps + 3,)),
            pltpu.SemaphoreType.DMA((steps,)),
        ],
        compiler_params=pltpu.CompilerParams(vmem_limit_bytes=62 << 20),
        cost_estimate=pl.CostEstimate(
            flops=6 * rows.shape[0] * CAP * width * hidden,
            bytes_accessed=15 << 20,
            transcendentals=rows.shape[0] * CAP * hidden,
        ),
        name="expert",
    )(rows, gate, up, down)


def combine_kernel(mixed, shares, rows, out, mixed_v, shares_v, rows_v, sems):
    parts, depth, width = rows_v.shape
    loads = [
        pltpu.make_async_copy(rows.at[pl.ds(i * depth, depth)], rows_v.at[i], sems.at[i])
        for i in range(parts)
    ]
    share_load = pltpu.make_async_copy(shares, shares_v, sems.at[parts])
    mixed_load = pltpu.make_async_copy(mixed, mixed_v, sems.at[parts + 1])
    share_load.start()
    for load in loads:
        load.start()
    mixed_load.start()
    share_load.wait()
    total = jnp.zeros((shares_v.shape[0], width), F32)
    for i in range(parts):
        loads[i].wait()
        total += jnp.dot(
            shares_v[:, i * depth : (i + 1) * depth], rows_v[i], preferred_element_type=F32
        )
    mixed_load.wait()
    out[:, :width] = (mixed_v[:, :width] + total[:TOK]).astype(BF16)
    out[:, width:] = (mixed_v[:, width:] + total[TOK:]).astype(BF16)


def combine(mixed, shares, rows, parts=4):
    return pl.pallas_call(
        combine_kernel,
        out_shape=jax.ShapeDtypeStruct(mixed.shape, BF16),
        in_specs=[hbm()] * 3,
        out_specs=vmem(),
        scratch_shapes=[
            pltpu.VMEM(mixed.shape, F32),
            pltpu.VMEM(shares.shape, BF16),
            pltpu.VMEM((parts, rows.shape[0] // parts, rows.shape[1]), BF16),
            pltpu.SemaphoreType.DMA((parts + 2,)),
        ],
        compiler_params=pltpu.CompilerParams(vmem_limit_bytes=62 << 20),
        cost_estimate=pl.CostEstimate(
            flops=2 * shares.shape[0] * rows.shape[0] * rows.shape[1],
            bytes_accessed=6 << 20,
            transcendentals=0,
        ),
        name="combine",
    )(mixed, shares, rows)


def slot_rows():
    slot = np.array(list(range(8)) * 2 + list(range(8, 12)) * 2, np.int32)
    part = np.array([0] * 8 + [1] * 8 + [0] * 4 + [1] * 4, np.int32)
    return slot, part


def routing(expert_ids, expert_weights):
    flat = expert_ids.reshape(-1)
    count = flat.shape[0]
    onehot = (flat[:, None] == jnp.arange(NREQ, dtype=jnp.int32)[None, :]).astype(BF16)
    earlier = (
        jnp.arange(count, dtype=jnp.int32)[None, :] < jnp.arange(count, dtype=jnp.int32)[:, None]
    ).astype(BF16)
    before = jnp.dot(earlier, onehot, preferred_element_type=F32)
    slot = jnp.sum(before * onehot.astype(F32), axis=1).astype(jnp.int32)
    place = (flat * CAP + slot).reshape(TOK, TOP)

    slot_at, part_at = slot_rows()
    row_place = (np.arange(NREQ, dtype=np.int32)[:, None] * CAP + slot_at[None, :]).reshape(-1)
    row_part = np.tile(part_at, NREQ)
    col_place = jnp.concatenate([place, place], axis=0)
    col_part = np.repeat(np.arange(2, dtype=np.int32), TOK)
    hit = jnp.zeros((row_place.shape[0], 2 * TOK), jnp.bool_)
    for k in range(TOP):
        hit = hit | (col_place[None, :, k] == row_place[:, None])
    picks = (hit & (row_part[:, None] == col_part[None, :])).astype(BF16)

    back_place = np.repeat(row_place.reshape(NREQ, 1, -1), 2, axis=1).reshape(-1)
    back_part = np.tile(part_at, 2 * NREQ)
    col_weight = jnp.concatenate([expert_weights, expert_weights], axis=0)
    shares = jnp.zeros((2 * TOK, back_place.shape[0]), F32)
    for k in range(TOP):
        shares = shares + jnp.where(
            col_place[:, k, None] == back_place[None, :], col_weight[:, k, None], 0.0
        )
    shares = jnp.where(back_part[None, :] == col_part[:, None], shares, 0.0)
    return picks, shares.astype(BF16)


def shards(
    residual,
    queries,
    new_keys,
    new_values,
    request_ids,
    page_store,
    page_sends,
    page_users,
    expert_ids,
    expert_weights,
    output_weight,
    norm_gain,
    gate_weight,
    up_weight,
    down_weight,
):
    me = lax.axis_index("req")
    width = residual.shape[1]
    half = width // 2
    swap = [(0, 1), (1, 0)]

    core = me % NC
    users = page_users[0].reshape(NCHIP, NC)
    user_a = jnp.where(core == 0, users[:, 0], users[:, 1])[:, None]
    user_b = jnp.where(core == 0, users[:, 1], users[:, 0])[:, None]
    group = jnp.arange(TOK // 16, dtype=jnp.int32)
    group_user = request_ids.reshape(TOK // 16, 16)[:, 0][None, :]
    hit_a, hit_b = group_user == user_a, group_user == user_b
    needed = (hit_a | hit_b).astype(jnp.int32)
    rank = jnp.sum(needed[:, None, :] * (group[None, :] < group[:, None]), axis=2)
    value = needed * (group[None, :] + 8 * hit_a + 16 * hit_b)
    slot = jnp.arange(SLOTS, dtype=jnp.int32)
    codes = jnp.sum(jnp.where(rank[:, None, :] == slot[None, :, None], value[:, None, :], 0), 2)

    note = jnp.zeros((8, queries.shape[1]), BF16)
    note = note.at[0, : NCHIP * SLOTS].set(codes.T.reshape(-1).astype(BF16))
    near, near_note, pages_far, sends_far = gather_near(queries, note, page_store, page_sends)
    near, near_note, far_in, pages_far, sends_far = lax.optimization_barrier(
        (near, near_note, output_weight, pages_far, sends_far)
    )
    weight_far = lax.ppermute(far_in, "tp", swap)
    pair = jnp.stack(
        [jnp.concatenate([queries, note], axis=0), jnp.concatenate([near, near_note], axis=0)]
    )
    line = gather_line(pair)

    table = chip_table()
    order = np.array([0, 1, 3, 2])
    chips = lax.dynamic_index_in_dim(
        jnp.asarray(table.reshape(NREQ, 4, 8)[:, order].reshape(NREQ, NCHIP)), me, 0, keepdims=False
    )
    page_a = page_sends[0][chips * NC + core]
    page_b = sends_far[0][chips * NC + core]
    keys_a, keys_b = turn_keys(page_store), turn_keys(pages_far)
    line, keys_a, keys_b, chips, page_a, page_b = lax.optimization_barrier(
        (line, keys_a, keys_b, chips, page_a, page_b)
    )
    pieces = gather_rest(line)
    own, own_sums = own_attention(request_ids, queries, new_keys, new_values)

    parts = None
    for index, piece in enumerate(pieces):
        if index == 3:
            piece, parts, weight_far = lax.optimization_barrier((piece, parts, weight_far))
        elif index > 0:
            piece, parts = lax.optimization_barrier((piece, parts))
        asked = piece[:, TOK, : NCHIP * SLOTS].reshape(8, SLOTS, NCHIP)
        asked = lax.dynamic_index_in_dim(asked, me // NC, 2, keepdims=False)
        rows = slice(8 * index, 8 * index + 8)
        parts = page_attention(
            chips[rows],
            page_a[rows],
            page_b[rows],
            asked.astype(jnp.int32).reshape(-1),
            piece,
            keys_a,
            keys_b,
            page_store,
            pages_far,
            parts,
        )
    arrived = lax.all_to_all(
        parts, "req", 0, 0, tiled=True, axis_index_groups=core_groups()
    )
    attended = merge_attention(codes.reshape(-1), arrived, own, own_sums)
    picks, shares = routing(expert_ids, expert_weights)
    attended_far = lax.ppermute(attended, "tp", swap)
    mixed, sent = project(
        lax.axis_index("tp")[None],
        attended,
        attended_far,
        output_weight,
        weight_far,
        residual,
        norm_gain[None, :],
        picks,
    )
    rows = lax.all_to_all(sent.reshape(NREQ, 2 * CAP, half), "req", 0, 0, tiled=True)
    result = run_expert(rows, gate_weight[0], up_weight[0], down_weight[0])
    returned = lax.all_to_all(
        result.reshape(2 * NREQ, 2 * CAP, width // 4), ("req", "tp"), 0, 0, tiled=True
    )
    return combine(mixed, shares, returned.reshape(-1, width // 4))


def solution(mesh):
    placed = (
        P("req", None),
        P("req", "tp"),
        P("req", "tp"),
        P("req", "tp"),
        P("req"),
        P("req", None, None, "tp"),
        P("req", None),
        P("req", None),
        P("req", None),
        P("req", None),
        P("tp", None),
        P(),
        P("req", None, "tp"),
        P("req", None, "tp"),
        P("req", "tp", None),
    )
    return jax.shard_map(
        shards, mesh=mesh, in_specs=placed, out_specs=P("req", "tp"), check_vma=False
    )
```

```python
import math

import jax
import jax.numpy as jnp
import numpy as np
from jax import lax
from jax.experimental import pallas as pl
from jax.experimental.pallas import tpu as pltpu
from jax.sharding import PartitionSpec as P

HD = 128
TOP = 4
HEADS = 4
PAGE = 128
TOK = 128
CAP = 12
SLOTS = 6
ROWS = SLOTS * 16
STAT = HEADS * ROWS
BLOCK = STAT + 16
MERGE_PARTS = 2
NORM_EPS = 1e-06
SCALE = 1.0 / math.sqrt(HD)
LOG2E = math.log2(math.e)
NEG = -1e30
F32 = jnp.float32
BF16 = jnp.bfloat16

NY, NZ, NX, NC = 4, 4, 2, 2
NREQ = NY * NZ * NX * NC
NCHIP = NY * NZ * NX


def req_index(y, z, x, c):
    return ((y * NZ + z) * NX + x) * NC + c


def all_coords():
    return [
        (y, z, x, c) for y in range(NY) for z in range(NZ) for x in range(NX) for c in range(NC)
    ]


def perm_x():
    return [(req_index(y, z, x, c), req_index(y, z, 1 - x, c)) for y, z, x, c in all_coords()]


def perm_core():
    return [(req_index(y, z, x, c), req_index(y, z, x, 1 - c)) for y, z, x, c in all_coords()]


def perm_ring(stage, step):
    pairs = []
    for y, z, x, c in all_coords():
        if (c + stage) % 2 == 0:
            to = req_index((y + step) % NY, z, x, c)
        else:
            to = req_index(y, (z + step) % NZ, x, c)
        pairs.append((req_index(y, z, x, c), to))
    return pairs


def chip_table():
    table = np.zeros((NREQ, NCHIP), np.int32)
    for y, z, x, c in all_coords():
        row = []
        for d1 in range(4):
            for d0 in range(4):
                for dx in range(2):
                    dy, dz = (d0, d1) if c == 0 else (d1, d0)
                    row.append(req_index((y - dy) % NY, (z - dz) % NZ, x ^ dx, 0) // NC)
        table[req_index(y, z, x, c)] = row
    return table


def core_groups():
    return [[chip * NC + core for chip in range(NCHIP)] for core in range(NC)]


def gather_line(pair):
    line = [pair] + [lax.ppermute(pair, "req", perm_ring(0, step)) for step in (1, 2, 3)]
    return jnp.stack(line).reshape(8, *pair.shape[1:])


def gather_rest(line):
    return [line] + [lax.ppermute(line, "req", perm_ring(1, step)) for step in (1, 3, 2)]


def attend(query, key_t, value_1, shift):
    scores = jnp.dot(query, key_t, preferred_element_type=F32)
    scores = shift(scores)
    top = jnp.max(scores, axis=1, keepdims=True)
    probs = jnp.exp2((scores - top) * (SCALE * LOG2E)).astype(BF16)
    both = jnp.dot(probs, value_1, preferred_element_type=F32)
    total = both[:, HD:]
    return both[:, :HD] / total, top * SCALE + jnp.log(total)


def by_head(rows):
    head = lax.broadcasted_iota(jnp.int32, (8, 128), 0) % HEADS
    tile = jnp.where(head == 0, rows[0], rows[1])
    tile = jnp.where(head == 2, rows[2], tile)
    return jnp.where(head == 3, rows[3], tile)


def page_kernel(chip_of, page_a, page_b, codes, pages_a_in, pages_b_in, *refs):
    out, blocks, pages_a, pages_b, held, sems, load_sems = refs[-7:]
    count = held.shape[0]
    pieces = refs[: count // 8]
    loads = [
        pltpu.make_async_copy(source, target, load_sems.at[n])
        for n, (source, target) in enumerate(
            [(pages_a_in, pages_a), (pages_b_in, pages_b)]
            + [(piece, blocks.at[pl.ds(8 * n, 8)]) for n, piece in enumerate(pieces)]
        )
    ]
    for load in loads:
        load.start()
    row = lax.broadcasted_iota(jnp.int32, (16, 128), 0)
    offset = lax.broadcasted_iota(jnp.int32, (16, 128), 1) - row
    sub = lax.broadcasted_iota(jnp.int32, (8, 128), 0)
    ones = jnp.ones((PAGE, HD), BF16)
    for load in loads:
        load.wait()

    def copy(i):
        return pltpu.make_async_copy(held.at[i], out.at[chip_of[i]], sems.at[i])

    def step(i, carry):
        pa, pb = page_a[i], page_b[i]
        code = [codes[i * SLOTS + j] for j in range(SLOTS)]
        first = [pl.multiple_of((c & 7) * 16, 16) for c in code]
        bias = jnp.concatenate(
            [
                jnp.concatenate(
                    [
                        jnp.full((16, PAGE), jnp.where((c & bit) != 0, 0.0, NEG), F32)
                        for bit in (8, 16)
                    ],
                    axis=1,
                )
                for c in code
            ],
            axis=0,
        )
        mine = [offset == jnp.where(c >= 8, (c & 7) * 16, -1024) for c in code]
        scores = []
        for head in range(HEADS):
            cols = slice(head * HD, (head + 1) * HD)
            query = jnp.concatenate(
                [blocks[i, pl.ds(first[j], 16), cols] for j in range(SLOTS)], axis=0
            )
            key = jnp.concatenate([pages_a[pa, 0, :, cols], pages_b[pb, 0, :, cols]], axis=0)
            scores.append(
                lax.dot_general(
                    query, key, (((1,), (1,)), ((), ())), preferred_element_type=F32
                )
                + bias
            )
        tops = [jnp.max(s, axis=1, keepdims=True) for s in scores]
        probs = [
            jnp.exp2((s - t) * (SCALE * LOG2E)).astype(BF16) for s, t in zip(scores, tops)
        ]
        boths = []
        for head in range(HEADS):
            cols = slice(head * HD, (head + 1) * HD)
            value_1 = jnp.concatenate(
                [
                    jnp.concatenate([pages_a[pa, 1, :, cols], ones], axis=1),
                    jnp.concatenate([pages_b[pb, 1, :, cols], ones], axis=1),
                ],
                axis=0,
            )
            boths.append(jnp.dot(probs[head], value_1, preferred_element_type=F32))
        sums = []
        for head in range(HEADS):
            total = boths[head][:, HD:]
            got = boths[head][:, :HD] / total
            held[i, head * ROWS : (head + 1) * ROWS, :] = got.astype(BF16)
            total = tops[head] * SCALE + jnp.log(total)
            here = jnp.where(mine[0], total[:16], NEG)
            for j in range(1, SLOTS):
                here = jnp.maximum(here, jnp.where(mine[j], total[16 * j : 16 * j + 16], NEG))
            sums.append(jnp.max(here, axis=0, keepdims=True))
        tile = by_head(sums)
        high = tile.astype(BF16).astype(F32)
        rest = tile - high
        middle = rest.astype(BF16).astype(F32)
        upper = jnp.where(sub < HEADS, high, middle)
        lower = jnp.where(sub < HEADS, rest - middle, 0.0)
        held[i, STAT:BLOCK, :] = jnp.concatenate([upper, lower], axis=0).astype(BF16)
        copy(i).start()
        return carry

    lax.fori_loop(0, count, step, 0, unroll=4)
    lax.fori_loop(0, count, lambda i, carry: (copy(i).wait(), carry)[1], 0)


def page_attention(chip_of, page_a, page_b, codes, pages_a, pages_b, pieces, last):
    count = 8 * len(pieces)
    before = [] if last is None else [last]
    return pl.pallas_call(
        page_kernel,
        out_shape=jax.ShapeDtypeStruct((NCHIP, BLOCK, HD), BF16),
        in_specs=[smem()] * 4 + [hbm()] * (2 + len(pieces) + len(before)),
        out_specs=hbm(),
        input_output_aliases={6 + len(pieces): 0} if before else {},
        scratch_shapes=[
            pltpu.VMEM((count, *pieces[0].shape[1:]), BF16),
            pltpu.VMEM(pages_a.shape, BF16),
            pltpu.VMEM(pages_b.shape, BF16),
            pltpu.VMEM((count, BLOCK, HD), BF16),
            pltpu.SemaphoreType.DMA((count,)),
            pltpu.SemaphoreType.DMA((2 + len(pieces),)),
        ],
        compiler_params=pltpu.CompilerParams(vmem_limit_bytes=62 << 20),
        cost_estimate=pl.CostEstimate(
            flops=count * HEADS * 16 * ROWS * HD * HD,
            bytes_accessed=5 << 20,
            transcendentals=count * HEADS * ROWS * 2 * PAGE,
        ),
        name="page_attention",
    )(chip_of, page_a, page_b, codes, pages_a, pages_b, *pieces, *before)


def smem():
    return pl.BlockSpec(memory_space=pltpu.SMEM)


def hbm():
    return pl.BlockSpec(memory_space=pltpu.HBM)


def vmem():
    return pl.BlockSpec(memory_space=pltpu.VMEM)


def own_kernel(request_col, request_row, queries, keys, values, out_hbm, total_hbm, out, total, sems):
    token = lax.broadcasted_iota(jnp.int32, (TOK, TOK), 0)
    key = lax.broadcasted_iota(jnp.int32, (TOK, TOK), 1)
    mask = (request_col[...] == request_row[...]) & (key <= token)
    ones = jnp.ones((TOK, HD), BF16)
    sums = []
    for head in range(HEADS):
        cols = slice(head * HD, (head + 1) * HD)
        got, low = attend(
            queries[:, cols],
            keys[:, cols].T,
            jnp.concatenate([values[:, cols], ones], axis=1),
            lambda s: jnp.where(mask, s, NEG),
        )
        out[head] = got
        sums.append(jnp.max(jnp.where(token == key, low, NEG), axis=0, keepdims=True))
    total[...] = by_head(sums)
    copies = [
        pltpu.make_async_copy(out, out_hbm, sems.at[0]),
        pltpu.make_async_copy(total, total_hbm, sems.at[1]),
    ]
    for copy in copies:
        copy.start()
    for copy in copies:
        copy.wait()


def own_attention(request_ids, queries, keys, values):
    return pl.pallas_call(
        own_kernel,
        out_shape=(
            jax.ShapeDtypeStruct((HEADS, TOK, HD), F32),
            jax.ShapeDtypeStruct((8, TOK), F32),
        ),
        in_specs=[vmem()] * 5,
        out_specs=(hbm(), hbm()),
        scratch_shapes=[
            pltpu.VMEM((HEADS, TOK, HD), F32),
            pltpu.VMEM((8, TOK), F32),
            pltpu.SemaphoreType.DMA((2,)),
        ],
        compiler_params=pltpu.CompilerParams(vmem_limit_bytes=62 << 20),
        cost_estimate=pl.CostEstimate(
            flops=64 << 20, bytes_accessed=1 << 20, transcendentals=HEADS * TOK * TOK
        ),
        name="own_attention",
    )(request_ids[:, None], request_ids[None, :], queries, keys, values)


def merge_kernel(
    codes, arrived_in, own_in, own_sums_in, out, acc, tiles, arrived, own, own_sums, sems
):
    part = NCHIP // MERGE_PARTS
    loads = [
        pltpu.make_async_copy(own_sums_in, own_sums, sems.at[0]),
        pltpu.make_async_copy(own_in, own, sems.at[1]),
    ] + [
        pltpu.make_async_copy(
            arrived_in.at[pl.ds(i * part, part)], arrived.at[pl.ds(i * part, part)], sems.at[2 + i]
        )
        for i in range(MERGE_PARTS)
    ]
    for load in loads:
        load.start()
    row = lax.broadcasted_iota(jnp.int32, (16, TOK), 0)
    offset = lax.broadcasted_iota(jnp.int32, (16, TOK), 1) - row

    def halves(tile):
        high = tile.astype(BF16).astype(F32)
        return high, tile - high

    def on_rows(parts, masks):
        blocks = []
        for head in range(HEADS):
            for mask in masks:
                blocks.append(
                    jnp.concatenate(
                        [
                            jnp.where(mask, jnp.broadcast_to(p[head : head + 1], (16, TOK)), 0.0)
                            for p in parts
                        ],
                        axis=1,
                    )
                )
        picked = jnp.concatenate(blocks, axis=0).astype(BF16)
        ones = jnp.ones((len(parts) * TOK, HD), BF16)
        return jnp.dot(picked, ones, preferred_element_type=F32)

    def collect(p, top):
        tile = arrived[p, STAT:BLOCK, :].astype(F32)
        tile = (tile[:8] + pltpu.roll(tile[:8], HEADS, 0)) + tile[8:]
        tiles[p] = tile
        return jnp.maximum(top, tile)

    loads[0].wait()
    top = own_sums[...]
    for i in range(MERGE_PARTS):
        loads[2 + i].wait()
        top = lax.fori_loop(i * part, (i + 1) * part, collect, top, unroll=4)
    loads[1].wait()
    whole = [offset == 16 * g for g in range(TOK // 16)]
    share = jnp.exp(own_sums[...] - top)
    acc[...] = own[...] * on_rows(halves(share), whole).reshape(HEADS, TOK, HD)

    def add(p, low):
        share = jnp.exp(tiles[p] - top).astype(BF16).astype(F32)
        code = [codes[p * SLOTS + j] for j in range(SLOTS)]
        masks = [offset == jnp.where(c >= 8, (c & 7) * 16, -1024) for c in code]
        factor = on_rows((share,), masks)
        for j in range(SLOTS):
            at = pl.ds(pl.multiple_of((code[j] & 7) * 16, 16), 16)
            for head in range(HEADS):
                start = head * ROWS + 16 * j
                part = arrived[p, start : start + 16, :].astype(F32)
                acc[head, at, :] += part * factor[start : start + 16]
        return low + share

    low = lax.fori_loop(0, NCHIP, add, share, unroll=4)
    factor = on_rows(halves(1.0 / low), whole)
    for head in range(HEADS):
        out[:, head * HD : (head + 1) * HD] = (
            acc[head] * factor[head * TOK : (head + 1) * TOK]
        ).astype(BF16)


def merge_attention(codes, arrived, own, own_sums):
    return pl.pallas_call(
        merge_kernel,
        out_shape=jax.ShapeDtypeStruct((TOK, HEADS * HD), BF16),
        in_specs=[smem()] + [hbm()] * 3,
        out_specs=vmem(),
        scratch_shapes=[
            pltpu.VMEM((HEADS, TOK, HD), F32),
            pltpu.VMEM((NCHIP, 8, TOK), F32),
            pltpu.VMEM((NCHIP, BLOCK, HD), BF16),
            pltpu.VMEM((HEADS, TOK, HD), F32),
            pltpu.VMEM((8, TOK), F32),
            pltpu.SemaphoreType.DMA((2 + MERGE_PARTS,)),
        ],
        compiler_params=pltpu.CompilerParams(vmem_limit_bytes=62 << 20),
        cost_estimate=pl.CostEstimate(
            flops=64 << 20, bytes_accessed=4 << 20, transcendentals=1 << 18
        ),
        name="merge_attention",
    )(codes, arrived, own, own_sums)


def project_kernel(
    side,
    att,
    att_far,
    weight_in,
    weight_far_in,
    residual_in,
    gain,
    picks_in,
    mixed,
    sent,
    both,
    kept,
    rows,
    weight,
    weight_far,
    residual,
    picks,
    load_sems,
    sems,
):
    loads = [
        pltpu.make_async_copy(source, target, load_sems.at[n])
        for n, (source, target) in enumerate(
            (
                (weight_in, weight),
                (residual_in, residual),
                (weight_far_in, weight_far),
                (picks_in, picks),
            )
        )
    ]
    for load in loads:
        load.start()
    half = residual.shape[1] // 2
    steps, step = rows.shape[0], rows.shape[1]
    loads[0].wait()
    total = jnp.dot(att[...], weight[...], preferred_element_type=F32)
    loads[1].wait()
    total += residual[...].astype(F32)
    loads[2].wait()
    total += jnp.dot(att_far[...], weight_far[...], preferred_element_type=F32)
    kept[...] = jnp.where(side[0] == 0, total[:, :half], total[:, half:])
    keep = pltpu.make_async_copy(kept, mixed, sems.at[steps])
    keep.start()
    scale = lax.rsqrt(jnp.mean(total * total, axis=1, keepdims=True) + NORM_EPS)
    normed = (total * scale * gain[...]).astype(BF16)
    both[:TOK] = normed[:, :half]
    both[TOK:] = normed[:, half:]
    copies = []
    loads[3].wait()
    for i in range(steps):
        rows[i] = jnp.dot(
            picks[i * step : (i + 1) * step], both[...], preferred_element_type=F32
        ).astype(BF16)
        copies.append(
            pltpu.make_async_copy(rows.at[i], sent.at[pl.ds(i * step, step)], sems.at[i])
        )
        copies[-1].start()
    keep.wait()
    for copy in copies:
        copy.wait()


def project(side, att, att_far, weight, weight_far, residual, gain, picks, steps=4):
    width = residual.shape[1]
    step = picks.shape[0] // steps
    return pl.pallas_call(
        project_kernel,
        out_shape=(
            jax.ShapeDtypeStruct((TOK, width // 2), F32),
            jax.ShapeDtypeStruct((picks.shape[0], width // 2), BF16),
        ),
        in_specs=[smem(), vmem(), vmem(), hbm(), hbm(), hbm(), vmem(), hbm()],
        out_specs=(hbm(), hbm()),
        scratch_shapes=[
            pltpu.VMEM((2 * TOK, width // 2), BF16),
            pltpu.VMEM((TOK, width // 2), F32),
            pltpu.VMEM((steps, step, width // 2), BF16),
            pltpu.VMEM(weight.shape, BF16),
            pltpu.VMEM(weight_far.shape, BF16),
            pltpu.VMEM(residual.shape, BF16),
            pltpu.VMEM(picks.shape, BF16),
            pltpu.SemaphoreType.DMA((4,)),
            pltpu.SemaphoreType.DMA((steps + 1,)),
        ],
        compiler_params=pltpu.CompilerParams(vmem_limit_bytes=62 << 20),
        cost_estimate=pl.CostEstimate(
            flops=4 * TOK * 512 * width + 2 * picks.shape[0] * 256 * width // 2,
            bytes_accessed=10 << 20,
            transcendentals=TOK,
        ),
        name="project_dispatch",
    )(side, att, att_far, weight, weight_far, residual, gain, picks)


def expert_kernel(rows, gate, up, down, out, rows_v, gate_v, up_v, down_v, out_v, sems, back):
    steps, count = rows_v.shape[0], rows_v.shape[1]
    width = gate.shape[0]
    half, quarter = width // 2, width // 4

    def fetch(i):
        return pltpu.make_async_copy(rows.at[pl.ds(i * count, count)], rows_v.at[i], sems.at[i])

    def send(i):
        return pltpu.make_async_copy(out_v.at[i], out.at[pl.ds(i * count, count)], back.at[i])

    loads = [
        pltpu.make_async_copy(src, dst, sems.at[steps + n])
        for n, (src, dst) in enumerate(((gate, gate_v), (up, up_v), (down, down_v)))
    ]
    fetch(0).start()
    for load in loads:
        load.start()
    for i in range(1, steps):
        fetch(i).start()
    low_half = lax.broadcasted_iota(jnp.int32, (count // 2, 8, half), 1) < 4
    low_quarter = lax.broadcasted_iota(jnp.int32, (count // 2, 8, quarter), 1) < 4
    def step(i, carry):
        fetch(i).wait()
        wide = rows_v[i].astype(F32)
        tail = wide[:, 16:24].reshape(count // 2, 2, 8, half)
        even, odd = tail[:, 0], tail[:, 1]
        tail_0 = jnp.where(low_half, even, pltpu.roll(odd, 4, 1))
        tail_1 = jnp.where(low_half, pltpu.roll(even, 4, 1), odd)
        left = jnp.concatenate(
            [wide[:, 0:8].reshape(count * 8, half), tail_0.reshape(count * 4, half)], axis=0
        )
        right = jnp.concatenate(
            [wide[:, 8:16].reshape(count * 8, half), tail_1.reshape(count * 4, half)], axis=0
        )
        tokens = jnp.concatenate([left.astype(BF16), right.astype(BF16)], axis=1)
        if i == 0:
            loads[0].wait()
        gate_act = jnp.dot(tokens, gate_v[...], preferred_element_type=F32)
        if i == 0:
            loads[1].wait()
        up_act = jnp.dot(tokens, up_v[...], preferred_element_type=F32)
        hidden = (gate_act / (1.0 + jnp.exp(-gate_act)) * up_act).astype(BF16)
        if i == 0:
            loads[2].wait()
        result = jnp.dot(hidden, down_v[...], preferred_element_type=F32)
        for side in range(2):
            cols = [slice((2 * side + q) * quarter, (2 * side + q + 1) * quarter) for q in range(2)]
            main = [result[: count * 8, c].reshape(count, 8, quarter) for c in cols]
            tail = [result[count * 8 :, c].reshape(count // 2, 8, quarter) for c in cols]
            even = jnp.where(low_quarter, tail[0], pltpu.roll(tail[1], 4, 1))
            odd = jnp.where(low_quarter, pltpu.roll(tail[0], 4, 1), tail[1])
            last = jnp.stack([even, odd], axis=1).reshape(count, 8, quarter)
            out_v[i, :, side] = jnp.concatenate(main + [last], axis=1).astype(BF16)
        send(i).start()
        return carry

    for i in range(steps):
        step(i, 0)
    for i in range(steps):
        send(i).wait()


def run_expert(rows, gate, up, down, steps=2):
    count = rows.shape[0] // steps
    width, hidden = gate.shape
    return pl.pallas_call(
        expert_kernel,
        out_shape=jax.ShapeDtypeStruct((rows.shape[0], 2, 2 * CAP, width // 4), BF16),
        in_specs=[hbm()] * 4,
        out_specs=hbm(),
        scratch_shapes=[
            pltpu.VMEM((steps, count, 2 * CAP, width // 2), BF16),
            pltpu.VMEM((width, hidden), BF16),
            pltpu.VMEM((width, hidden), BF16),
            pltpu.VMEM((hidden, width), BF16),
            pltpu.VMEM((steps, count, 2, 2 * CAP, width // 4), BF16),
            pltpu.SemaphoreType.DMA((steps + 3,)),
            pltpu.SemaphoreType.DMA((steps,)),
        ],
        compiler_params=pltpu.CompilerParams(vmem_limit_bytes=62 << 20),
        cost_estimate=pl.CostEstimate(
            flops=6 * rows.shape[0] * CAP * width * hidden,
            bytes_accessed=15 << 20,
            transcendentals=rows.shape[0] * CAP * hidden,
        ),
        name="expert",
    )(rows, gate, up, down)


def combine_kernel(mixed, shares, rows, out, mixed_v, shares_v, rows_v, sems):
    parts, depth, width = rows_v.shape
    loads = [
        pltpu.make_async_copy(rows.at[pl.ds(i * depth, depth)], rows_v.at[i], sems.at[i])
        for i in range(parts)
    ]
    share_load = pltpu.make_async_copy(shares, shares_v, sems.at[parts])
    mixed_load = pltpu.make_async_copy(mixed, mixed_v, sems.at[parts + 1])
    share_load.start()
    for load in loads:
        load.start()
    mixed_load.start()
    share_load.wait()
    total = jnp.zeros((shares_v.shape[0], width), F32)
    for i in range(parts):
        loads[i].wait()
        total += jnp.dot(
            shares_v[:, i * depth : (i + 1) * depth], rows_v[i], preferred_element_type=F32
        )
    mixed_load.wait()
    out[:, :width] = (mixed_v[:, :width] + total[:TOK]).astype(BF16)
    out[:, width:] = (mixed_v[:, width:] + total[TOK:]).astype(BF16)


def combine(mixed, shares, rows, parts=4):
    return pl.pallas_call(
        combine_kernel,
        out_shape=jax.ShapeDtypeStruct(mixed.shape, BF16),
        in_specs=[hbm()] * 3,
        out_specs=vmem(),
        scratch_shapes=[
            pltpu.VMEM(mixed.shape, F32),
            pltpu.VMEM(shares.shape, BF16),
            pltpu.VMEM((parts, rows.shape[0] // parts, rows.shape[1]), BF16),
            pltpu.SemaphoreType.DMA((parts + 2,)),
        ],
        compiler_params=pltpu.CompilerParams(vmem_limit_bytes=62 << 20),
        cost_estimate=pl.CostEstimate(
            flops=2 * shares.shape[0] * rows.shape[0] * rows.shape[1],
            bytes_accessed=6 << 20,
            transcendentals=0,
        ),
        name="combine",
    )(mixed, shares, rows)


def slot_rows():
    slot = np.array(list(range(8)) * 2 + list(range(8, 12)) * 2, np.int32)
    part = np.array([0] * 8 + [1] * 8 + [0] * 4 + [1] * 4, np.int32)
    return slot, part


def routing(expert_ids, expert_weights):
    flat = expert_ids.reshape(-1)
    count = flat.shape[0]
    onehot = (flat[:, None] == jnp.arange(NREQ, dtype=jnp.int32)[None, :]).astype(BF16)
    earlier = (
        jnp.arange(count, dtype=jnp.int32)[None, :] < jnp.arange(count, dtype=jnp.int32)[:, None]
    ).astype(BF16)
    before = jnp.dot(earlier, onehot, preferred_element_type=F32)
    slot = jnp.sum(before * onehot.astype(F32), axis=1).astype(jnp.int32)
    place = (flat * CAP + slot).reshape(TOK, TOP)

    slot_at, part_at = slot_rows()
    row_place = (np.arange(NREQ, dtype=np.int32)[:, None] * CAP + slot_at[None, :]).reshape(-1)
    row_part = np.tile(part_at, NREQ)
    col_place = jnp.concatenate([place, place], axis=0)
    col_part = np.repeat(np.arange(2, dtype=np.int32), TOK)
    hit = jnp.zeros((row_place.shape[0], 2 * TOK), jnp.bool_)
    for k in range(TOP):
        hit = hit | (col_place[None, :, k] == row_place[:, None])
    picks = (hit & (row_part[:, None] == col_part[None, :])).astype(BF16)

    back_place = np.repeat(row_place.reshape(NREQ, 1, -1), 2, axis=1).reshape(-1)
    back_part = np.tile(part_at, 2 * NREQ)
    col_weight = jnp.concatenate([expert_weights, expert_weights], axis=0)
    shares = jnp.zeros((2 * TOK, back_place.shape[0]), F32)
    for k in range(TOP):
        shares = shares + jnp.where(
            col_place[:, k, None] == back_place[None, :], col_weight[:, k, None], 0.0
        )
    shares = jnp.where(back_part[None, :] == col_part[:, None], shares, 0.0)
    return picks, shares.astype(BF16)


def group_codes(users, ids, core):
    users = users.reshape(-1, NCHIP, NC)
    user_a = jnp.where(core == 0, users[..., 0], users[..., 1])[..., None]
    user_b = jnp.where(core == 0, users[..., 1], users[..., 0])[..., None]
    group = jnp.arange(TOK // 16, dtype=jnp.int32)
    group_user = ids.reshape(-1, 1, TOK // 16, 16)[..., 0]
    hit_a, hit_b = group_user == user_a, group_user == user_b
    needed = (hit_a | hit_b).astype(jnp.int32)
    rank = jnp.sum(needed[..., None, :] * (group[None, :] < group[:, None]), axis=-1)
    value = needed * (group + 8 * hit_a + 16 * hit_b)
    slot = jnp.arange(SLOTS, dtype=jnp.int32)
    return jnp.sum(
        jnp.where(rank[..., None, :] == slot[:, None], value[..., None, :], 0), axis=-1
    )


def shards(
    residual,
    queries,
    new_keys,
    new_values,
    request_ids,
    page_store,
    page_sends,
    page_users,
    expert_ids,
    expert_weights,
    output_weight,
    norm_gain,
    gate_weight,
    up_weight,
    down_weight,
):
    me = lax.axis_index("req")
    width = residual.shape[1]
    half = width // 2
    swap = [(0, 1), (1, 0)]

    near, users, ids = [
        jnp.stack([own, lax.ppermute(own, "req", perm_x())])
        for own in (queries, page_users[0], request_ids)
    ]
    pages_far = lax.ppermute(page_store, "req", perm_core())
    sends_far = lax.ppermute(page_sends, "req", perm_core())
    codes = group_codes(users, ids, me % NC)
    note = jnp.zeros((2, 8, queries.shape[1]), BF16)
    note = note.at[:, 0, : NCHIP * SLOTS].set(
        codes.transpose(0, 2, 1).reshape(2, NCHIP * SLOTS).astype(BF16)
    )
    pair = jnp.concatenate([near, note], axis=1)
    pair, far_in, pages_far, sends_far = lax.optimization_barrier(
        (pair, output_weight, pages_far, sends_far)
    )
    weight_far = lax.ppermute(far_in, "tp", swap)
    line = gather_line(pair)

    table = chip_table()
    order = np.array([0, 1, 3, 2])
    chips = lax.dynamic_index_in_dim(
        jnp.asarray(table.reshape(NREQ, 4, 8)[:, order].reshape(NREQ, NCHIP)), me, 0, keepdims=False
    )
    core = me % NC
    page_a = page_sends[0][chips * NC + core]
    page_b = sends_far[0][chips * NC + core]
    line, chips, page_a, page_b = lax.optimization_barrier((line, chips, page_a, page_b))
    pieces = gather_rest(line)
    own, own_sums = own_attention(request_ids, queries, new_keys, new_values)
    picks, shares = routing(expert_ids, expert_weights)
    own, picks = lax.optimization_barrier((own, picks))

    parts = None
    for first, last in ((0, 1), (1, 4)):
        group = pieces[first:last]
        if first:
            group, parts, weight_far = lax.optimization_barrier((group, parts, weight_far))
        asked = jnp.concatenate([piece[:, TOK, : NCHIP * SLOTS] for piece in group], axis=0)
        asked = asked.reshape(-1, SLOTS, NCHIP)
        asked = lax.dynamic_index_in_dim(asked, me // NC, 2, keepdims=False)
        rows = slice(8 * first, 8 * last)
        parts = page_attention(
            chips[rows],
            page_a[rows],
            page_b[rows],
            asked.astype(jnp.int32).reshape(-1),
            page_store,
            pages_far,
            group,
            parts,
        )
    arrived = lax.all_to_all(
        parts, "req", 0, 0, tiled=True, axis_index_groups=core_groups()
    )
    attended = merge_attention(codes[0].reshape(-1), arrived, own, own_sums)
    attended_far = lax.ppermute(attended, "tp", swap)
    mixed, sent = project(
        lax.axis_index("tp")[None],
        attended,
        attended_far,
        output_weight,
        weight_far,
        residual,
        norm_gain[None, :],
        picks,
    )
    rows = lax.all_to_all(sent.reshape(NREQ, 2 * CAP, half), "req", 0, 0, tiled=True)
    result = run_expert(rows, gate_weight[0], up_weight[0], down_weight[0])
    returned = lax.all_to_all(
        result.reshape(2 * NREQ, 2 * CAP, width // 4), ("req", "tp"), 0, 0, tiled=True
    )
    return combine(mixed, shares, returned.reshape(-1, width // 4))


def solution(mesh):
    placed = (
        P("req", None),
        P("req", "tp"),
        P("req", "tp"),
        P("req", "tp"),
        P("req"),
        P("req", None, None, "tp"),
        P("req", None),
        P("req", None),
        P("req", None),
        P("req", None),
        P("tp", None),
        P(),
        P("req", None, "tp"),
        P("req", None, "tp"),
        P("req", "tp", None),
    )
    return jax.shard_map(
        shards, mesh=mesh, in_specs=placed, out_specs=P("req", "tp"), check_vma=False
    )
```

```python
import math

import jax
import jax.numpy as jnp
import numpy as np
from jax import lax
from jax.experimental import pallas as pl
from jax.experimental.pallas import tpu as pltpu
from jax.sharding import PartitionSpec as P

HD = 128
TOP = 4
HEADS = 4
PAGE = 128
TOK = 128
CAP = 12
SLOTS = 6
ROWS = SLOTS * 16
STAT = HEADS * ROWS
BLOCK = STAT + 16
MERGE_PARTS = 2
NORM_EPS = 1e-06
SCALE = 1.0 / math.sqrt(HD)
LOG2E = math.log2(math.e)
NEG = -1e30
F32 = jnp.float32
BF16 = jnp.bfloat16

NY, NZ, NX, NC = 4, 4, 2, 2
NREQ = NY * NZ * NX * NC
NCHIP = NY * NZ * NX


def req_index(y, z, x, c):
    return ((y * NZ + z) * NX + x) * NC + c


def all_coords():
    return [
        (y, z, x, c) for y in range(NY) for z in range(NZ) for x in range(NX) for c in range(NC)
    ]


def perm_x():
    return [(req_index(y, z, x, c), req_index(y, z, 1 - x, c)) for y, z, x, c in all_coords()]


def perm_core():
    return [(req_index(y, z, x, c), req_index(y, z, x, 1 - c)) for y, z, x, c in all_coords()]


def perm_ring(stage, step):
    pairs = []
    for y, z, x, c in all_coords():
        if (c + stage) % 2 == 0:
            to = req_index((y + step) % NY, z, x, c)
        else:
            to = req_index(y, (z + step) % NZ, x, c)
        pairs.append((req_index(y, z, x, c), to))
    return pairs


PIECES = tuple((step, far) for step in (0, 1, 3, 2) for far in (0, 1))


def chip_table():
    table = np.zeros((NREQ, NCHIP), np.int32)
    for y, z, x, c in all_coords():
        row = []
        for d1, dx in PIECES:
            for d0 in range(4):
                dy, dz = (d0, d1) if c == 0 else (d1, d0)
                row.append(req_index((y - dy) % NY, (z - dz) % NZ, x ^ dx, 0) // NC)
        table[req_index(y, z, x, c)] = row
    return table


def core_groups():
    return [[chip * NC + core for chip in range(NCHIP)] for core in range(NC)]


def ring_line(block):
    return [block] + [lax.ppermute(block, "req", perm_ring(0, step)) for step in (1, 2, 3)]


def ring_rest(line):
    return [lax.ppermute(line, "req", perm_ring(1, step)) for step in (1, 3, 2)]


def attend(query, key_t, value_1, shift):
    scores = jnp.dot(query, key_t, preferred_element_type=F32)
    scores = shift(scores)
    top = jnp.max(scores, axis=1, keepdims=True)
    probs = jnp.exp2((scores - top) * (SCALE * LOG2E)).astype(BF16)
    both = jnp.dot(probs, value_1, preferred_element_type=F32)
    total = both[:, HD:]
    return both[:, :HD] / total, top * SCALE + jnp.log(total)


def by_head(rows):
    head = lax.broadcasted_iota(jnp.int32, (8, 128), 0) % HEADS
    tile = jnp.where(head == 0, rows[0], rows[1])
    tile = jnp.where(head == 2, rows[2], tile)
    return jnp.where(head == 3, rows[3], tile)


def page_kernel(here, chip_of, page_a, page_b, pages_a_in, pages_b_in, *refs):
    out, blocks, pages_a, pages_b, held, notes, codes, sems, load_sems, note_sem = refs[-10:]
    count = held.shape[0]
    pieces = refs[: count // 8]
    loads = [
        pltpu.make_async_copy(source, target, load_sems.at[n])
        for n, (source, target) in enumerate(
            [(piece, blocks.at[pl.ds(8 * n, 8)]) for n, piece in enumerate(pieces)]
            + [(pages_a_in, pages_a), (pages_b_in, pages_b)]
        )
    ]
    for load in loads:
        load.start()
    row = lax.broadcasted_iota(jnp.int32, (16, 128), 0)
    offset = lax.broadcasted_iota(jnp.int32, (16, 128), 1) - row
    sub = lax.broadcasted_iota(jnp.int32, (8, 128), 0)
    ones = jnp.ones((PAGE, HD), BF16)
    for load in loads[: len(pieces)]:
        load.wait()
    width = notes.shape[1]
    for i in range(count):
        words = blocks[i, TOK : TOK + 8, :width].astype(F32).astype(jnp.int32)
        notes[i : i + 1, :] = words[:1]
    note_copy = pltpu.make_async_copy(notes, codes, note_sem)
    note_copy.start()
    for load in loads[len(pieces) :]:
        load.wait()
    note_copy.wait()
    chip = here[0]

    def copy(i):
        return pltpu.make_async_copy(held.at[i], out.at[chip_of[i]], sems.at[i])

    def step(i, carry):
        pa, pb = page_a[i], page_b[i]
        code = [codes[i, j * NCHIP + chip] for j in range(SLOTS)]
        first = [pl.multiple_of((c & 7) * 16, 16) for c in code]
        bias = jnp.concatenate(
            [
                jnp.concatenate(
                    [
                        jnp.full((16, PAGE), jnp.where((c & bit) != 0, 0.0, NEG), F32)
                        for bit in (8, 16)
                    ],
                    axis=1,
                )
                for c in code
            ],
            axis=0,
        )
        mine = [offset == jnp.where(c >= 8, (c & 7) * 16, -1024) for c in code]
        scores = []
        for head in range(HEADS):
            cols = slice(head * HD, (head + 1) * HD)
            query = jnp.concatenate(
                [blocks[i, pl.ds(first[j], 16), cols] for j in range(SLOTS)], axis=0
            )
            key = jnp.concatenate([pages_a[pa, 0, :, cols], pages_b[pb, 0, :, cols]], axis=0)
            scores.append(
                lax.dot_general(
                    query, key, (((1,), (1,)), ((), ())), preferred_element_type=F32
                )
                + bias
            )
        tops = [jnp.max(s, axis=1, keepdims=True) for s in scores]
        probs = [
            jnp.exp2((s - t) * (SCALE * LOG2E)).astype(BF16) for s, t in zip(scores, tops)
        ]
        boths = []
        for head in range(HEADS):
            cols = slice(head * HD, (head + 1) * HD)
            value_1 = jnp.concatenate(
                [
                    jnp.concatenate([pages_a[pa, 1, :, cols], ones], axis=1),
                    jnp.concatenate([pages_b[pb, 1, :, cols], ones], axis=1),
                ],
                axis=0,
            )
            boths.append(jnp.dot(probs[head], value_1, preferred_element_type=F32))
        sums = []
        for head in range(HEADS):
            total = boths[head][:, HD:]
            got = boths[head][:, :HD] / total
            held[i, head * ROWS : (head + 1) * ROWS, :] = got.astype(BF16)
            total = tops[head] * SCALE + jnp.log(total)
            here = jnp.where(mine[0], total[:16], NEG)
            for j in range(1, SLOTS):
                here = jnp.maximum(here, jnp.where(mine[j], total[16 * j : 16 * j + 16], NEG))
            sums.append(jnp.max(here, axis=0, keepdims=True))
        tile = by_head(sums)
        high = tile.astype(BF16).astype(F32)
        rest = tile - high
        middle = rest.astype(BF16).astype(F32)
        upper = jnp.where(sub < HEADS, high, middle)
        lower = jnp.where(sub < HEADS, rest - middle, 0.0)
        held[i, STAT:BLOCK, :] = jnp.concatenate([upper, lower], axis=0).astype(BF16)
        copy(i).start()
        return carry

    lax.fori_loop(0, count, step, 0, unroll=4)
    lax.fori_loop(0, count, lambda i, carry: (copy(i).wait(), carry)[1], 0)


def page_attention(here, chip_of, page_a, page_b, pages_a, pages_b, pieces, last):
    count = 8 * len(pieces)
    width = -(-NCHIP * SLOTS // 128) * 128
    before = [] if last is None else [last]
    return pl.pallas_call(
        page_kernel,
        out_shape=jax.ShapeDtypeStruct((NCHIP, BLOCK, HD), BF16),
        in_specs=[smem()] * 4 + [hbm()] * (2 + len(pieces) + len(before)),
        out_specs=hbm(),
        input_output_aliases={6 + len(pieces): 0} if before else {},
        scratch_shapes=[
            pltpu.VMEM((count, *pieces[0].shape[1:]), BF16),
            pltpu.VMEM(pages_a.shape, BF16),
            pltpu.VMEM(pages_b.shape, BF16),
            pltpu.VMEM((count, BLOCK, HD), BF16),
            pltpu.VMEM((count, width), jnp.int32),
            pltpu.SMEM((count, width), jnp.int32),
            pltpu.SemaphoreType.DMA((count,)),
            pltpu.SemaphoreType.DMA((2 + len(pieces),)),
            pltpu.SemaphoreType.DMA,
        ],
        compiler_params=pltpu.CompilerParams(vmem_limit_bytes=62 << 20),
        cost_estimate=pl.CostEstimate(
            flops=count * HEADS * 16 * ROWS * HD * HD,
            bytes_accessed=5 << 20,
            transcendentals=count * HEADS * ROWS * 2 * PAGE,
        ),
        name="page_attention",
    )(here, chip_of, page_a, page_b, pages_a, pages_b, *pieces, *before)


def smem():
    return pl.BlockSpec(memory_space=pltpu.SMEM)


def hbm():
    return pl.BlockSpec(memory_space=pltpu.HBM)


def vmem():
    return pl.BlockSpec(memory_space=pltpu.VMEM)


def own_kernel(request_col, request_row, queries, keys, values, out_hbm, total_hbm, out, total, sems):
    token = lax.broadcasted_iota(jnp.int32, (TOK, TOK), 0)
    key = lax.broadcasted_iota(jnp.int32, (TOK, TOK), 1)
    mask = (request_col[...] == request_row[...]) & (key <= token)
    ones = jnp.ones((TOK, HD), BF16)
    sums = []
    for head in range(HEADS):
        cols = slice(head * HD, (head + 1) * HD)
        got, low = attend(
            queries[:, cols],
            keys[:, cols].T,
            jnp.concatenate([values[:, cols], ones], axis=1),
            lambda s: jnp.where(mask, s, NEG),
        )
        out[head] = got
        sums.append(jnp.max(jnp.where(token == key, low, NEG), axis=0, keepdims=True))
    total[...] = by_head(sums)
    copies = [
        pltpu.make_async_copy(out, out_hbm, sems.at[0]),
        pltpu.make_async_copy(total, total_hbm, sems.at[1]),
    ]
    for copy in copies:
        copy.start()
    for copy in copies:
        copy.wait()


def own_attention(request_ids, queries, keys, values):
    return pl.pallas_call(
        own_kernel,
        out_shape=(
            jax.ShapeDtypeStruct((HEADS, TOK, HD), F32),
            jax.ShapeDtypeStruct((8, TOK), F32),
        ),
        in_specs=[vmem()] * 5,
        out_specs=(hbm(), hbm()),
        scratch_shapes=[
            pltpu.VMEM((HEADS, TOK, HD), F32),
            pltpu.VMEM((8, TOK), F32),
            pltpu.SemaphoreType.DMA((2,)),
        ],
        compiler_params=pltpu.CompilerParams(vmem_limit_bytes=62 << 20),
        cost_estimate=pl.CostEstimate(
            flops=64 << 20, bytes_accessed=1 << 20, transcendentals=HEADS * TOK * TOK
        ),
        name="own_attention",
    )(request_ids[:, None], request_ids[None, :], queries, keys, values)


def merge_kernel(
    codes, arrived_in, own_in, own_sums_in, out, acc, tiles, arrived, own, own_sums, sems
):
    part = NCHIP // MERGE_PARTS
    loads = [
        pltpu.make_async_copy(own_sums_in, own_sums, sems.at[0]),
        pltpu.make_async_copy(own_in, own, sems.at[1]),
    ] + [
        pltpu.make_async_copy(
            arrived_in.at[pl.ds(i * part, part)], arrived.at[pl.ds(i * part, part)], sems.at[2 + i]
        )
        for i in range(MERGE_PARTS)
    ]
    for load in loads:
        load.start()
    row = lax.broadcasted_iota(jnp.int32, (16, TOK), 0)
    offset = lax.broadcasted_iota(jnp.int32, (16, TOK), 1) - row

    def halves(tile):
        high = tile.astype(BF16).astype(F32)
        return high, tile - high

    def on_rows(parts, masks):
        blocks = []
        for head in range(HEADS):
            for mask in masks:
                blocks.append(
                    jnp.concatenate(
                        [
                            jnp.where(mask, jnp.broadcast_to(p[head : head + 1], (16, TOK)), 0.0)
                            for p in parts
                        ],
                        axis=1,
                    )
                )
        picked = jnp.concatenate(blocks, axis=0).astype(BF16)
        ones = jnp.ones((len(parts) * TOK, HD), BF16)
        return jnp.dot(picked, ones, preferred_element_type=F32)

    def collect(p, top):
        tile = arrived[p, STAT:BLOCK, :].astype(F32)
        tile = (tile[:8] + pltpu.roll(tile[:8], HEADS, 0)) + tile[8:]
        tiles[p] = tile
        return jnp.maximum(top, tile)

    loads[0].wait()
    top = own_sums[...]
    for i in range(MERGE_PARTS):
        loads[2 + i].wait()
        top = lax.fori_loop(i * part, (i + 1) * part, collect, top, unroll=4)
    loads[1].wait()
    whole = [offset == 16 * g for g in range(TOK // 16)]
    share = jnp.exp(own_sums[...] - top)
    acc[...] = own[...] * on_rows(halves(share), whole).reshape(HEADS, TOK, HD)

    def add(p, low):
        share = jnp.exp(tiles[p] - top).astype(BF16).astype(F32)
        code = [codes[p * SLOTS + j] for j in range(SLOTS)]
        masks = [offset == jnp.where(c >= 8, (c & 7) * 16, -1024) for c in code]
        factor = on_rows((share,), masks)
        for j in range(SLOTS):
            at = pl.ds(pl.multiple_of((code[j] & 7) * 16, 16), 16)
            for head in range(HEADS):
                start = head * ROWS + 16 * j
                part = arrived[p, start : start + 16, :].astype(F32)
                acc[head, at, :] += part * factor[start : start + 16]
        return low + share

    low = lax.fori_loop(0, NCHIP, add, share, unroll=4)
    factor = on_rows(halves(1.0 / low), whole)
    for head in range(HEADS):
        out[:, head * HD : (head + 1) * HD] = (
            acc[head] * factor[head * TOK : (head + 1) * TOK]
        ).astype(BF16)


def merge_attention(codes, arrived, own, own_sums):
    return pl.pallas_call(
        merge_kernel,
        out_shape=jax.ShapeDtypeStruct((TOK, HEADS * HD), BF16),
        in_specs=[smem()] + [hbm()] * 3,
        out_specs=vmem(),
        scratch_shapes=[
            pltpu.VMEM((HEADS, TOK, HD), F32),
            pltpu.VMEM((NCHIP, 8, TOK), F32),
            pltpu.VMEM((NCHIP, BLOCK, HD), BF16),
            pltpu.VMEM((HEADS, TOK, HD), F32),
            pltpu.VMEM((8, TOK), F32),
            pltpu.SemaphoreType.DMA((2 + MERGE_PARTS,)),
        ],
        compiler_params=pltpu.CompilerParams(vmem_limit_bytes=62 << 20),
        cost_estimate=pl.CostEstimate(
            flops=64 << 20, bytes_accessed=4 << 20, transcendentals=1 << 18
        ),
        name="merge_attention",
    )(codes, arrived, own, own_sums)


def project_kernel(
    side,
    att,
    att_far,
    weight_in,
    weight_mine,
    weight_other,
    residual_in,
    gain,
    picks_in,
    mixed,
    sent,
    both,
    kept,
    rows,
    weight,
    weight_far,
    residual,
    picks,
    load_sems,
    sems,
):
    part = weight_mine.shape[0]
    loads = [
        pltpu.make_async_copy(source, target, load_sems.at[n])
        for n, (source, target) in enumerate(
            (
                (weight_in, weight),
                (residual_in, residual),
                (weight_mine, weight_far.at[pl.ds(pl.multiple_of(side[1] * part, part), part)]),
                (weight_other, weight_far.at[pl.ds(pl.multiple_of(side[2] * part, part), part)]),
                (picks_in, picks),
            )
        )
    ]
    for load in loads:
        load.start()
    half = residual.shape[1] // 2
    steps, step = rows.shape[0], rows.shape[1]
    loads[0].wait()
    total = jnp.dot(att[...], weight[...], preferred_element_type=F32)
    loads[1].wait()
    total += residual[...].astype(F32)
    loads[2].wait()
    loads[3].wait()
    total += jnp.dot(att_far[...], weight_far[...], preferred_element_type=F32)
    kept[...] = jnp.where(side[0] == 0, total[:, :half], total[:, half:])
    keep = pltpu.make_async_copy(kept, mixed, sems.at[steps])
    keep.start()
    scale = lax.rsqrt(jnp.mean(total * total, axis=1, keepdims=True) + NORM_EPS)
    normed = (total * scale * gain[...]).astype(BF16)
    both[:TOK] = normed[:, :half]
    both[TOK:] = normed[:, half:]
    copies = []
    loads[4].wait()
    for i in range(steps):
        rows[i] = jnp.dot(
            picks[i * step : (i + 1) * step], both[...], preferred_element_type=F32
        ).astype(BF16)
        copies.append(
            pltpu.make_async_copy(rows.at[i], sent.at[pl.ds(i * step, step)], sems.at[i])
        )
        copies[-1].start()
    keep.wait()
    for copy in copies:
        copy.wait()


def project(side, att, att_far, weight, weight_mine, weight_other, residual, gain, picks, steps=4):
    width = residual.shape[1]
    step = picks.shape[0] // steps
    return pl.pallas_call(
        project_kernel,
        out_shape=(
            jax.ShapeDtypeStruct((TOK, width // 2), F32),
            jax.ShapeDtypeStruct((picks.shape[0], width // 2), BF16),
        ),
        in_specs=[smem(), vmem(), vmem(), hbm(), hbm(), hbm(), hbm(), vmem(), hbm()],
        out_specs=(hbm(), hbm()),
        scratch_shapes=[
            pltpu.VMEM((2 * TOK, width // 2), BF16),
            pltpu.VMEM((TOK, width // 2), F32),
            pltpu.VMEM((steps, step, width // 2), BF16),
            pltpu.VMEM(weight.shape, BF16),
            pltpu.VMEM((2 * weight_mine.shape[0], width), BF16),
            pltpu.VMEM(residual.shape, BF16),
            pltpu.VMEM(picks.shape, BF16),
            pltpu.SemaphoreType.DMA((5,)),
            pltpu.SemaphoreType.DMA((steps + 1,)),
        ],
        compiler_params=pltpu.CompilerParams(vmem_limit_bytes=62 << 20),
        cost_estimate=pl.CostEstimate(
            flops=4 * TOK * 512 * width + 2 * picks.shape[0] * 256 * width // 2,
            bytes_accessed=10 << 20,
            transcendentals=TOK,
        ),
        name="project_dispatch",
    )(side, att, att_far, weight, weight_mine, weight_other, residual, gain, picks)


def expert_kernel(rows, gate, up, down, out, rows_v, gate_v, up_v, down_v, out_v, sems, back):
    steps, count = rows_v.shape[0], rows_v.shape[1]
    width = gate.shape[0]
    half, quarter = width // 2, width // 4

    def fetch(i):
        return pltpu.make_async_copy(rows.at[pl.ds(i * count, count)], rows_v.at[i], sems.at[i])

    def send(i):
        return pltpu.make_async_copy(out_v.at[i], out.at[pl.ds(i * count, count)], back.at[i])

    loads = [
        pltpu.make_async_copy(src, dst, sems.at[steps + n])
        for n, (src, dst) in enumerate(((gate, gate_v), (up, up_v), (down, down_v)))
    ]
    fetch(0).start()
    for load in loads:
        load.start()
    for i in range(1, steps):
        fetch(i).start()
    low_half = lax.broadcasted_iota(jnp.int32, (count // 2, 8, half), 1) < 4
    low_quarter = lax.broadcasted_iota(jnp.int32, (count // 2, 8, quarter), 1) < 4
    def step(i, carry):
        fetch(i).wait()
        wide = rows_v[i].astype(F32)
        tail = wide[:, 16:24].reshape(count // 2, 2, 8, half)
        even, odd = tail[:, 0], tail[:, 1]
        tail_0 = jnp.where(low_half, even, pltpu.roll(odd, 4, 1))
        tail_1 = jnp.where(low_half, pltpu.roll(even, 4, 1), odd)
        left = jnp.concatenate(
            [wide[:, 0:8].reshape(count * 8, half), tail_0.reshape(count * 4, half)], axis=0
        )
        right = jnp.concatenate(
            [wide[:, 8:16].reshape(count * 8, half), tail_1.reshape(count * 4, half)], axis=0
        )
        tokens = jnp.concatenate([left.astype(BF16), right.astype(BF16)], axis=1)
        if i == 0:
            loads[0].wait()
        gate_act = jnp.dot(tokens, gate_v[...], preferred_element_type=F32)
        if i == 0:
            loads[1].wait()
        up_act = jnp.dot(tokens, up_v[...], preferred_element_type=F32)
        hidden = (gate_act / (1.0 + jnp.exp(-gate_act)) * up_act).astype(BF16)
        if i == 0:
            loads[2].wait()
        result = jnp.dot(hidden, down_v[...], preferred_element_type=F32)
        for side in range(2):
            cols = [slice((2 * side + q) * quarter, (2 * side + q + 1) * quarter) for q in range(2)]
            main = [result[: count * 8, c].reshape(count, 8, quarter) for c in cols]
            tail = [result[count * 8 :, c].reshape(count // 2, 8, quarter) for c in cols]
            even = jnp.where(low_quarter, tail[0], pltpu.roll(tail[1], 4, 1))
            odd = jnp.where(low_quarter, pltpu.roll(tail[0], 4, 1), tail[1])
            last = jnp.stack([even, odd], axis=1).reshape(count, 8, quarter)
            out_v[i, :, side] = jnp.concatenate(main + [last], axis=1).astype(BF16)
        send(i).start()
        return carry

    for i in range(steps):
        step(i, 0)
    for i in range(steps):
        send(i).wait()


def run_expert(rows, gate, up, down, steps=2):
    count = rows.shape[0] // steps
    width, hidden = gate.shape
    return pl.pallas_call(
        expert_kernel,
        out_shape=jax.ShapeDtypeStruct((rows.shape[0], 2, 2 * CAP, width // 4), BF16),
        in_specs=[hbm()] * 4,
        out_specs=hbm(),
        scratch_shapes=[
            pltpu.VMEM((steps, count, 2 * CAP, width // 2), BF16),
            pltpu.VMEM((width, hidden), BF16),
            pltpu.VMEM((width, hidden), BF16),
            pltpu.VMEM((hidden, width), BF16),
            pltpu.VMEM((steps, count, 2, 2 * CAP, width // 4), BF16),
            pltpu.SemaphoreType.DMA((steps + 3,)),
            pltpu.SemaphoreType.DMA((steps,)),
        ],
        compiler_params=pltpu.CompilerParams(vmem_limit_bytes=62 << 20),
        cost_estimate=pl.CostEstimate(
            flops=6 * rows.shape[0] * CAP * width * hidden,
            bytes_accessed=15 << 20,
            transcendentals=rows.shape[0] * CAP * hidden,
        ),
        name="expert",
    )(rows, gate, up, down)


def combine_kernel(mixed, shares, rows, out, mixed_v, shares_v, rows_v, sems):
    parts, depth, width = rows_v.shape
    loads = [
        pltpu.make_async_copy(rows.at[pl.ds(i * depth, depth)], rows_v.at[i], sems.at[i])
        for i in range(parts)
    ]
    share_load = pltpu.make_async_copy(shares, shares_v, sems.at[parts])
    mixed_load = pltpu.make_async_copy(mixed, mixed_v, sems.at[parts + 1])
    share_load.start()
    for load in loads:
        load.start()
    mixed_load.start()
    share_load.wait()
    total = jnp.zeros((shares_v.shape[0], width), F32)
    for i in range(parts):
        loads[i].wait()
        total += jnp.dot(
            shares_v[:, i * depth : (i + 1) * depth], rows_v[i], preferred_element_type=F32
        )
    mixed_load.wait()
    out[:, :width] = (mixed_v[:, :width] + total[:TOK]).astype(BF16)
    out[:, width:] = (mixed_v[:, width:] + total[TOK:]).astype(BF16)


def combine(mixed, shares, rows, parts=4):
    return pl.pallas_call(
        combine_kernel,
        out_shape=jax.ShapeDtypeStruct(mixed.shape, BF16),
        in_specs=[hbm()] * 3,
        out_specs=vmem(),
        scratch_shapes=[
            pltpu.VMEM(mixed.shape, F32),
            pltpu.VMEM(shares.shape, BF16),
            pltpu.VMEM((parts, rows.shape[0] // parts, rows.shape[1]), BF16),
            pltpu.SemaphoreType.DMA((parts + 2,)),
        ],
        compiler_params=pltpu.CompilerParams(vmem_limit_bytes=62 << 20),
        cost_estimate=pl.CostEstimate(
            flops=2 * shares.shape[0] * rows.shape[0] * rows.shape[1],
            bytes_accessed=6 << 20,
            transcendentals=0,
        ),
        name="combine",
    )(mixed, shares, rows)


def slot_rows():
    slot = np.array(list(range(8)) * 2 + list(range(8, 12)) * 2, np.int32)
    part = np.array([0] * 8 + [1] * 8 + [0] * 4 + [1] * 4, np.int32)
    return slot, part


def routing(expert_ids, expert_weights):
    flat = expert_ids.reshape(-1)
    count = flat.shape[0]
    onehot = (flat[:, None] == jnp.arange(NREQ, dtype=jnp.int32)[None, :]).astype(BF16)
    earlier = (
        jnp.arange(count, dtype=jnp.int32)[None, :] < jnp.arange(count, dtype=jnp.int32)[:, None]
    ).astype(BF16)
    before = jnp.dot(earlier, onehot, preferred_element_type=F32)
    slot = jnp.sum(before * onehot.astype(F32), axis=1).astype(jnp.int32)
    place = (flat * CAP + slot).reshape(TOK, TOP)

    slot_at, part_at = slot_rows()
    row_place = (np.arange(NREQ, dtype=np.int32)[:, None] * CAP + slot_at[None, :]).reshape(-1)
    row_part = np.tile(part_at, NREQ)
    col_place = jnp.concatenate([place, place], axis=0)
    col_part = np.repeat(np.arange(2, dtype=np.int32), TOK)
    hit = jnp.zeros((row_place.shape[0], 2 * TOK), jnp.bool_)
    for k in range(TOP):
        hit = hit | (col_place[None, :, k] == row_place[:, None])
    picks = (hit & (row_part[:, None] == col_part[None, :])).astype(BF16)

    back_place = np.repeat(row_place.reshape(NREQ, 1, -1), 2, axis=1).reshape(-1)
    back_part = np.tile(part_at, 2 * NREQ)
    col_weight = jnp.concatenate([expert_weights, expert_weights], axis=0)
    shares = jnp.zeros((2 * TOK, back_place.shape[0]), F32)
    for k in range(TOP):
        shares = shares + jnp.where(
            col_place[:, k, None] == back_place[None, :], col_weight[:, k, None], 0.0
        )
    shares = jnp.where(back_part[None, :] == col_part[:, None], shares, 0.0)
    return picks, shares.astype(BF16)


def group_codes(users, ids, core):
    users = users.reshape(NCHIP, NC)
    user_a = jnp.where(core == 0, users[:, 0], users[:, 1])[:, None]
    user_b = jnp.where(core == 0, users[:, 1], users[:, 0])[:, None]
    group = jnp.arange(TOK // 16, dtype=jnp.int32)
    group_user = ids.reshape(1, TOK // 16, 16)[..., 0]
    hit_a, hit_b = group_user == user_a, group_user == user_b
    needed = (hit_a | hit_b).astype(jnp.int32)
    rank = jnp.sum(needed[:, None, :] * (group[None, :] < group[:, None]), axis=2)
    value = needed * (group + 8 * hit_a + 16 * hit_b)
    slot = jnp.arange(SLOTS, dtype=jnp.int32)
    return jnp.sum(jnp.where(rank[:, None, :] == slot[:, None], value[:, None, :], 0), axis=2)


def shards(
    residual,
    queries,
    new_keys,
    new_values,
    request_ids,
    page_store,
    page_sends,
    page_users,
    expert_ids,
    expert_weights,
    output_weight,
    norm_gain,
    gate_weight,
    up_weight,
    down_weight,
):
    me = lax.axis_index("req")
    width = residual.shape[1]
    half = width // 2
    swap = [(0, 1), (1, 0)]

    core = me % NC
    pages_far = lax.ppermute(page_store, "req", perm_core())
    sends_far = lax.ppermute(page_sends, "req", perm_core())
    codes = group_codes(page_users[0], request_ids, core)
    note = jnp.zeros((8, queries.shape[1]), BF16)
    note = note.at[0, : NCHIP * SLOTS].set(codes.T.reshape(-1).astype(BF16))
    block = jnp.concatenate([queries, note], axis=0)
    far_rows = output_weight.shape[0] // NC
    far_part = lax.dynamic_slice_in_dim(output_weight, core * far_rows, far_rows, 0)
    near = lax.ppermute(block, "req", perm_x())
    line_a = ring_line(block)
    near, line_a, pages_far, sends_far, far_part = lax.optimization_barrier(
        (near, line_a, pages_far, sends_far, far_part)
    )
    weight_mine = lax.ppermute(far_part, "tp", swap)
    line = jnp.stack(line_a + ring_line(near))

    chips = lax.dynamic_index_in_dim(jnp.asarray(chip_table()), me, 0, keepdims=False)
    page_a = page_sends[0][chips * NC + core]
    page_b = sends_far[0][chips * NC + core]
    line, chips, page_a, page_b = lax.optimization_barrier((line, chips, page_a, page_b))
    pieces = [line] + ring_rest(line)
    here = me // NC
    own, own_sums = own_attention(request_ids, queries, new_keys, new_values)
    picks, shares = routing(expert_ids, expert_weights)
    own, picks = lax.optimization_barrier((own, picks))

    parts = None
    for first, last in ((0, 1), (1, 4)):
        group = pieces[first:last]
        if first:
            weight_other = lax.ppermute(weight_mine, "req", perm_core())
            group, parts, weight_mine, weight_other = lax.optimization_barrier(
                (group, parts, weight_mine, weight_other)
            )
        rows = slice(8 * first, 8 * last)
        parts = page_attention(
            here[None], chips[rows], page_a[rows], page_b[rows], page_store, pages_far, group, parts
        )
    arrived = lax.all_to_all(
        parts, "req", 0, 0, tiled=True, axis_index_groups=core_groups()
    )
    attended = merge_attention(codes.reshape(-1), arrived, own, own_sums)
    attended_far = lax.ppermute(attended, "tp", swap)
    mixed, sent = project(
        jnp.stack([lax.axis_index("tp"), core, 1 - core]),
        attended,
        attended_far,
        output_weight,
        weight_mine,
        weight_other,
        residual,
        norm_gain[None, :],
        picks,
    )
    rows = lax.all_to_all(sent.reshape(NREQ, 2 * CAP, half), "req", 0, 0, tiled=True)
    result = run_expert(rows, gate_weight[0], up_weight[0], down_weight[0])
    returned = lax.all_to_all(
        result.reshape(2 * NREQ, 2 * CAP, width // 4), ("req", "tp"), 0, 0, tiled=True
    )
    return combine(mixed, shares, returned.reshape(-1, width // 4))


def solution(mesh):
    placed = (
        P("req", None),
        P("req", "tp"),
        P("req", "tp"),
        P("req", "tp"),
        P("req"),
        P("req", None, None, "tp"),
        P("req", None),
        P("req", None),
        P("req", None),
        P("req", None),
        P("tp", None),
        P(),
        P("req", None, "tp"),
        P("req", None, "tp"),
        P("req", "tp", None),
    )
    return jax.shard_map(
        shards, mesh=mesh, in_specs=placed, out_specs=P("req", "tp"), check_vma=False
    )
```

```python
import math

import jax
import jax.numpy as jnp
import numpy as np
from jax import lax
from jax.experimental import pallas as pl
from jax.experimental.pallas import tpu as pltpu
from jax.sharding import PartitionSpec as P

HD = 128
TOP = 4
HEADS = 4
PAGE = 128
TOK = 128
CAP = 12
SLOTS = 6
ROWS = SLOTS * 16
STAT = HEADS * ROWS
BLOCK = STAT + 16
MERGE_PARTS = 2
NORM_EPS = 1e-06
SCALE = 1.0 / math.sqrt(HD)
LOG2E = math.log2(math.e)
NEG = -1e30
F32 = jnp.float32
BF16 = jnp.bfloat16

NY, NZ, NX, NC = 4, 4, 2, 2
NREQ = NY * NZ * NX * NC
NCHIP = NY * NZ * NX


def req_index(y, z, x, c):
    return ((y * NZ + z) * NX + x) * NC + c


def all_coords():
    return [
        (y, z, x, c) for y in range(NY) for z in range(NZ) for x in range(NX) for c in range(NC)
    ]


def perm_x():
    return [(req_index(y, z, x, c), req_index(y, z, 1 - x, c)) for y, z, x, c in all_coords()]


def perm_core():
    return [(req_index(y, z, x, c), req_index(y, z, x, 1 - c)) for y, z, x, c in all_coords()]


def perm_ring(stage, step):
    pairs = []
    for y, z, x, c in all_coords():
        if (c + stage) % 2 == 0:
            to = req_index((y + step) % NY, z, x, c)
        else:
            to = req_index(y, (z + step) % NZ, x, c)
        pairs.append((req_index(y, z, x, c), to))
    return pairs


PIECES = tuple((step, far) for step in (0, 1, 3, 2) for far in (0, 1))


def chip_table():
    table = np.zeros((NREQ, NCHIP), np.int32)
    for y, z, x, c in all_coords():
        row = []
        for d1, dx in PIECES:
            for d0 in range(4):
                dy, dz = (d0, d1) if c == 0 else (d1, d0)
                row.append(req_index((y - dy) % NY, (z - dz) % NZ, x ^ dx, 0) // NC)
        table[req_index(y, z, x, c)] = row
    return table


def core_groups():
    return [[chip * NC + core for chip in range(NCHIP)] for core in range(NC)]


def ring_line(block):
    return [block] + [lax.ppermute(block, "req", perm_ring(0, step)) for step in (1, 2, 3)]


def stack_kernel(*refs):
    out, sems = refs[-2:]
    copies = [
        pltpu.make_async_copy(block, out.at[i], sems.at[i]) for i, block in enumerate(refs[:-2])
    ]
    for copy in copies:
        copy.start()
    for copy in copies:
        copy.wait()


def stack_blocks(blocks):
    count = len(blocks)
    size = math.prod(blocks[0].shape) * 2
    return pl.pallas_call(
        stack_kernel,
        out_shape=jax.ShapeDtypeStruct((count, *blocks[0].shape), BF16),
        in_specs=[pl.BlockSpec(memory_space=pl.ANY)] * count,
        out_specs=pl.BlockSpec(memory_space=pl.ANY),
        scratch_shapes=[pltpu.SemaphoreType.DMA((count,))],
        compiler_params=pltpu.CompilerParams(vmem_limit_bytes=8 << 20),
        cost_estimate=pl.CostEstimate(
            flops=0, bytes_accessed=2 * count * size, transcendentals=0
        ),
        name="stack_blocks",
    )(*blocks)


def ring_rest(line):
    return [lax.ppermute(line, "req", perm_ring(1, step)) for step in (1, 3, 2)]


def attend(query, key_t, value_1, shift):
    scores = jnp.dot(query, key_t, preferred_element_type=F32)
    scores = shift(scores)
    top = jnp.max(scores, axis=1, keepdims=True)
    probs = jnp.exp2((scores - top) * (SCALE * LOG2E)).astype(BF16)
    both = jnp.dot(probs, value_1, preferred_element_type=F32)
    total = both[:, HD:]
    return both[:, :HD] / total, top * SCALE + jnp.log(total)


def by_head(rows):
    head = lax.broadcasted_iota(jnp.int32, (8, 128), 0) % HEADS
    tile = jnp.where(head == 0, rows[0], rows[1])
    tile = jnp.where(head == 2, rows[2], tile)
    return jnp.where(head == 3, rows[3], tile)


def page_kernel(here, chip_of, page_a, page_b, pages_a_in, pages_b_in, *refs):
    out, blocks, pages_a, pages_b, held, notes, codes, sems, load_sems, note_sem = refs[-10:]
    count = held.shape[0]
    pieces = refs[: count // 8]
    loads = [
        pltpu.make_async_copy(source, target, load_sems.at[n])
        for n, (source, target) in enumerate(
            [(piece, blocks.at[pl.ds(8 * n, 8)]) for n, piece in enumerate(pieces)]
            + [(pages_a_in, pages_a), (pages_b_in, pages_b)]
        )
    ]
    for load in loads:
        load.start()
    row = lax.broadcasted_iota(jnp.int32, (16, 128), 0)
    offset = lax.broadcasted_iota(jnp.int32, (16, 128), 1) - row
    sub = lax.broadcasted_iota(jnp.int32, (8, 128), 0)
    ones = jnp.ones((PAGE, HD), BF16)
    for load in loads[: len(pieces)]:
        load.wait()
    width = notes.shape[1]
    for i in range(count):
        words = blocks[i, TOK : TOK + 8, :width].astype(F32).astype(jnp.int32)
        notes[i : i + 1, :] = words[:1]
    note_copy = pltpu.make_async_copy(notes, codes, note_sem)
    note_copy.start()
    for load in loads[len(pieces) :]:
        load.wait()
    note_copy.wait()
    chip = here[0]

    def copy(i):
        return pltpu.make_async_copy(held.at[i], out.at[chip_of[i]], sems.at[i])

    def step(i, carry):
        pa, pb = page_a[i], page_b[i]
        code = [codes[i, j * NCHIP + chip] for j in range(SLOTS)]
        first = [pl.multiple_of((c & 7) * 16, 16) for c in code]
        bias = jnp.concatenate(
            [
                jnp.concatenate(
                    [
                        jnp.full((16, PAGE), jnp.where((c & bit) != 0, 0.0, NEG), F32)
                        for bit in (8, 16)
                    ],
                    axis=1,
                )
                for c in code
            ],
            axis=0,
        )
        mine = [offset == jnp.where(c >= 8, (c & 7) * 16, -1024) for c in code]
        scores = []
        for head in range(HEADS):
            cols = slice(head * HD, (head + 1) * HD)
            query = jnp.concatenate(
                [blocks[i, pl.ds(first[j], 16), cols] for j in range(SLOTS)], axis=0
            )
            key = jnp.concatenate([pages_a[pa, 0, :, cols], pages_b[pb, 0, :, cols]], axis=0)
            scores.append(
                lax.dot_general(
                    query, key, (((1,), (1,)), ((), ())), preferred_element_type=F32
                )
                + bias
            )
        tops = [jnp.max(s, axis=1, keepdims=True) for s in scores]
        probs = [
            jnp.exp2((s - t) * (SCALE * LOG2E)).astype(BF16) for s, t in zip(scores, tops)
        ]
        boths = []
        for head in range(HEADS):
            cols = slice(head * HD, (head + 1) * HD)
            value_1 = jnp.concatenate(
                [
                    jnp.concatenate([pages_a[pa, 1, :, cols], ones], axis=1),
                    jnp.concatenate([pages_b[pb, 1, :, cols], ones], axis=1),
                ],
                axis=0,
            )
            boths.append(jnp.dot(probs[head], value_1, preferred_element_type=F32))
        sums = []
        for head in range(HEADS):
            total = boths[head][:, HD:]
            got = boths[head][:, :HD] / total
            held[i, head * ROWS : (head + 1) * ROWS, :] = got.astype(BF16)
            total = tops[head] * SCALE + jnp.log(total)
            here = jnp.where(mine[0], total[:16], NEG)
            for j in range(1, SLOTS):
                here = jnp.maximum(here, jnp.where(mine[j], total[16 * j : 16 * j + 16], NEG))
            sums.append(jnp.max(here, axis=0, keepdims=True))
        tile = by_head(sums)
        high = tile.astype(BF16).astype(F32)
        rest = tile - high
        middle = rest.astype(BF16).astype(F32)
        upper = jnp.where(sub < HEADS, high, middle)
        lower = jnp.where(sub < HEADS, rest - middle, 0.0)
        held[i, STAT:BLOCK, :] = jnp.concatenate([upper, lower], axis=0).astype(BF16)
        copy(i).start()
        return carry

    lax.fori_loop(0, count, step, 0, unroll=4)
    lax.fori_loop(0, count, lambda i, carry: (copy(i).wait(), carry)[1], 0)


def page_attention(here, chip_of, page_a, page_b, pages_a, pages_b, pieces, last):
    count = 8 * len(pieces)
    width = -(-NCHIP * SLOTS // 128) * 128
    before = [] if last is None else [last]
    return pl.pallas_call(
        page_kernel,
        out_shape=jax.ShapeDtypeStruct((NCHIP, BLOCK, HD), BF16),
        in_specs=[smem()] * 4 + [hbm()] * (2 + len(pieces) + len(before)),
        out_specs=hbm(),
        input_output_aliases={6 + len(pieces): 0} if before else {},
        scratch_shapes=[
            pltpu.VMEM((count, *pieces[0].shape[1:]), BF16),
            pltpu.VMEM(pages_a.shape, BF16),
            pltpu.VMEM(pages_b.shape, BF16),
            pltpu.VMEM((count, BLOCK, HD), BF16),
            pltpu.VMEM((count, width), jnp.int32),
            pltpu.SMEM((count, width), jnp.int32),
            pltpu.SemaphoreType.DMA((count,)),
            pltpu.SemaphoreType.DMA((2 + len(pieces),)),
            pltpu.SemaphoreType.DMA,
        ],
        compiler_params=pltpu.CompilerParams(vmem_limit_bytes=62 << 20),
        cost_estimate=pl.CostEstimate(
            flops=count * HEADS * 16 * ROWS * HD * HD,
            bytes_accessed=5 << 20,
            transcendentals=count * HEADS * ROWS * 2 * PAGE,
        ),
        name="page_attention",
    )(here, chip_of, page_a, page_b, pages_a, pages_b, *pieces, *before)


def smem():
    return pl.BlockSpec(memory_space=pltpu.SMEM)


def hbm():
    return pl.BlockSpec(memory_space=pltpu.HBM)


def vmem():
    return pl.BlockSpec(memory_space=pltpu.VMEM)


def own_kernel(request_col, request_row, queries, keys, values, out_hbm, total_hbm, out, total, sems):
    token = lax.broadcasted_iota(jnp.int32, (TOK, TOK), 0)
    key = lax.broadcasted_iota(jnp.int32, (TOK, TOK), 1)
    mask = (request_col[...] == request_row[...]) & (key <= token)
    ones = jnp.ones((TOK, HD), BF16)
    sums = []
    for head in range(HEADS):
        cols = slice(head * HD, (head + 1) * HD)
        got, low = attend(
            queries[:, cols],
            keys[:, cols].T,
            jnp.concatenate([values[:, cols], ones], axis=1),
            lambda s: jnp.where(mask, s, NEG),
        )
        out[head] = got
        sums.append(jnp.max(jnp.where(token == key, low, NEG), axis=0, keepdims=True))
    total[...] = by_head(sums)
    copies = [
        pltpu.make_async_copy(out, out_hbm, sems.at[0]),
        pltpu.make_async_copy(total, total_hbm, sems.at[1]),
    ]
    for copy in copies:
        copy.start()
    for copy in copies:
        copy.wait()


def own_attention(request_ids, queries, keys, values):
    return pl.pallas_call(
        own_kernel,
        out_shape=(
            jax.ShapeDtypeStruct((HEADS, TOK, HD), F32),
            jax.ShapeDtypeStruct((8, TOK), F32),
        ),
        in_specs=[vmem()] * 5,
        out_specs=(hbm(), hbm()),
        scratch_shapes=[
            pltpu.VMEM((HEADS, TOK, HD), F32),
            pltpu.VMEM((8, TOK), F32),
            pltpu.SemaphoreType.DMA((2,)),
        ],
        compiler_params=pltpu.CompilerParams(vmem_limit_bytes=62 << 20),
        cost_estimate=pl.CostEstimate(
            flops=64 << 20, bytes_accessed=1 << 20, transcendentals=HEADS * TOK * TOK
        ),
        name="own_attention",
    )(request_ids[:, None], request_ids[None, :], queries, keys, values)


def merge_kernel(
    codes, arrived_in, own_in, own_sums_in, out, acc, tiles, arrived, own, own_sums, sems
):
    part = NCHIP // MERGE_PARTS
    loads = [
        pltpu.make_async_copy(own_sums_in, own_sums, sems.at[0]),
        pltpu.make_async_copy(own_in, own, sems.at[1]),
    ] + [
        pltpu.make_async_copy(
            arrived_in.at[pl.ds(i * part, part)], arrived.at[pl.ds(i * part, part)], sems.at[2 + i]
        )
        for i in range(MERGE_PARTS)
    ]
    for load in loads:
        load.start()
    row = lax.broadcasted_iota(jnp.int32, (16, TOK), 0)
    offset = lax.broadcasted_iota(jnp.int32, (16, TOK), 1) - row

    def halves(tile):
        high = tile.astype(BF16).astype(F32)
        return high, tile - high

    def on_rows(parts, masks):
        blocks = []
        for head in range(HEADS):
            for mask in masks:
                blocks.append(
                    jnp.concatenate(
                        [
                            jnp.where(mask, jnp.broadcast_to(p[head : head + 1], (16, TOK)), 0.0)
                            for p in parts
                        ],
                        axis=1,
                    )
                )
        picked = jnp.concatenate(blocks, axis=0).astype(BF16)
        ones = jnp.ones((len(parts) * TOK, HD), BF16)
        return jnp.dot(picked, ones, preferred_element_type=F32)

    def collect(p, top):
        tile = arrived[p, STAT:BLOCK, :].astype(F32)
        tile = (tile[:8] + pltpu.roll(tile[:8], HEADS, 0)) + tile[8:]
        tiles[p] = tile
        return jnp.maximum(top, tile)

    loads[0].wait()
    top = own_sums[...]
    for i in range(MERGE_PARTS):
        loads[2 + i].wait()
        top = lax.fori_loop(i * part, (i + 1) * part, collect, top, unroll=4)
    loads[1].wait()
    whole = [offset == 16 * g for g in range(TOK // 16)]
    share = jnp.exp(own_sums[...] - top)
    acc[...] = own[...] * on_rows(halves(share), whole).reshape(HEADS, TOK, HD)

    def add(p, low):
        share = jnp.exp(tiles[p] - top).astype(BF16).astype(F32)
        code = [codes[p * SLOTS + j] for j in range(SLOTS)]
        masks = [offset == jnp.where(c >= 8, (c & 7) * 16, -1024) for c in code]
        factor = on_rows((share,), masks)
        for j in range(SLOTS):
            at = pl.ds(pl.multiple_of((code[j] & 7) * 16, 16), 16)
            for head in range(HEADS):
                start = head * ROWS + 16 * j
                part = arrived[p, start : start + 16, :].astype(F32)
                acc[head, at, :] += part * factor[start : start + 16]
        return low + share

    low = lax.fori_loop(0, NCHIP, add, share, unroll=4)
    factor = on_rows(halves(1.0 / low), whole)
    for head in range(HEADS):
        out[:, head * HD : (head + 1) * HD] = (
            acc[head] * factor[head * TOK : (head + 1) * TOK]
        ).astype(BF16)


def merge_attention(codes, arrived, own, own_sums):
    return pl.pallas_call(
        merge_kernel,
        out_shape=jax.ShapeDtypeStruct((TOK, HEADS * HD), BF16),
        in_specs=[smem()] + [hbm()] * 3,
        out_specs=vmem(),
        scratch_shapes=[
            pltpu.VMEM((HEADS, TOK, HD), F32),
            pltpu.VMEM((NCHIP, 8, TOK), F32),
            pltpu.VMEM((NCHIP, BLOCK, HD), BF16),
            pltpu.VMEM((HEADS, TOK, HD), F32),
            pltpu.VMEM((8, TOK), F32),
            pltpu.SemaphoreType.DMA((2 + MERGE_PARTS,)),
        ],
        compiler_params=pltpu.CompilerParams(vmem_limit_bytes=62 << 20),
        cost_estimate=pl.CostEstimate(
            flops=64 << 20, bytes_accessed=4 << 20, transcendentals=1 << 18
        ),
        name="merge_attention",
    )(codes, arrived, own, own_sums)


def project_kernel(
    side,
    att,
    att_far,
    weight_in,
    weight_mine,
    weight_other,
    residual_in,
    gain,
    picks_in,
    mixed,
    sent,
    both,
    kept,
    rows,
    weight,
    weight_far,
    residual,
    picks,
    load_sems,
    sems,
):
    part = weight_mine.shape[0]
    loads = [
        pltpu.make_async_copy(source, target, load_sems.at[n])
        for n, (source, target) in enumerate(
            (
                (weight_in, weight),
                (residual_in, residual),
                (weight_mine, weight_far.at[pl.ds(pl.multiple_of(side[1] * part, part), part)]),
                (weight_other, weight_far.at[pl.ds(pl.multiple_of(side[2] * part, part), part)]),
                (picks_in, picks),
            )
        )
    ]
    for load in loads:
        load.start()
    half = residual.shape[1] // 2
    steps, step = rows.shape[0], rows.shape[1]
    loads[0].wait()
    total = jnp.dot(att[...], weight[...], preferred_element_type=F32)
    loads[1].wait()
    total += residual[...].astype(F32)
    loads[2].wait()
    loads[3].wait()
    total += jnp.dot(att_far[...], weight_far[...], preferred_element_type=F32)
    kept[...] = jnp.where(side[0] == 0, total[:, :half], total[:, half:])
    keep = pltpu.make_async_copy(kept, mixed, sems.at[steps])
    keep.start()
    scale = lax.rsqrt(jnp.mean(total * total, axis=1, keepdims=True) + NORM_EPS)
    normed = (total * scale * gain[...]).astype(BF16)
    both[:TOK] = normed[:, :half]
    both[TOK:] = normed[:, half:]
    copies = []
    loads[4].wait()
    for i in range(steps):
        rows[i] = jnp.dot(
            picks[i * step : (i + 1) * step], both[...], preferred_element_type=F32
        ).astype(BF16)
        copies.append(
            pltpu.make_async_copy(rows.at[i], sent.at[pl.ds(i * step, step)], sems.at[i])
        )
        copies[-1].start()
    keep.wait()
    for copy in copies:
        copy.wait()


def project(side, att, att_far, weight, weight_mine, weight_other, residual, gain, picks, steps=4):
    width = residual.shape[1]
    step = picks.shape[0] // steps
    return pl.pallas_call(
        project_kernel,
        out_shape=(
            jax.ShapeDtypeStruct((TOK, width // 2), F32),
            jax.ShapeDtypeStruct((picks.shape[0], width // 2), BF16),
        ),
        in_specs=[smem(), vmem(), vmem(), hbm(), hbm(), hbm(), hbm(), vmem(), hbm()],
        out_specs=(hbm(), hbm()),
        scratch_shapes=[
            pltpu.VMEM((2 * TOK, width // 2), BF16),
            pltpu.VMEM((TOK, width // 2), F32),
            pltpu.VMEM((steps, step, width // 2), BF16),
            pltpu.VMEM(weight.shape, BF16),
            pltpu.VMEM((2 * weight_mine.shape[0], width), BF16),
            pltpu.VMEM(residual.shape, BF16),
            pltpu.VMEM(picks.shape, BF16),
            pltpu.SemaphoreType.DMA((5,)),
            pltpu.SemaphoreType.DMA((steps + 1,)),
        ],
        compiler_params=pltpu.CompilerParams(vmem_limit_bytes=62 << 20),
        cost_estimate=pl.CostEstimate(
            flops=4 * TOK * 512 * width + 2 * picks.shape[0] * 256 * width // 2,
            bytes_accessed=10 << 20,
            transcendentals=TOK,
        ),
        name="project_dispatch",
    )(side, att, att_far, weight, weight_mine, weight_other, residual, gain, picks)


def expert_kernel(rows, gate, up, down, out, rows_v, gate_v, up_v, down_v, out_v, sems, back):
    steps, count = rows_v.shape[0], rows_v.shape[1]
    width = gate.shape[0]
    half, quarter = width // 2, width // 4

    def fetch(i):
        return pltpu.make_async_copy(rows.at[pl.ds(i * count, count)], rows_v.at[i], sems.at[i])

    def send(i):
        return pltpu.make_async_copy(out_v.at[i], out.at[pl.ds(i * count, count)], back.at[i])

    loads = [
        pltpu.make_async_copy(src, dst, sems.at[steps + n])
        for n, (src, dst) in enumerate(((gate, gate_v), (up, up_v), (down, down_v)))
    ]
    fetch(0).start()
    for load in loads:
        load.start()
    for i in range(1, steps):
        fetch(i).start()
    low_half = lax.broadcasted_iota(jnp.int32, (count // 2, 8, half), 1) < 4
    low_quarter = lax.broadcasted_iota(jnp.int32, (count // 2, 8, quarter), 1) < 4
    def step(i, carry):
        fetch(i).wait()
        wide = rows_v[i].astype(F32)
        tail = wide[:, 16:24].reshape(count // 2, 2, 8, half)
        even, odd = tail[:, 0], tail[:, 1]
        tail_0 = jnp.where(low_half, even, pltpu.roll(odd, 4, 1))
        tail_1 = jnp.where(low_half, pltpu.roll(even, 4, 1), odd)
        left = jnp.concatenate(
            [wide[:, 0:8].reshape(count * 8, half), tail_0.reshape(count * 4, half)], axis=0
        )
        right = jnp.concatenate(
            [wide[:, 8:16].reshape(count * 8, half), tail_1.reshape(count * 4, half)], axis=0
        )
        tokens = jnp.concatenate([left.astype(BF16), right.astype(BF16)], axis=1)
        if i == 0:
            loads[0].wait()
        gate_act = jnp.dot(tokens, gate_v[...], preferred_element_type=F32)
        if i == 0:
            loads[1].wait()
        up_act = jnp.dot(tokens, up_v[...], preferred_element_type=F32)
        hidden = (gate_act / (1.0 + jnp.exp(-gate_act)) * up_act).astype(BF16)
        if i == 0:
            loads[2].wait()
        result = jnp.dot(hidden, down_v[...], preferred_element_type=F32)
        for side in range(2):
            cols = [slice((2 * side + q) * quarter, (2 * side + q + 1) * quarter) for q in range(2)]
            main = [result[: count * 8, c].reshape(count, 8, quarter) for c in cols]
            tail = [result[count * 8 :, c].reshape(count // 2, 8, quarter) for c in cols]
            even = jnp.where(low_quarter, tail[0], pltpu.roll(tail[1], 4, 1))
            odd = jnp.where(low_quarter, pltpu.roll(tail[0], 4, 1), tail[1])
            last = jnp.stack([even, odd], axis=1).reshape(count, 8, quarter)
            out_v[i, :, side] = jnp.concatenate(main + [last], axis=1).astype(BF16)
        send(i).start()
        return carry

    for i in range(steps):
        step(i, 0)
    for i in range(steps):
        send(i).wait()


def run_expert(rows, gate, up, down, steps=2):
    count = rows.shape[0] // steps
    width, hidden = gate.shape
    return pl.pallas_call(
        expert_kernel,
        out_shape=jax.ShapeDtypeStruct((rows.shape[0], 2, 2 * CAP, width // 4), BF16),
        in_specs=[hbm()] * 4,
        out_specs=hbm(),
        scratch_shapes=[
            pltpu.VMEM((steps, count, 2 * CAP, width // 2), BF16),
            pltpu.VMEM((width, hidden), BF16),
            pltpu.VMEM((width, hidden), BF16),
            pltpu.VMEM((hidden, width), BF16),
            pltpu.VMEM((steps, count, 2, 2 * CAP, width // 4), BF16),
            pltpu.SemaphoreType.DMA((steps + 3,)),
            pltpu.SemaphoreType.DMA((steps,)),
        ],
        compiler_params=pltpu.CompilerParams(vmem_limit_bytes=62 << 20),
        cost_estimate=pl.CostEstimate(
            flops=6 * rows.shape[0] * CAP * width * hidden,
            bytes_accessed=15 << 20,
            transcendentals=rows.shape[0] * CAP * hidden,
        ),
        name="expert",
    )(rows, gate, up, down)


def combine_kernel(mixed, shares, rows, out, mixed_v, shares_v, rows_v, sems):
    parts, depth, width = rows_v.shape
    loads = [
        pltpu.make_async_copy(rows.at[pl.ds(i * depth, depth)], rows_v.at[i], sems.at[i])
        for i in range(parts)
    ]
    share_load = pltpu.make_async_copy(shares, shares_v, sems.at[parts])
    mixed_load = pltpu.make_async_copy(mixed, mixed_v, sems.at[parts + 1])
    share_load.start()
    for load in loads:
        load.start()
    mixed_load.start()
    share_load.wait()
    total = jnp.zeros((shares_v.shape[0], width), F32)
    for i in range(parts):
        loads[i].wait()
        total += jnp.dot(
            shares_v[:, i * depth : (i + 1) * depth], rows_v[i], preferred_element_type=F32
        )
    mixed_load.wait()
    out[:, :width] = (mixed_v[:, :width] + total[:TOK]).astype(BF16)
    out[:, width:] = (mixed_v[:, width:] + total[TOK:]).astype(BF16)


def combine(mixed, shares, rows, parts=4):
    return pl.pallas_call(
        combine_kernel,
        out_shape=jax.ShapeDtypeStruct(mixed.shape, BF16),
        in_specs=[hbm()] * 3,
        out_specs=vmem(),
        scratch_shapes=[
            pltpu.VMEM(mixed.shape, F32),
            pltpu.VMEM(shares.shape, BF16),
            pltpu.VMEM((parts, rows.shape[0] // parts, rows.shape[1]), BF16),
            pltpu.SemaphoreType.DMA((parts + 2,)),
        ],
        compiler_params=pltpu.CompilerParams(vmem_limit_bytes=62 << 20),
        cost_estimate=pl.CostEstimate(
            flops=2 * shares.shape[0] * rows.shape[0] * rows.shape[1],
            bytes_accessed=6 << 20,
            transcendentals=0,
        ),
        name="combine",
    )(mixed, shares, rows)


def slot_rows():
    slot = np.array(list(range(8)) * 2 + list(range(8, 12)) * 2, np.int32)
    part = np.array([0] * 8 + [1] * 8 + [0] * 4 + [1] * 4, np.int32)
    return slot, part


def routing(expert_ids, expert_weights):
    flat = expert_ids.reshape(-1)
    count = flat.shape[0]
    onehot = (flat[:, None] == jnp.arange(NREQ, dtype=jnp.int32)[None, :]).astype(BF16)
    earlier = (
        jnp.arange(count, dtype=jnp.int32)[None, :] < jnp.arange(count, dtype=jnp.int32)[:, None]
    ).astype(BF16)
    before = jnp.dot(earlier, onehot, preferred_element_type=F32)
    slot = jnp.sum(before * onehot.astype(F32), axis=1).astype(jnp.int32)
    place = (flat * CAP + slot).reshape(TOK, TOP)

    slot_at, part_at = slot_rows()
    row_place = (np.arange(NREQ, dtype=np.int32)[:, None] * CAP + slot_at[None, :]).reshape(-1)
    row_part = np.tile(part_at, NREQ)
    col_place = jnp.concatenate([place, place], axis=0)
    col_part = np.repeat(np.arange(2, dtype=np.int32), TOK)
    hit = jnp.zeros((row_place.shape[0], 2 * TOK), jnp.bool_)
    for k in range(TOP):
        hit = hit | (col_place[None, :, k] == row_place[:, None])
    picks = (hit & (row_part[:, None] == col_part[None, :])).astype(BF16)

    back_place = np.repeat(row_place.reshape(NREQ, 1, -1), 2, axis=1).reshape(-1)
    back_part = np.tile(part_at, 2 * NREQ)
    col_weight = jnp.concatenate([expert_weights, expert_weights], axis=0)
    shares = jnp.zeros((2 * TOK, back_place.shape[0]), F32)
    for k in range(TOP):
        shares = shares + jnp.where(
            col_place[:, k, None] == back_place[None, :], col_weight[:, k, None], 0.0
        )
    shares = jnp.where(back_part[None, :] == col_part[:, None], shares, 0.0)
    return picks, shares.astype(BF16)


def group_codes(users, ids, core):
    users = users.reshape(NCHIP, NC)
    user_a = jnp.where(core == 0, users[:, 0], users[:, 1])[:, None]
    user_b = jnp.where(core == 0, users[:, 1], users[:, 0])[:, None]
    group = jnp.arange(TOK // 16, dtype=jnp.int32)
    group_user = ids.reshape(1, TOK // 16, 16)[..., 0]
    hit_a, hit_b = group_user == user_a, group_user == user_b
    needed = (hit_a | hit_b).astype(jnp.int32)
    rank = jnp.sum(needed[:, None, :] * (group[None, :] < group[:, None]), axis=2)
    value = needed * (group + 8 * hit_a + 16 * hit_b)
    slot = jnp.arange(SLOTS, dtype=jnp.int32)
    return jnp.sum(jnp.where(rank[:, None, :] == slot[:, None], value[:, None, :], 0), axis=2)


def shards(
    residual,
    queries,
    new_keys,
    new_values,
    request_ids,
    page_store,
    page_sends,
    page_users,
    expert_ids,
    expert_weights,
    output_weight,
    norm_gain,
    gate_weight,
    up_weight,
    down_weight,
):
    me = lax.axis_index("req")
    width = residual.shape[1]
    half = width // 2
    swap = [(0, 1), (1, 0)]

    core = me % NC
    pages_far = lax.ppermute(page_store, "req", perm_core())
    sends_far = lax.ppermute(page_sends, "req", perm_core())
    codes = group_codes(page_users[0], request_ids, core)
    note = jnp.zeros((8, queries.shape[1]), BF16)
    note = note.at[0, : NCHIP * SLOTS].set(codes.T.reshape(-1).astype(BF16))
    block = jnp.concatenate([queries, note], axis=0)
    near = lax.ppermute(block, "req", perm_x())
    line_a = ring_line(block)
    near, line_a, pages_far, sends_far, weight = lax.optimization_barrier(
        (near, line_a, pages_far, sends_far, output_weight)
    )
    line = stack_blocks(line_a + ring_line(near))
    far_rows = weight.shape[0] // NC
    far_part = lax.dynamic_slice_in_dim(weight, core * far_rows, far_rows, 0)
    weight_mine = lax.ppermute(far_part, "tp", swap)

    chips = lax.dynamic_index_in_dim(jnp.asarray(chip_table()), me, 0, keepdims=False)
    page_a = page_sends[0][chips * NC + core]
    page_b = sends_far[0][chips * NC + core]
    line, chips, page_a, page_b = lax.optimization_barrier((line, chips, page_a, page_b))
    pieces = [line] + ring_rest(line)
    here = me // NC
    own, own_sums = own_attention(request_ids, queries, new_keys, new_values)
    picks, shares = routing(expert_ids, expert_weights)

    parts = None
    for first, last in ((0, 1), (1, 4)):
        group = pieces[first:last]
        if first:
            group, parts = lax.optimization_barrier((group, parts))
        rows = slice(8 * first, 8 * last)
        parts = page_attention(
            here[None], chips[rows], page_a[rows], page_b[rows], page_store, pages_far, group, parts
        )
    parts, weight_mine = lax.optimization_barrier((parts, weight_mine))
    weight_other = lax.ppermute(weight_mine, "req", perm_core())
    arrived = lax.all_to_all(
        parts, "req", 0, 0, tiled=True, axis_index_groups=core_groups()
    )
    own, picks, weight_other = lax.optimization_barrier((own, picks, weight_other))
    attended = merge_attention(codes.reshape(-1), arrived, own, own_sums)
    attended_far = lax.ppermute(attended, "tp", swap)
    mixed, sent = project(
        jnp.stack([lax.axis_index("tp"), core, 1 - core]),
        attended,
        attended_far,
        output_weight,
        weight_mine,
        weight_other,
        residual,
        norm_gain[None, :],
        picks,
    )
    rows = lax.all_to_all(sent.reshape(NREQ, 2 * CAP, half), "req", 0, 0, tiled=True)
    result = run_expert(rows, gate_weight[0], up_weight[0], down_weight[0])
    returned = lax.all_to_all(
        result.reshape(2 * NREQ, 2 * CAP, width // 4), ("req", "tp"), 0, 0, tiled=True
    )
    return combine(mixed, shares, returned.reshape(-1, width // 4))


def solution(mesh):
    placed = (
        P("req", None),
        P("req", "tp"),
        P("req", "tp"),
        P("req", "tp"),
        P("req"),
        P("req", None, None, "tp"),
        P("req", None),
        P("req", None),
        P("req", None),
        P("req", None),
        P("tp", None),
        P(),
        P("req", None, "tp"),
        P("req", None, "tp"),
        P("req", "tp", None),
    )
    return jax.shard_map(
        shards, mesh=mesh, in_specs=placed, out_specs=P("req", "tp"), check_vma=False
    )
```

```python
import math

import jax
import jax.numpy as jnp
import numpy as np
from jax import lax
from jax.experimental import pallas as pl
from jax.experimental.pallas import tpu as pltpu
from jax.sharding import PartitionSpec as P

HD = 128
TOP = 4
HEADS = 4
PAGE = 128
TOK = 128
CAP = 12
SLOTS = 6
ROWS = SLOTS * 16
STAT = HEADS * ROWS
BLOCK = STAT + 16
MERGE_PARTS = 2
NORM_EPS = 1e-06
SCALE = 1.0 / math.sqrt(HD)
LOG2E = math.log2(math.e)
NEG = -1e30
F32 = jnp.float32
BF16 = jnp.bfloat16

NY, NZ, NX, NC = 4, 4, 2, 2
NREQ = NY * NZ * NX * NC
NCHIP = NY * NZ * NX


def req_index(y, z, x, c):
    return ((y * NZ + z) * NX + x) * NC + c


def all_coords():
    return [
        (y, z, x, c) for y in range(NY) for z in range(NZ) for x in range(NX) for c in range(NC)
    ]


def perm_x():
    return [(req_index(y, z, x, c), req_index(y, z, 1 - x, c)) for y, z, x, c in all_coords()]


def perm_core():
    return [(req_index(y, z, x, c), req_index(y, z, x, 1 - c)) for y, z, x, c in all_coords()]


def perm_ring(stage, step):
    pairs = []
    for y, z, x, c in all_coords():
        if (c + stage) % 2 == 0:
            to = req_index((y + step) % NY, z, x, c)
        else:
            to = req_index(y, (z + step) % NZ, x, c)
        pairs.append((req_index(y, z, x, c), to))
    return pairs


PIECES = tuple((step, far) for step in (0, 1, 3, 2) for far in (0, 1))


def chip_table():
    table = np.zeros((NREQ, NCHIP), np.int32)
    for y, z, x, c in all_coords():
        row = []
        for d1, dx in PIECES:
            for d0 in range(4):
                dy, dz = (d0, d1) if c == 0 else (d1, d0)
                row.append(req_index((y - dy) % NY, (z - dz) % NZ, x ^ dx, 0) // NC)
        table[req_index(y, z, x, c)] = row
    return table


def core_groups():
    return [[chip * NC + core for chip in range(NCHIP)] for core in range(NC)]


def ring_line(block):
    return [block] + [lax.ppermute(block, "req", perm_ring(0, step)) for step in (1, 2, 3)]


def stack_kernel(*refs):
    out, sems = refs[-2:]
    copies = [
        pltpu.make_async_copy(block, out.at[i], sems.at[i]) for i, block in enumerate(refs[:-2])
    ]
    for copy in copies:
        copy.start()
    for copy in copies:
        copy.wait()


def stack_blocks(blocks):
    count = len(blocks)
    size = math.prod(blocks[0].shape) * 2
    return pl.pallas_call(
        stack_kernel,
        out_shape=jax.ShapeDtypeStruct((count, *blocks[0].shape), BF16),
        in_specs=[pl.BlockSpec(memory_space=pl.ANY)] * count,
        out_specs=pl.BlockSpec(memory_space=pl.ANY),
        scratch_shapes=[pltpu.SemaphoreType.DMA((count,))],
        compiler_params=pltpu.CompilerParams(vmem_limit_bytes=8 << 20),
        cost_estimate=pl.CostEstimate(
            flops=0, bytes_accessed=2 * count * size, transcendentals=0
        ),
        name="stack_blocks",
    )(*blocks)


def ring_rest(line):
    return [lax.ppermute(line, "req", perm_ring(1, step)) for step in (1, 3, 2)]


def attend(query, key_t, value_1, shift):
    scores = jnp.dot(query, key_t, preferred_element_type=F32)
    scores = shift(scores)
    top = jnp.max(scores, axis=1, keepdims=True)
    probs = jnp.exp2((scores - top) * (SCALE * LOG2E)).astype(BF16)
    both = jnp.dot(probs, value_1, preferred_element_type=F32)
    total = both[:, HD:]
    return both[:, :HD] / total, top * SCALE + jnp.log(total)


def by_head(rows):
    head = lax.broadcasted_iota(jnp.int32, (8, 128), 0) % HEADS
    tile = jnp.where(head == 0, rows[0], rows[1])
    tile = jnp.where(head == 2, rows[2], tile)
    return jnp.where(head == 3, rows[3], tile)


def page_kernel(place, chip_of, page_a, page_b, pages_a_in, pages_b_in, *refs):
    out, blocks, pages_a, pages_b, held, notes, codes, sems, load_sems, note_sem = refs[-10:]
    count = held.shape[0]
    pieces = refs[: count // 8]
    loads = [
        pltpu.make_async_copy(source, target, load_sems.at[n])
        for n, (source, target) in enumerate(
            [(piece, blocks.at[pl.ds(8 * n, 8)]) for n, piece in enumerate(pieces)]
            + [(pages_a_in, pages_a), (pages_b_in, pages_b)]
        )
    ]
    for load in loads:
        load.start()
    row = lax.broadcasted_iota(jnp.int32, (16, 128), 0)
    offset = lax.broadcasted_iota(jnp.int32, (16, 128), 1) - row
    sub = lax.broadcasted_iota(jnp.int32, (8, 128), 0)
    ones = jnp.ones((PAGE, HD), BF16)
    for load in loads[: len(pieces)]:
        load.wait()
    for i in range(count):
        words = blocks[i, TOK : TOK + 8, :128].astype(F32).astype(jnp.int32)
        notes[8 * i : 8 * i + 8, :] = words
    note_copy = pltpu.make_async_copy(notes, codes, note_sem)
    note_copy.start()
    for load in loads[len(pieces) :]:
        load.wait()
    note_copy.wait()

    def copy(i):
        return pltpu.make_async_copy(held.at[i], out.at[chip_of[i]], sems.at[i])

    def step(i, carry):
        pa, pb = page_a[i], page_b[i]
        code = [codes[i * 8 + j, place[0]] for j in range(SLOTS)]
        first = [pl.multiple_of((c & 7) * 16, 16) for c in code]
        bias = jnp.concatenate(
            [
                jnp.concatenate(
                    [
                        jnp.full((16, PAGE), jnp.where((c & bit) != 0, 0.0, NEG), F32)
                        for bit in (8, 16)
                    ],
                    axis=1,
                )
                for c in code
            ],
            axis=0,
        )
        mine = [offset == jnp.where(c >= 8, (c & 7) * 16, -1024) for c in code]
        scores = []
        for head in range(HEADS):
            cols = slice(head * HD, (head + 1) * HD)
            query = jnp.concatenate(
                [blocks[i, pl.ds(first[j], 16), cols] for j in range(SLOTS)], axis=0
            )
            key = jnp.concatenate([pages_a[pa, 0, :, cols], pages_b[pb, 0, :, cols]], axis=0)
            scores.append(
                lax.dot_general(
                    query, key, (((1,), (1,)), ((), ())), preferred_element_type=F32
                )
                + bias
            )
        tops = [jnp.max(s, axis=1, keepdims=True) for s in scores]
        probs = [
            jnp.exp2((s - t) * (SCALE * LOG2E)).astype(BF16) for s, t in zip(scores, tops)
        ]
        boths = []
        for head in range(HEADS):
            cols = slice(head * HD, (head + 1) * HD)
            value_1 = jnp.concatenate(
                [
                    jnp.concatenate([pages_a[pa, 1, :, cols], ones], axis=1),
                    jnp.concatenate([pages_b[pb, 1, :, cols], ones], axis=1),
                ],
                axis=0,
            )
            boths.append(jnp.dot(probs[head], value_1, preferred_element_type=F32))
        sums = []
        for head in range(HEADS):
            total = boths[head][:, HD:]
            got = boths[head][:, :HD] / total
            held[i, head * ROWS : (head + 1) * ROWS, :] = got.astype(BF16)
            total = tops[head] * SCALE + jnp.log(total)
            here = jnp.where(mine[0], total[:16], NEG)
            for j in range(1, SLOTS):
                here = jnp.maximum(here, jnp.where(mine[j], total[16 * j : 16 * j + 16], NEG))
            sums.append(jnp.max(here, axis=0, keepdims=True))
        tile = by_head(sums)
        high = tile.astype(BF16).astype(F32)
        rest = tile - high
        middle = rest.astype(BF16).astype(F32)
        upper = jnp.where(sub < HEADS, high, middle)
        lower = jnp.where(sub < HEADS, rest - middle, 0.0)
        held[i, STAT:BLOCK, :] = jnp.concatenate([upper, lower], axis=0).astype(BF16)
        copy(i).start()
        return carry

    lax.fori_loop(0, count, step, 0, unroll=4)
    lax.fori_loop(0, count, lambda i, carry: (copy(i).wait(), carry)[1], 0)


def page_attention(here, chip_of, page_a, page_b, pages_a, pages_b, pieces, last):
    count = 8 * len(pieces)
    before = [] if last is None else [last]
    return pl.pallas_call(
        page_kernel,
        out_shape=jax.ShapeDtypeStruct((NCHIP, BLOCK, HD), BF16),
        in_specs=[smem()] * 4 + [hbm()] * (2 + len(pieces) + len(before)),
        out_specs=hbm(),
        input_output_aliases={6 + len(pieces): 0} if before else {},
        scratch_shapes=[
            pltpu.VMEM((count, *pieces[0].shape[1:]), BF16),
            pltpu.VMEM(pages_a.shape, BF16),
            pltpu.VMEM(pages_b.shape, BF16),
            pltpu.VMEM((count, BLOCK, HD), BF16),
            pltpu.VMEM((count * 8, 128), jnp.int32),
            pltpu.SMEM((count * 8, 128), jnp.int32),
            pltpu.SemaphoreType.DMA((count,)),
            pltpu.SemaphoreType.DMA((2 + len(pieces),)),
            pltpu.SemaphoreType.DMA,
        ],
        compiler_params=pltpu.CompilerParams(vmem_limit_bytes=62 << 20),
        cost_estimate=pl.CostEstimate(
            flops=count * HEADS * 16 * ROWS * HD * HD,
            bytes_accessed=5 << 20,
            transcendentals=count * HEADS * ROWS * 2 * PAGE,
        ),
        name="page_attention",
    )(here, chip_of, page_a, page_b, pages_a, pages_b, *pieces, *before)


def smem():
    return pl.BlockSpec(memory_space=pltpu.SMEM)


def hbm():
    return pl.BlockSpec(memory_space=pltpu.HBM)


def vmem():
    return pl.BlockSpec(memory_space=pltpu.VMEM)


def own_kernel(request_col, request_row, queries, keys, values, out_hbm, total_hbm, out, total, sems):
    token = lax.broadcasted_iota(jnp.int32, (TOK, TOK), 0)
    key = lax.broadcasted_iota(jnp.int32, (TOK, TOK), 1)
    mask = (request_col[...] == request_row[...]) & (key <= token)
    ones = jnp.ones((TOK, HD), BF16)
    sums = []
    for head in range(HEADS):
        cols = slice(head * HD, (head + 1) * HD)
        got, low = attend(
            queries[:, cols],
            keys[:, cols].T,
            jnp.concatenate([values[:, cols], ones], axis=1),
            lambda s: jnp.where(mask, s, NEG),
        )
        out[head] = got
        sums.append(jnp.max(jnp.where(token == key, low, NEG), axis=0, keepdims=True))
    total[...] = by_head(sums)
    copies = [
        pltpu.make_async_copy(out, out_hbm, sems.at[0]),
        pltpu.make_async_copy(total, total_hbm, sems.at[1]),
    ]
    for copy in copies:
        copy.start()
    for copy in copies:
        copy.wait()


def own_attention(request_ids, queries, keys, values):
    return pl.pallas_call(
        own_kernel,
        out_shape=(
            jax.ShapeDtypeStruct((HEADS, TOK, HD), F32),
            jax.ShapeDtypeStruct((8, TOK), F32),
        ),
        in_specs=[vmem()] * 5,
        out_specs=(hbm(), hbm()),
        scratch_shapes=[
            pltpu.VMEM((HEADS, TOK, HD), F32),
            pltpu.VMEM((8, TOK), F32),
            pltpu.SemaphoreType.DMA((2,)),
        ],
        compiler_params=pltpu.CompilerParams(vmem_limit_bytes=62 << 20),
        cost_estimate=pl.CostEstimate(
            flops=64 << 20, bytes_accessed=1 << 20, transcendentals=HEADS * TOK * TOK
        ),
        name="own_attention",
    )(request_ids[:, None], request_ids[None, :], queries, keys, values)


def merge_kernel(
    here, codes, arrived_in, own_in, own_sums_in, out, acc, tiles, arrived, own, own_sums, sems
):
    part = NCHIP // MERGE_PARTS
    loads = [
        pltpu.make_async_copy(own_sums_in, own_sums, sems.at[0]),
        pltpu.make_async_copy(own_in, own, sems.at[1]),
    ] + [
        pltpu.make_async_copy(
            arrived_in.at[pl.ds(i * part, part)], arrived.at[pl.ds(i * part, part)], sems.at[2 + i]
        )
        for i in range(MERGE_PARTS)
    ]
    for load in loads:
        load.start()
    row = lax.broadcasted_iota(jnp.int32, (16, TOK), 0)
    offset = lax.broadcasted_iota(jnp.int32, (16, TOK), 1) - row

    def halves(tile):
        high = tile.astype(BF16).astype(F32)
        return high, tile - high

    def on_rows(parts, masks):
        blocks = []
        for head in range(HEADS):
            for mask in masks:
                blocks.append(
                    jnp.concatenate(
                        [
                            jnp.where(mask, jnp.broadcast_to(p[head : head + 1], (16, TOK)), 0.0)
                            for p in parts
                        ],
                        axis=1,
                    )
                )
        picked = jnp.concatenate(blocks, axis=0).astype(BF16)
        ones = jnp.ones((len(parts) * TOK, HD), BF16)
        return jnp.dot(picked, ones, preferred_element_type=F32)

    def collect(p, top):
        tile = arrived[p, STAT:BLOCK, :].astype(F32)
        tile = (tile[:8] + pltpu.roll(tile[:8], HEADS, 0)) + tile[8:]
        tiles[p] = tile
        return jnp.maximum(top, tile)

    loads[0].wait()
    top = own_sums[...]
    for i in range(MERGE_PARTS):
        loads[2 + i].wait()
        top = lax.fori_loop(i * part, (i + 1) * part, collect, top, unroll=4)
    loads[1].wait()
    whole = [offset == 16 * g for g in range(TOK // 16)]
    share = jnp.exp(own_sums[...] - top)
    acc[...] = own[...] * on_rows(halves(share), whole).reshape(HEADS, TOK, HD)

    def add(p, low):
        share = jnp.exp(tiles[p] - top).astype(BF16).astype(F32)
        code = [codes[j, p * NC + here[0] % NC] for j in range(SLOTS)]
        masks = [offset == jnp.where(c >= 8, (c & 7) * 16, -1024) for c in code]
        factor = on_rows((share,), masks)
        for j in range(SLOTS):
            at = pl.ds(pl.multiple_of((code[j] & 7) * 16, 16), 16)
            for head in range(HEADS):
                start = head * ROWS + 16 * j
                part = arrived[p, start : start + 16, :].astype(F32)
                acc[head, at, :] += part * factor[start : start + 16]
        return low + share

    low = lax.fori_loop(0, NCHIP, add, share, unroll=4)
    factor = on_rows(halves(1.0 / low), whole)
    for head in range(HEADS):
        out[:, head * HD : (head + 1) * HD] = (
            acc[head] * factor[head * TOK : (head + 1) * TOK]
        ).astype(BF16)


def merge_attention(here, codes, arrived, own, own_sums):
    return pl.pallas_call(
        merge_kernel,
        out_shape=jax.ShapeDtypeStruct((TOK, HEADS * HD), BF16),
        in_specs=[smem()] * 2 + [hbm()] * 3,
        out_specs=vmem(),
        scratch_shapes=[
            pltpu.VMEM((HEADS, TOK, HD), F32),
            pltpu.VMEM((NCHIP, 8, TOK), F32),
            pltpu.VMEM((NCHIP, BLOCK, HD), BF16),
            pltpu.VMEM((HEADS, TOK, HD), F32),
            pltpu.VMEM((8, TOK), F32),
            pltpu.SemaphoreType.DMA((2 + MERGE_PARTS,)),
        ],
        compiler_params=pltpu.CompilerParams(vmem_limit_bytes=62 << 20),
        cost_estimate=pl.CostEstimate(
            flops=64 << 20, bytes_accessed=4 << 20, transcendentals=1 << 18
        ),
        name="merge_attention",
    )(here, codes, arrived, own, own_sums)


def project_kernel(
    side,
    att,
    att_far,
    weight_in,
    weight_mine,
    weight_other,
    residual_in,
    gain,
    picks_in,
    mixed,
    sent,
    both,
    kept,
    rows,
    weight,
    weight_far,
    residual,
    picks,
    load_sems,
    sems,
):
    part = weight_mine.shape[0]
    loads = [
        pltpu.make_async_copy(source, target, load_sems.at[n])
        for n, (source, target) in enumerate(
            (
                (weight_in, weight),
                (residual_in, residual),
                (weight_mine, weight_far.at[pl.ds(pl.multiple_of(side[1] * part, part), part)]),
                (weight_other, weight_far.at[pl.ds(pl.multiple_of(side[2] * part, part), part)]),
                (picks_in, picks),
            )
        )
    ]
    for load in loads:
        load.start()
    half = residual.shape[1] // 2
    steps, step = rows.shape[0], rows.shape[1]
    loads[0].wait()
    total = jnp.dot(att[...], weight[...], preferred_element_type=F32)
    loads[1].wait()
    total += residual[...].astype(F32)
    loads[2].wait()
    loads[3].wait()
    total += jnp.dot(att_far[...], weight_far[...], preferred_element_type=F32)
    kept[...] = jnp.where(side[0] == 0, total[:, :half], total[:, half:])
    keep = pltpu.make_async_copy(kept, mixed, sems.at[steps])
    keep.start()
    scale = lax.rsqrt(jnp.mean(total * total, axis=1, keepdims=True) + NORM_EPS)
    normed = (total * scale * gain[...]).astype(BF16)
    both[:TOK] = normed[:, :half]
    both[TOK:] = normed[:, half:]
    copies = []
    loads[4].wait()
    for i in range(steps):
        rows[i] = jnp.dot(
            picks[i * step : (i + 1) * step], both[...], preferred_element_type=F32
        ).astype(BF16)
        copies.append(
            pltpu.make_async_copy(rows.at[i], sent.at[pl.ds(i * step, step)], sems.at[i])
        )
        copies[-1].start()
    keep.wait()
    for copy in copies:
        copy.wait()


def project(side, att, att_far, weight, weight_mine, weight_other, residual, gain, picks, steps=4):
    width = residual.shape[1]
    step = picks.shape[0] // steps
    return pl.pallas_call(
        project_kernel,
        out_shape=(
            jax.ShapeDtypeStruct((TOK, width // 2), F32),
            jax.ShapeDtypeStruct((picks.shape[0], width // 2), BF16),
        ),
        in_specs=[smem(), vmem(), vmem(), hbm(), hbm(), hbm(), hbm(), vmem(), hbm()],
        out_specs=(hbm(), hbm()),
        scratch_shapes=[
            pltpu.VMEM((2 * TOK, width // 2), BF16),
            pltpu.VMEM((TOK, width // 2), F32),
            pltpu.VMEM((steps, step, width // 2), BF16),
            pltpu.VMEM(weight.shape, BF16),
            pltpu.VMEM((2 * weight_mine.shape[0], width), BF16),
            pltpu.VMEM(residual.shape, BF16),
            pltpu.VMEM(picks.shape, BF16),
            pltpu.SemaphoreType.DMA((5,)),
            pltpu.SemaphoreType.DMA((steps + 1,)),
        ],
        compiler_params=pltpu.CompilerParams(vmem_limit_bytes=62 << 20),
        cost_estimate=pl.CostEstimate(
            flops=4 * TOK * 512 * width + 2 * picks.shape[0] * 256 * width // 2,
            bytes_accessed=10 << 20,
            transcendentals=TOK,
        ),
        name="project_dispatch",
    )(side, att, att_far, weight, weight_mine, weight_other, residual, gain, picks)


def expert_kernel(rows, gate, up, down, out, rows_v, gate_v, up_v, down_v, out_v, sems, back):
    steps, count = rows_v.shape[0], rows_v.shape[1]
    width = gate.shape[0]
    half, quarter = width // 2, width // 4

    def fetch(i):
        return pltpu.make_async_copy(rows.at[pl.ds(i * count, count)], rows_v.at[i], sems.at[i])

    def send(i):
        return pltpu.make_async_copy(out_v.at[i], out.at[pl.ds(i * count, count)], back.at[i])

    loads = [
        pltpu.make_async_copy(src, dst, sems.at[steps + n])
        for n, (src, dst) in enumerate(((gate, gate_v), (up, up_v), (down, down_v)))
    ]
    fetch(0).start()
    for load in loads:
        load.start()
    for i in range(1, steps):
        fetch(i).start()
    low_half = lax.broadcasted_iota(jnp.int32, (count // 2, 8, half), 1) < 4
    low_quarter = lax.broadcasted_iota(jnp.int32, (count // 2, 8, quarter), 1) < 4
    def step(i, carry):
        fetch(i).wait()
        wide = rows_v[i].astype(F32)
        tail = wide[:, 16:24].reshape(count // 2, 2, 8, half)
        even, odd = tail[:, 0], tail[:, 1]
        tail_0 = jnp.where(low_half, even, pltpu.roll(odd, 4, 1))
        tail_1 = jnp.where(low_half, pltpu.roll(even, 4, 1), odd)
        left = jnp.concatenate(
            [wide[:, 0:8].reshape(count * 8, half), tail_0.reshape(count * 4, half)], axis=0
        )
        right = jnp.concatenate(
            [wide[:, 8:16].reshape(count * 8, half), tail_1.reshape(count * 4, half)], axis=0
        )
        tokens = jnp.concatenate([left.astype(BF16), right.astype(BF16)], axis=1)
        if i == 0:
            loads[0].wait()
        gate_act = jnp.dot(tokens, gate_v[...], preferred_element_type=F32)
        if i == 0:
            loads[1].wait()
        up_act = jnp.dot(tokens, up_v[...], preferred_element_type=F32)
        hidden = (gate_act / (1.0 + jnp.exp(-gate_act)) * up_act).astype(BF16)
        if i == 0:
            loads[2].wait()
        result = jnp.dot(hidden, down_v[...], preferred_element_type=F32)
        for side in range(2):
            cols = [slice((2 * side + q) * quarter, (2 * side + q + 1) * quarter) for q in range(2)]
            main = [result[: count * 8, c].reshape(count, 8, quarter) for c in cols]
            tail = [result[count * 8 :, c].reshape(count // 2, 8, quarter) for c in cols]
            even = jnp.where(low_quarter, tail[0], pltpu.roll(tail[1], 4, 1))
            odd = jnp.where(low_quarter, pltpu.roll(tail[0], 4, 1), tail[1])
            last = jnp.stack([even, odd], axis=1).reshape(count, 8, quarter)
            out_v[i, :, side] = jnp.concatenate(main + [last], axis=1).astype(BF16)
        send(i).start()
        return carry

    for i in range(steps):
        step(i, 0)
    for i in range(steps):
        send(i).wait()


def run_expert(rows, gate, up, down, steps=2):
    count = rows.shape[0] // steps
    width, hidden = gate.shape
    return pl.pallas_call(
        expert_kernel,
        out_shape=jax.ShapeDtypeStruct((rows.shape[0], 2, 2 * CAP, width // 4), BF16),
        in_specs=[hbm()] * 4,
        out_specs=hbm(),
        scratch_shapes=[
            pltpu.VMEM((steps, count, 2 * CAP, width // 2), BF16),
            pltpu.VMEM((width, hidden), BF16),
            pltpu.VMEM((width, hidden), BF16),
            pltpu.VMEM((hidden, width), BF16),
            pltpu.VMEM((steps, count, 2, 2 * CAP, width // 4), BF16),
            pltpu.SemaphoreType.DMA((steps + 3,)),
            pltpu.SemaphoreType.DMA((steps,)),
        ],
        compiler_params=pltpu.CompilerParams(vmem_limit_bytes=62 << 20),
        cost_estimate=pl.CostEstimate(
            flops=6 * rows.shape[0] * CAP * width * hidden,
            bytes_accessed=15 << 20,
            transcendentals=rows.shape[0] * CAP * hidden,
        ),
        name="expert",
    )(rows, gate, up, down)


def combine_kernel(mixed, shares, rows, out, mixed_v, shares_v, rows_v, sems):
    parts, depth, width = rows_v.shape
    loads = [
        pltpu.make_async_copy(rows.at[pl.ds(i * depth, depth)], rows_v.at[i], sems.at[i])
        for i in range(parts)
    ]
    share_load = pltpu.make_async_copy(shares, shares_v, sems.at[parts])
    mixed_load = pltpu.make_async_copy(mixed, mixed_v, sems.at[parts + 1])
    share_load.start()
    for load in loads:
        load.start()
    mixed_load.start()
    share_load.wait()
    total = jnp.zeros((shares_v.shape[0], width), F32)
    for i in range(parts):
        loads[i].wait()
        total += jnp.dot(
            shares_v[:, i * depth : (i + 1) * depth], rows_v[i], preferred_element_type=F32
        )
    mixed_load.wait()
    out[:, :width] = (mixed_v[:, :width] + total[:TOK]).astype(BF16)
    out[:, width:] = (mixed_v[:, width:] + total[TOK:]).astype(BF16)


def combine(mixed, shares, rows, parts=4):
    return pl.pallas_call(
        combine_kernel,
        out_shape=jax.ShapeDtypeStruct(mixed.shape, BF16),
        in_specs=[hbm()] * 3,
        out_specs=vmem(),
        scratch_shapes=[
            pltpu.VMEM(mixed.shape, F32),
            pltpu.VMEM(shares.shape, BF16),
            pltpu.VMEM((parts, rows.shape[0] // parts, rows.shape[1]), BF16),
            pltpu.SemaphoreType.DMA((parts + 2,)),
        ],
        compiler_params=pltpu.CompilerParams(vmem_limit_bytes=62 << 20),
        cost_estimate=pl.CostEstimate(
            flops=2 * shares.shape[0] * rows.shape[0] * rows.shape[1],
            bytes_accessed=6 << 20,
            transcendentals=0,
        ),
        name="combine",
    )(mixed, shares, rows)


def slot_rows():
    slot = np.array(list(range(8)) * 2 + list(range(8, 12)) * 2, np.int32)
    part = np.array([0] * 8 + [1] * 8 + [0] * 4 + [1] * 4, np.int32)
    return slot, part


def routing(expert_ids, expert_weights):
    flat = expert_ids.reshape(-1)
    count = flat.shape[0]
    onehot = (flat[:, None] == jnp.arange(NREQ, dtype=jnp.int32)[None, :]).astype(BF16)
    earlier = (
        jnp.arange(count, dtype=jnp.int32)[None, :] < jnp.arange(count, dtype=jnp.int32)[:, None]
    ).astype(BF16)
    before = jnp.dot(earlier, onehot, preferred_element_type=F32)
    slot = jnp.sum(before * onehot.astype(F32), axis=1).astype(jnp.int32)
    place = (flat * CAP + slot).reshape(TOK, TOP)

    slot_at, part_at = slot_rows()
    row_place = (np.arange(NREQ, dtype=np.int32)[:, None] * CAP + slot_at[None, :]).reshape(-1)
    row_part = np.tile(part_at, NREQ)
    col_place = jnp.concatenate([place, place], axis=0)
    col_part = np.repeat(np.arange(2, dtype=np.int32), TOK)
    hit = jnp.zeros((row_place.shape[0], 2 * TOK), jnp.bool_)
    for k in range(TOP):
        hit = hit | (col_place[None, :, k] == row_place[:, None])
    picks = (hit & (row_part[:, None] == col_part[None, :])).astype(BF16)

    back_place = np.repeat(row_place.reshape(NREQ, 1, -1), 2, axis=1).reshape(-1)
    back_part = np.tile(part_at, 2 * NREQ)
    col_weight = jnp.concatenate([expert_weights, expert_weights], axis=0)
    shares = jnp.zeros((2 * TOK, back_place.shape[0]), F32)
    for k in range(TOP):
        shares = shares + jnp.where(
            col_place[:, k, None] == back_place[None, :], col_weight[:, k, None], 0.0
        )
    shares = jnp.where(back_part[None, :] == col_part[:, None], shares, 0.0)
    return picks, shares.astype(BF16)


def note_kernel(ids, users, queries, block, codes):
    lane = lax.broadcasted_iota(jnp.int32, (8, 128), 1)
    slot = lax.broadcasted_iota(jnp.int32, (8, 128), 0)
    user = jnp.broadcast_to(users[...], (8, 128))
    other = jnp.where(lane % 2 == 0, pltpu.roll(user, 127, 1), pltpu.roll(user, 1, 1))
    rank = jnp.zeros((8, 128), jnp.int32)
    total = jnp.zeros((8, 128), jnp.int32)
    for group in range(TOK // 16):
        mine = user == ids[group * 16]
        theirs = other == ids[group * 16]
        value = group + jnp.where(mine, 8, 0) + jnp.where(theirs, 16, 0)
        needed = mine | theirs
        total = jnp.where(needed & (rank == slot), value, total)
        rank = rank + jnp.where(needed, 1, 0)
    codes[...] = total
    block[:TOK] = queries[...]
    block[TOK:] = jnp.zeros((8, block.shape[1]), BF16)
    block[TOK:, :128] = total.astype(F32).astype(BF16)


def make_block(ids, users, queries):
    return pl.pallas_call(
        note_kernel,
        out_shape=(
            jax.ShapeDtypeStruct((TOK + 8, queries.shape[1]), BF16),
            jax.ShapeDtypeStruct((8, 128), jnp.int32),
        ),
        in_specs=[smem(), vmem(), vmem()],
        out_specs=(vmem(), vmem()),
        compiler_params=pltpu.CompilerParams(vmem_limit_bytes=62 << 20),
        cost_estimate=pl.CostEstimate(flops=1 << 16, bytes_accessed=1 << 18, transcendentals=0),
        name="make_block",
    )(ids, users, queries)


def shards(
    residual,
    queries,
    new_keys,
    new_values,
    request_ids,
    page_store,
    page_sends,
    page_users,
    expert_ids,
    expert_weights,
    output_weight,
    norm_gain,
    gate_weight,
    up_weight,
    down_weight,
):
    me = lax.axis_index("req")
    width = residual.shape[1]
    half = width // 2
    swap = [(0, 1), (1, 0)]

    core = me % NC
    pages_far = lax.ppermute(page_store, "req", perm_core())
    sends_far = lax.ppermute(page_sends, "req", perm_core())
    users = jnp.pad(page_users, ((0, 0), (0, 128 - NREQ)), constant_values=-1)
    block, codes = make_block(request_ids, users, queries)
    near = lax.ppermute(block, "req", perm_x())
    line_a = ring_line(block)
    near, line_a, pages_far, sends_far, weight = lax.optimization_barrier(
        (near, line_a, pages_far, sends_far, output_weight)
    )
    line = stack_blocks(line_a + ring_line(near))
    far_rows = weight.shape[0] // NC
    far_part = lax.dynamic_slice_in_dim(weight, core * far_rows, far_rows, 0)
    weight_mine = lax.ppermute(far_part, "tp", swap)

    chips = lax.dynamic_index_in_dim(jnp.asarray(chip_table()), me, 0, keepdims=False)
    page_a = page_sends[0][chips * NC + core]
    page_b = sends_far[0][chips * NC + core]
    line, chips, page_a, page_b = lax.optimization_barrier((line, chips, page_a, page_b))
    pieces = [line] + ring_rest(line)
    own, own_sums = own_attention(request_ids, queries, new_keys, new_values)
    picks, shares = routing(expert_ids, expert_weights)

    parts = None
    for first, last in ((0, 1), (1, 4)):
        group = pieces[first:last]
        if first:
            group, parts = lax.optimization_barrier((group, parts))
        rows = slice(8 * first, 8 * last)
        parts = page_attention(
            me[None], chips[rows], page_a[rows], page_b[rows], page_store, pages_far, group, parts
        )
    parts, weight_mine = lax.optimization_barrier((parts, weight_mine))
    weight_other = lax.ppermute(weight_mine, "req", perm_core())
    arrived = lax.all_to_all(
        parts, "req", 0, 0, tiled=True, axis_index_groups=core_groups()
    )
    own, picks, weight_other = lax.optimization_barrier((own, picks, weight_other))
    attended = merge_attention(me[None], codes, arrived, own, own_sums)
    attended_far = lax.ppermute(attended, "tp", swap)
    mixed, sent = project(
        jnp.stack([lax.axis_index("tp"), core, 1 - core]),
        attended,
        attended_far,
        output_weight,
        weight_mine,
        weight_other,
        residual,
        norm_gain[None, :],
        picks,
    )
    rows = lax.all_to_all(sent.reshape(NREQ, 2 * CAP, half), "req", 0, 0, tiled=True)
    result = run_expert(rows, gate_weight[0], up_weight[0], down_weight[0])
    returned = lax.all_to_all(
        result.reshape(2 * NREQ, 2 * CAP, width // 4), ("req", "tp"), 0, 0, tiled=True
    )
    return combine(mixed, shares, returned.reshape(-1, width // 4))


def solution(mesh):
    placed = (
        P("req", None),
        P("req", "tp"),
        P("req", "tp"),
        P("req", "tp"),
        P("req"),
        P("req", None, None, "tp"),
        P("req", None),
        P("req", None),
        P("req", None),
        P("req", None),
        P("tp", None),
        P(),
        P("req", None, "tp"),
        P("req", None, "tp"),
        P("req", "tp", None),
    )
    return jax.shard_map(
        shards, mesh=mesh, in_specs=placed, out_specs=P("req", "tp"), check_vma=False
    )
```

```python
import math

import jax
import jax.numpy as jnp
import numpy as np
from jax import lax
from jax.experimental import pallas as pl
from jax.experimental.pallas import tpu as pltpu
from jax.sharding import PartitionSpec as P

HD = 128
TOP = 4
HEADS = 4
PAGE = 128
TOK = 128
CAP = 12
SLOTS = 6
ROWS = SLOTS * 16
STAT = HEADS * ROWS
BLOCK = STAT + 16
MERGE_PARTS = 2
NORM_EPS = 1e-06
SCALE = 1.0 / math.sqrt(HD)
LOG2E = math.log2(math.e)
NEG = -1e30
F32 = jnp.float32
BF16 = jnp.bfloat16

NY, NZ, NX, NC = 4, 4, 2, 2
NREQ = NY * NZ * NX * NC
NCHIP = NY * NZ * NX


def req_index(y, z, x, c):
    return ((y * NZ + z) * NX + x) * NC + c


def all_coords():
    return [
        (y, z, x, c) for y in range(NY) for z in range(NZ) for x in range(NX) for c in range(NC)
    ]


def perm_x():
    return [(req_index(y, z, x, c), req_index(y, z, 1 - x, c)) for y, z, x, c in all_coords()]


def perm_core():
    return [(req_index(y, z, x, c), req_index(y, z, x, 1 - c)) for y, z, x, c in all_coords()]


def perm_ring(stage, step):
    pairs = []
    for y, z, x, c in all_coords():
        if (c + stage) % 2 == 0:
            to = req_index((y + step) % NY, z, x, c)
        else:
            to = req_index(y, (z + step) % NZ, x, c)
        pairs.append((req_index(y, z, x, c), to))
    return pairs


PIECES = tuple((step, far) for step in (0, 1, 3, 2) for far in (0, 1))


def chip_table():
    table = np.zeros((NREQ, NCHIP), np.int32)
    for y, z, x, c in all_coords():
        row = []
        for d1, dx in PIECES:
            for d0 in range(4):
                dy, dz = (d0, d1) if c == 0 else (d1, d0)
                row.append(req_index((y - dy) % NY, (z - dz) % NZ, x ^ dx, 0) // NC)
        table[req_index(y, z, x, c)] = row
    return table


def core_groups():
    return [[chip * NC + core for chip in range(NCHIP)] for core in range(NC)]


def ring_line(block):
    return [block] + [lax.ppermute(block, "req", perm_ring(0, step)) for step in (1, 2, 3)]


def stack_kernel(*refs):
    out, sems = refs[-2:]
    copies = [
        pltpu.make_async_copy(block, out.at[i], sems.at[i]) for i, block in enumerate(refs[:-2])
    ]
    for copy in copies:
        copy.start()
    for copy in copies:
        copy.wait()


def stack_blocks(blocks):
    count = len(blocks)
    size = math.prod(blocks[0].shape) * 2
    return pl.pallas_call(
        stack_kernel,
        out_shape=jax.ShapeDtypeStruct((count, *blocks[0].shape), BF16),
        in_specs=[hbm()] + [pl.BlockSpec(memory_space=pl.ANY)] * (count - 1),
        out_specs=pl.BlockSpec(memory_space=pl.ANY),
        scratch_shapes=[pltpu.SemaphoreType.DMA((count,))],
        compiler_params=pltpu.CompilerParams(vmem_limit_bytes=8 << 20),
        cost_estimate=pl.CostEstimate(
            flops=0, bytes_accessed=2 * count * size, transcendentals=0
        ),
        name="stack_blocks",
    )(*blocks)


def ring_rest(line):
    return [lax.ppermute(line, "req", perm_ring(1, step)) for step in (1, 3, 2)]


def attend(query, key_t, value_1, shift):
    scores = jnp.dot(query, key_t, preferred_element_type=F32)
    scores = shift(scores)
    top = jnp.max(scores, axis=1, keepdims=True)
    probs = jnp.exp2((scores - top) * (SCALE * LOG2E)).astype(BF16)
    both = jnp.dot(probs, value_1, preferred_element_type=F32)
    total = both[:, HD:]
    return both[:, :HD] / total, top * SCALE + jnp.log(total)


def by_head(rows):
    head = lax.broadcasted_iota(jnp.int32, (8, 128), 0) % HEADS
    tile = jnp.where(head == 0, rows[0], rows[1])
    tile = jnp.where(head == 2, rows[2], tile)
    return jnp.where(head == 3, rows[3], tile)


def page_kernel(place, chip_of, page_a, page_b, pages_a_in, pages_b_in, *refs):
    out, blocks, pages_a, pages_b, held, notes, codes, sems, load_sems, note_sem = refs[-10:]
    count = held.shape[0]
    pieces = refs[: count // 8]
    loads = [
        pltpu.make_async_copy(source, target, load_sems.at[n])
        for n, (source, target) in enumerate(
            [(piece, blocks.at[pl.ds(8 * n, 8)]) for n, piece in enumerate(pieces)]
            + [(pages_a_in, pages_a), (pages_b_in, pages_b)]
        )
    ]
    for load in loads:
        load.start()
    row = lax.broadcasted_iota(jnp.int32, (16, 128), 0)
    offset = lax.broadcasted_iota(jnp.int32, (16, 128), 1) - row
    sub = lax.broadcasted_iota(jnp.int32, (8, 128), 0)
    ones = jnp.ones((PAGE, HD), BF16)
    for load in loads[: len(pieces)]:
        load.wait()
    lane = lax.broadcasted_iota(jnp.int32, (8, 128), 1)
    words = jnp.zeros((8, 128), F32)
    for i in range(count):
        sent = blocks[i, TOK : TOK + 8, :128].astype(F32)
        mine = jnp.sum(jnp.where(lane == place[0], sent, 0.0), axis=1, keepdims=True)
        words = jnp.where(lane == i, mine, words)
    notes[...] = words.astype(jnp.int32)
    note_copy = pltpu.make_async_copy(notes, codes, note_sem)
    note_copy.start()
    for load in loads[len(pieces) :]:
        load.wait()
    note_copy.wait()

    def copy(i):
        return pltpu.make_async_copy(held.at[i], out.at[chip_of[i]], sems.at[i])

    def step(i, carry):
        pa, pb = page_a[i], page_b[i]
        code = [codes[j, i] for j in range(SLOTS)]
        first = [pl.multiple_of((c & 7) * 16, 16) for c in code]
        bias = jnp.concatenate(
            [
                jnp.concatenate(
                    [
                        jnp.full((16, PAGE), jnp.where((c & bit) != 0, 0.0, NEG), F32)
                        for bit in (8, 16)
                    ],
                    axis=1,
                )
                for c in code
            ],
            axis=0,
        )
        mine = [offset == jnp.where(c >= 8, (c & 7) * 16, -1024) for c in code]
        scores = []
        for head in range(HEADS):
            cols = slice(head * HD, (head + 1) * HD)
            query = jnp.concatenate(
                [blocks[i, pl.ds(first[j], 16), cols] for j in range(SLOTS)], axis=0
            )
            key = jnp.concatenate([pages_a[pa, 0, :, cols], pages_b[pb, 0, :, cols]], axis=0)
            scores.append(
                lax.dot_general(
                    query, key, (((1,), (1,)), ((), ())), preferred_element_type=F32
                )
                + bias
            )
        tops = [jnp.max(s, axis=1, keepdims=True) for s in scores]
        probs = [
            jnp.exp2((s - t) * (SCALE * LOG2E)).astype(BF16) for s, t in zip(scores, tops)
        ]
        boths = []
        for head in range(HEADS):
            cols = slice(head * HD, (head + 1) * HD)
            value_1 = jnp.concatenate(
                [
                    jnp.concatenate([pages_a[pa, 1, :, cols], ones], axis=1),
                    jnp.concatenate([pages_b[pb, 1, :, cols], ones], axis=1),
                ],
                axis=0,
            )
            boths.append(jnp.dot(probs[head], value_1, preferred_element_type=F32))
        sums = []
        for head in range(HEADS):
            total = boths[head][:, HD:]
            got = boths[head][:, :HD] / total
            held[i, head * ROWS : (head + 1) * ROWS, :] = got.astype(BF16)
            total = tops[head] * SCALE + jnp.log(total)
            here = jnp.where(mine[0], total[:16], NEG)
            for j in range(1, SLOTS):
                here = jnp.maximum(here, jnp.where(mine[j], total[16 * j : 16 * j + 16], NEG))
            sums.append(jnp.max(here, axis=0, keepdims=True))
        tile = by_head(sums)
        high = tile.astype(BF16).astype(F32)
        rest = tile - high
        middle = rest.astype(BF16).astype(F32)
        upper = jnp.where(sub < HEADS, high, middle)
        lower = jnp.where(sub < HEADS, rest - middle, 0.0)
        held[i, STAT:BLOCK, :] = jnp.concatenate([upper, lower], axis=0).astype(BF16)
        copy(i).start()
        return carry

    lax.fori_loop(0, count, step, 0, unroll=4)
    lax.fori_loop(0, count, lambda i, carry: (copy(i).wait(), carry)[1], 0)


def page_attention(here, chip_of, page_a, page_b, pages_a, pages_b, pieces, last):
    count = 8 * len(pieces)
    before = [] if last is None else [last]
    return pl.pallas_call(
        page_kernel,
        out_shape=jax.ShapeDtypeStruct((NCHIP, BLOCK, HD), BF16),
        in_specs=[smem()] * 4 + [hbm()] * (2 + len(pieces) + len(before)),
        out_specs=hbm(),
        input_output_aliases={6 + len(pieces): 0} if before else {},
        scratch_shapes=[
            pltpu.VMEM((count, *pieces[0].shape[1:]), BF16),
            pltpu.VMEM(pages_a.shape, BF16),
            pltpu.VMEM(pages_b.shape, BF16),
            pltpu.VMEM((count, BLOCK, HD), BF16),
            pltpu.VMEM((8, 128), jnp.int32),
            pltpu.SMEM((8, 128), jnp.int32),
            pltpu.SemaphoreType.DMA((count,)),
            pltpu.SemaphoreType.DMA((2 + len(pieces),)),
            pltpu.SemaphoreType.DMA,
        ],
        compiler_params=pltpu.CompilerParams(vmem_limit_bytes=62 << 20),
        cost_estimate=pl.CostEstimate(
            flops=count * HEADS * 16 * ROWS * HD * HD,
            bytes_accessed=5 << 20,
            transcendentals=count * HEADS * ROWS * 2 * PAGE,
        ),
        name="page_attention",
    )(here, chip_of, page_a, page_b, pages_a, pages_b, *pieces, *before)


def smem():
    return pl.BlockSpec(memory_space=pltpu.SMEM)


def hbm():
    return pl.BlockSpec(memory_space=pltpu.HBM)


def vmem():
    return pl.BlockSpec(memory_space=pltpu.VMEM)


def own_kernel(request_col, request_row, queries, keys, values, out_hbm, total_hbm, out, total, sems):
    token = lax.broadcasted_iota(jnp.int32, (TOK, TOK), 0)
    key = lax.broadcasted_iota(jnp.int32, (TOK, TOK), 1)
    mask = (request_col[...] == request_row[...]) & (key <= token)
    ones = jnp.ones((TOK, HD), BF16)
    sums = []
    for head in range(HEADS):
        cols = slice(head * HD, (head + 1) * HD)
        got, low = attend(
            queries[:, cols],
            keys[:, cols].T,
            jnp.concatenate([values[:, cols], ones], axis=1),
            lambda s: jnp.where(mask, s, NEG),
        )
        out[head] = got
        sums.append(jnp.max(jnp.where(token == key, low, NEG), axis=0, keepdims=True))
    total[...] = by_head(sums)
    copies = [
        pltpu.make_async_copy(out, out_hbm, sems.at[0]),
        pltpu.make_async_copy(total, total_hbm, sems.at[1]),
    ]
    for copy in copies:
        copy.start()
    for copy in copies:
        copy.wait()


def own_attention(request_ids, queries, keys, values):
    return pl.pallas_call(
        own_kernel,
        out_shape=(
            jax.ShapeDtypeStruct((HEADS, TOK, HD), F32),
            jax.ShapeDtypeStruct((8, TOK), F32),
        ),
        in_specs=[vmem()] * 5,
        out_specs=(hbm(), hbm()),
        scratch_shapes=[
            pltpu.VMEM((HEADS, TOK, HD), F32),
            pltpu.VMEM((8, TOK), F32),
            pltpu.SemaphoreType.DMA((2,)),
        ],
        compiler_params=pltpu.CompilerParams(vmem_limit_bytes=62 << 20),
        cost_estimate=pl.CostEstimate(
            flops=64 << 20, bytes_accessed=1 << 20, transcendentals=HEADS * TOK * TOK
        ),
        name="own_attention",
    )(request_ids[:, None], request_ids[None, :], queries, keys, values)


def merge_kernel(
    here, codes, arrived_in, own_in, own_sums_in, out, acc, tiles, arrived, own, own_sums, sems
):
    part = NCHIP // MERGE_PARTS
    loads = [
        pltpu.make_async_copy(own_sums_in, own_sums, sems.at[0]),
        pltpu.make_async_copy(own_in, own, sems.at[1]),
    ] + [
        pltpu.make_async_copy(
            arrived_in.at[pl.ds(i * part, part)], arrived.at[pl.ds(i * part, part)], sems.at[2 + i]
        )
        for i in range(MERGE_PARTS)
    ]
    for load in loads:
        load.start()
    row = lax.broadcasted_iota(jnp.int32, (16, TOK), 0)
    offset = lax.broadcasted_iota(jnp.int32, (16, TOK), 1) - row

    def halves(tile):
        high = tile.astype(BF16).astype(F32)
        return high, tile - high

    def on_rows(parts, masks):
        blocks = []
        for head in range(HEADS):
            for mask in masks:
                blocks.append(
                    jnp.concatenate(
                        [
                            jnp.where(mask, jnp.broadcast_to(p[head : head + 1], (16, TOK)), 0.0)
                            for p in parts
                        ],
                        axis=1,
                    )
                )
        picked = jnp.concatenate(blocks, axis=0).astype(BF16)
        ones = jnp.ones((len(parts) * TOK, HD), BF16)
        return jnp.dot(picked, ones, preferred_element_type=F32)

    def collect(p, top):
        tile = arrived[p, STAT:BLOCK, :].astype(F32)
        tile = (tile[:8] + pltpu.roll(tile[:8], HEADS, 0)) + tile[8:]
        tiles[p] = tile
        return jnp.maximum(top, tile)

    loads[0].wait()
    top = own_sums[...]
    for i in range(MERGE_PARTS):
        loads[2 + i].wait()
        top = lax.fori_loop(i * part, (i + 1) * part, collect, top, unroll=4)
    loads[1].wait()
    whole = [offset == 16 * g for g in range(TOK // 16)]
    share = jnp.exp(own_sums[...] - top)
    acc[...] = own[...] * on_rows(halves(share), whole).reshape(HEADS, TOK, HD)

    def add(p, low):
        share = jnp.exp(tiles[p] - top).astype(BF16).astype(F32)
        code = [codes[j, p * NC + here[0] % NC] for j in range(SLOTS)]
        masks = [offset == jnp.where(c >= 8, (c & 7) * 16, -1024) for c in code]
        factor = on_rows((share,), masks)
        for j in range(SLOTS):
            at = pl.ds(pl.multiple_of((code[j] & 7) * 16, 16), 16)
            for head in range(HEADS):
                start = head * ROWS + 16 * j
                part = arrived[p, start : start + 16, :].astype(F32)
                acc[head, at, :] += part * factor[start : start + 16]
        return low + share

    low = lax.fori_loop(0, NCHIP, add, share, unroll=4)
    factor = on_rows(halves(1.0 / low), whole)
    for head in range(HEADS):
        out[:, head * HD : (head + 1) * HD] = (
            acc[head] * factor[head * TOK : (head + 1) * TOK]
        ).astype(BF16)


def merge_attention(here, codes, arrived, own, own_sums):
    return pl.pallas_call(
        merge_kernel,
        out_shape=jax.ShapeDtypeStruct((TOK, HEADS * HD), BF16),
        in_specs=[smem()] * 2 + [hbm()] * 3,
        out_specs=vmem(),
        scratch_shapes=[
            pltpu.VMEM((HEADS, TOK, HD), F32),
            pltpu.VMEM((NCHIP, 8, TOK), F32),
            pltpu.VMEM((NCHIP, BLOCK, HD), BF16),
            pltpu.VMEM((HEADS, TOK, HD), F32),
            pltpu.VMEM((8, TOK), F32),
            pltpu.SemaphoreType.DMA((2 + MERGE_PARTS,)),
        ],
        compiler_params=pltpu.CompilerParams(vmem_limit_bytes=62 << 20),
        cost_estimate=pl.CostEstimate(
            flops=64 << 20, bytes_accessed=4 << 20, transcendentals=1 << 18
        ),
        name="merge_attention",
    )(here, codes, arrived, own, own_sums)


def project_kernel(
    side,
    att,
    att_far,
    weight_in,
    weight_mine,
    weight_other,
    residual_in,
    gain,
    picks_in,
    mixed,
    sent,
    both,
    kept,
    rows,
    weight,
    weight_far,
    residual,
    picks,
    load_sems,
    sems,
):
    part = weight_mine.shape[0]
    loads = [
        pltpu.make_async_copy(source, target, load_sems.at[n])
        for n, (source, target) in enumerate(
            (
                (weight_in, weight),
                (residual_in, residual),
                (weight_mine, weight_far.at[pl.ds(pl.multiple_of(side[1] * part, part), part)]),
                (weight_other, weight_far.at[pl.ds(pl.multiple_of(side[2] * part, part), part)]),
                (picks_in, picks),
            )
        )
    ]
    for load in loads:
        load.start()
    half = residual.shape[1] // 2
    steps, step = rows.shape[0], rows.shape[1]
    loads[0].wait()
    total = jnp.dot(att[...], weight[...], preferred_element_type=F32)
    loads[1].wait()
    total += residual[...].astype(F32)
    loads[2].wait()
    loads[3].wait()
    total += jnp.dot(att_far[...], weight_far[...], preferred_element_type=F32)
    kept[...] = jnp.where(side[0] == 0, total[:, :half], total[:, half:])
    keep = pltpu.make_async_copy(kept, mixed, sems.at[steps])
    keep.start()
    scale = lax.rsqrt(jnp.mean(total * total, axis=1, keepdims=True) + NORM_EPS)
    normed = (total * scale * gain[...]).astype(BF16)
    both[:TOK] = normed[:, :half]
    both[TOK:] = normed[:, half:]
    copies = []
    loads[4].wait()
    for i in range(steps):
        rows[i] = jnp.dot(
            picks[i * step : (i + 1) * step], both[...], preferred_element_type=F32
        ).astype(BF16)
        copies.append(
            pltpu.make_async_copy(rows.at[i], sent.at[pl.ds(i * step, step)], sems.at[i])
        )
        copies[-1].start()
    keep.wait()
    for copy in copies:
        copy.wait()


def project(side, att, att_far, weight, weight_mine, weight_other, residual, gain, picks, steps=4):
    width = residual.shape[1]
    step = picks.shape[0] // steps
    return pl.pallas_call(
        project_kernel,
        out_shape=(
            jax.ShapeDtypeStruct((TOK, width // 2), F32),
            jax.ShapeDtypeStruct((picks.shape[0], width // 2), BF16),
        ),
        in_specs=[smem(), vmem(), vmem(), hbm(), hbm(), hbm(), hbm(), vmem(), hbm()],
        out_specs=(hbm(), hbm()),
        scratch_shapes=[
            pltpu.VMEM((2 * TOK, width // 2), BF16),
            pltpu.VMEM((TOK, width // 2), F32),
            pltpu.VMEM((steps, step, width // 2), BF16),
            pltpu.VMEM(weight.shape, BF16),
            pltpu.VMEM((2 * weight_mine.shape[0], width), BF16),
            pltpu.VMEM(residual.shape, BF16),
            pltpu.VMEM(picks.shape, BF16),
            pltpu.SemaphoreType.DMA((5,)),
            pltpu.SemaphoreType.DMA((steps + 1,)),
        ],
        compiler_params=pltpu.CompilerParams(vmem_limit_bytes=62 << 20),
        cost_estimate=pl.CostEstimate(
            flops=4 * TOK * 512 * width + 2 * picks.shape[0] * 256 * width // 2,
            bytes_accessed=10 << 20,
            transcendentals=TOK,
        ),
        name="project_dispatch",
    )(side, att, att_far, weight, weight_mine, weight_other, residual, gain, picks)


def expert_kernel(rows, gate, up, down, out, rows_v, gate_v, up_v, down_v, out_v, sems, back):
    steps, count = rows_v.shape[0], rows_v.shape[1]
    width = gate.shape[0]
    half, quarter = width // 2, width // 4

    def fetch(i):
        return pltpu.make_async_copy(rows.at[pl.ds(i * count, count)], rows_v.at[i], sems.at[i])

    def send(i):
        return pltpu.make_async_copy(out_v.at[i], out.at[pl.ds(i * count, count)], back.at[i])

    loads = [
        pltpu.make_async_copy(src, dst, sems.at[steps + n])
        for n, (src, dst) in enumerate(((gate, gate_v), (up, up_v), (down, down_v)))
    ]
    fetch(0).start()
    for load in loads:
        load.start()
    for i in range(1, steps):
        fetch(i).start()
    low_half = lax.broadcasted_iota(jnp.int32, (count // 2, 8, half), 1) < 4
    low_quarter = lax.broadcasted_iota(jnp.int32, (count // 2, 8, quarter), 1) < 4
    def step(i, carry):
        fetch(i).wait()
        wide = rows_v[i].astype(F32)
        tail = wide[:, 16:24].reshape(count // 2, 2, 8, half)
        even, odd = tail[:, 0], tail[:, 1]
        tail_0 = jnp.where(low_half, even, pltpu.roll(odd, 4, 1))
        tail_1 = jnp.where(low_half, pltpu.roll(even, 4, 1), odd)
        left = jnp.concatenate(
            [wide[:, 0:8].reshape(count * 8, half), tail_0.reshape(count * 4, half)], axis=0
        )
        right = jnp.concatenate(
            [wide[:, 8:16].reshape(count * 8, half), tail_1.reshape(count * 4, half)], axis=0
        )
        tokens = jnp.concatenate([left.astype(BF16), right.astype(BF16)], axis=1)
        if i == 0:
            loads[0].wait()
        gate_act = jnp.dot(tokens, gate_v[...], preferred_element_type=F32)
        if i == 0:
            loads[1].wait()
        up_act = jnp.dot(tokens, up_v[...], preferred_element_type=F32)
        hidden = (gate_act / (1.0 + jnp.exp(-gate_act)) * up_act).astype(BF16)
        if i == 0:
            loads[2].wait()
        result = jnp.dot(hidden, down_v[...], preferred_element_type=F32)
        for side in range(2):
            cols = [slice((2 * side + q) * quarter, (2 * side + q + 1) * quarter) for q in range(2)]
            main = [result[: count * 8, c].reshape(count, 8, quarter) for c in cols]
            tail = [result[count * 8 :, c].reshape(count // 2, 8, quarter) for c in cols]
            even = jnp.where(low_quarter, tail[0], pltpu.roll(tail[1], 4, 1))
            odd = jnp.where(low_quarter, pltpu.roll(tail[0], 4, 1), tail[1])
            last = jnp.stack([even, odd], axis=1).reshape(count, 8, quarter)
            out_v[i, :, side] = jnp.concatenate(main + [last], axis=1).astype(BF16)
        send(i).start()
        return carry

    for i in range(steps):
        step(i, 0)
    for i in range(steps):
        send(i).wait()


def run_expert(rows, gate, up, down, steps=2):
    count = rows.shape[0] // steps
    width, hidden = gate.shape
    return pl.pallas_call(
        expert_kernel,
        out_shape=jax.ShapeDtypeStruct((rows.shape[0], 2, 2 * CAP, width // 4), BF16),
        in_specs=[hbm()] * 4,
        out_specs=hbm(),
        scratch_shapes=[
            pltpu.VMEM((steps, count, 2 * CAP, width // 2), BF16),
            pltpu.VMEM((width, hidden), BF16),
            pltpu.VMEM((width, hidden), BF16),
            pltpu.VMEM((hidden, width), BF16),
            pltpu.VMEM((steps, count, 2, 2 * CAP, width // 4), BF16),
            pltpu.SemaphoreType.DMA((steps + 3,)),
            pltpu.SemaphoreType.DMA((steps,)),
        ],
        compiler_params=pltpu.CompilerParams(vmem_limit_bytes=62 << 20),
        cost_estimate=pl.CostEstimate(
            flops=6 * rows.shape[0] * CAP * width * hidden,
            bytes_accessed=15 << 20,
            transcendentals=rows.shape[0] * CAP * hidden,
        ),
        name="expert",
    )(rows, gate, up, down)


def combine_kernel(mixed, shares, rows, out, mixed_v, shares_v, rows_v, sems):
    parts, depth, width = rows_v.shape
    loads = [
        pltpu.make_async_copy(rows.at[pl.ds(i * depth, depth)], rows_v.at[i], sems.at[i])
        for i in range(parts)
    ]
    share_load = pltpu.make_async_copy(shares, shares_v, sems.at[parts])
    mixed_load = pltpu.make_async_copy(mixed, mixed_v, sems.at[parts + 1])
    share_load.start()
    for load in loads:
        load.start()
    mixed_load.start()
    share_load.wait()
    total = jnp.zeros((shares_v.shape[0], width), F32)
    for i in range(parts):
        loads[i].wait()
        total += jnp.dot(
            shares_v[:, i * depth : (i + 1) * depth], rows_v[i], preferred_element_type=F32
        )
    mixed_load.wait()
    out[:, :width] = (mixed_v[:, :width] + total[:TOK]).astype(BF16)
    out[:, width:] = (mixed_v[:, width:] + total[TOK:]).astype(BF16)


def combine(mixed, shares, rows, parts=4):
    return pl.pallas_call(
        combine_kernel,
        out_shape=jax.ShapeDtypeStruct(mixed.shape, BF16),
        in_specs=[hbm()] * 3,
        out_specs=vmem(),
        scratch_shapes=[
            pltpu.VMEM(mixed.shape, F32),
            pltpu.VMEM(shares.shape, BF16),
            pltpu.VMEM((parts, rows.shape[0] // parts, rows.shape[1]), BF16),
            pltpu.SemaphoreType.DMA((parts + 2,)),
        ],
        compiler_params=pltpu.CompilerParams(vmem_limit_bytes=62 << 20),
        cost_estimate=pl.CostEstimate(
            flops=2 * shares.shape[0] * rows.shape[0] * rows.shape[1],
            bytes_accessed=6 << 20,
            transcendentals=0,
        ),
        name="combine",
    )(mixed, shares, rows)


def slot_rows():
    slot = np.array(list(range(8)) * 2 + list(range(8, 12)) * 2, np.int32)
    part = np.array([0] * 8 + [1] * 8 + [0] * 4 + [1] * 4, np.int32)
    return slot, part


def routing(expert_ids, expert_weights):
    flat = expert_ids.reshape(-1)
    count = flat.shape[0]
    onehot = (flat[:, None] == jnp.arange(NREQ, dtype=jnp.int32)[None, :]).astype(BF16)
    earlier = (
        jnp.arange(count, dtype=jnp.int32)[None, :] < jnp.arange(count, dtype=jnp.int32)[:, None]
    ).astype(BF16)
    before = jnp.dot(earlier, onehot, preferred_element_type=F32)
    slot = jnp.sum(before * onehot.astype(F32), axis=1).astype(jnp.int32)
    place = (flat * CAP + slot).reshape(TOK, TOP)

    slot_at, part_at = slot_rows()
    row_place = (np.arange(NREQ, dtype=np.int32)[:, None] * CAP + slot_at[None, :]).reshape(-1)
    row_part = np.tile(part_at, NREQ)
    col_place = jnp.concatenate([place, place], axis=0)
    col_part = np.repeat(np.arange(2, dtype=np.int32), TOK)
    hit = jnp.zeros((row_place.shape[0], 2 * TOK), jnp.bool_)
    for k in range(TOP):
        hit = hit | (col_place[None, :, k] == row_place[:, None])
    picks = (hit & (row_part[:, None] == col_part[None, :])).astype(BF16)

    back_place = np.repeat(row_place.reshape(NREQ, 1, -1), 2, axis=1).reshape(-1)
    back_part = np.tile(part_at, 2 * NREQ)
    col_weight = jnp.concatenate([expert_weights, expert_weights], axis=0)
    shares = jnp.zeros((2 * TOK, back_place.shape[0]), F32)
    for k in range(TOP):
        shares = shares + jnp.where(
            col_place[:, k, None] == back_place[None, :], col_weight[:, k, None], 0.0
        )
    shares = jnp.where(back_part[None, :] == col_part[:, None], shares, 0.0)
    return picks, shares.astype(BF16)


def note_kernel(ids, users, queries, block, codes, wide):
    lane = lax.broadcasted_iota(jnp.int32, (8, 128), 1)
    slot = lax.broadcasted_iota(jnp.int32, (8, 128), 0)
    wide[...] = jnp.full((8, 128), -1, jnp.int32)
    wide[:1, : users.shape[1]] = users[...]
    user = jnp.broadcast_to(wide[:1], (8, 128))
    other = jnp.where(lane % 2 == 0, pltpu.roll(user, 127, 1), pltpu.roll(user, 1, 1))
    rank = jnp.zeros((8, 128), jnp.int32)
    total = jnp.zeros((8, 128), jnp.int32)
    for group in range(TOK // 16):
        mine = user == ids[group * 16]
        theirs = other == ids[group * 16]
        value = group + jnp.where(mine, 8, 0) + jnp.where(theirs, 16, 0)
        needed = mine | theirs
        total = jnp.where(needed & (rank == slot), value, total)
        rank = rank + jnp.where(needed, 1, 0)
    codes[...] = total
    block[:TOK] = queries[...]
    block[TOK:] = jnp.zeros((8, block.shape[1]), BF16)
    block[TOK:, :128] = total.astype(F32).astype(BF16)


def make_block(ids, users, queries):
    return pl.pallas_call(
        note_kernel,
        out_shape=(
            jax.ShapeDtypeStruct((TOK + 8, queries.shape[1]), BF16),
            jax.ShapeDtypeStruct((8, 128), jnp.int32),
        ),
        in_specs=[smem(), vmem(), vmem()],
        out_specs=(vmem(), vmem()),
        scratch_shapes=[pltpu.VMEM((8, 128), jnp.int32)],
        compiler_params=pltpu.CompilerParams(vmem_limit_bytes=62 << 20),
        cost_estimate=pl.CostEstimate(flops=1 << 16, bytes_accessed=1 << 18, transcendentals=0),
        name="make_block",
    )(ids, users, queries)


def shards(
    residual,
    queries,
    new_keys,
    new_values,
    request_ids,
    page_store,
    page_sends,
    page_users,
    expert_ids,
    expert_weights,
    output_weight,
    norm_gain,
    gate_weight,
    up_weight,
    down_weight,
):
    me = lax.axis_index("req")
    width = residual.shape[1]
    half = width // 2
    swap = [(0, 1), (1, 0)]

    core = me % NC
    pages_far = lax.ppermute(page_store, "req", perm_core())
    sends_far = lax.ppermute(page_sends, "req", perm_core())
    block, codes = make_block(request_ids, page_users, queries)
    near = lax.ppermute(block, "req", perm_x())
    line_a = ring_line(block)
    near, line_a, pages_far, sends_far, weight = lax.optimization_barrier(
        (near, line_a, pages_far, sends_far, output_weight)
    )
    line = stack_blocks(line_a + ring_line(near))
    far_rows = weight.shape[0] // NC
    far_part = lax.dynamic_slice_in_dim(weight, core * far_rows, far_rows, 0)
    weight_mine = lax.ppermute(far_part, "tp", swap)

    chips = lax.dynamic_index_in_dim(jnp.asarray(chip_table()), me, 0, keepdims=False)
    page_a = page_sends[0][chips * NC + core]
    page_b = sends_far[0][chips * NC + core]
    line, chips, page_a, page_b = lax.optimization_barrier((line, chips, page_a, page_b))
    pieces = [line] + ring_rest(line)
    own, own_sums = own_attention(request_ids, queries, new_keys, new_values)
    picks, shares = routing(expert_ids, expert_weights)

    parts = None
    for first, last in ((0, 1), (1, 4)):
        group = pieces[first:last]
        if first:
            group, parts = lax.optimization_barrier((group, parts))
        rows = slice(8 * first, 8 * last)
        parts = page_attention(
            me[None], chips[rows], page_a[rows], page_b[rows], page_store, pages_far, group, parts
        )
    parts, weight_mine = lax.optimization_barrier((parts, weight_mine))
    weight_other = lax.ppermute(weight_mine, "req", perm_core())
    arrived = lax.all_to_all(
        parts, "req", 0, 0, tiled=True, axis_index_groups=core_groups()
    )
    own, picks, weight_other = lax.optimization_barrier((own, picks, weight_other))
    attended = merge_attention(me[None], codes, arrived, own, own_sums)
    attended_far = lax.ppermute(attended, "tp", swap)
    mixed, sent = project(
        jnp.stack([lax.axis_index("tp"), core, 1 - core]),
        attended,
        attended_far,
        output_weight,
        weight_mine,
        weight_other,
        residual,
        norm_gain[None, :],
        picks,
    )
    rows = lax.all_to_all(sent.reshape(NREQ, 2 * CAP, half), "req", 0, 0, tiled=True)
    result = run_expert(rows, gate_weight[0], up_weight[0], down_weight[0])
    returned = lax.all_to_all(
        result.reshape(2 * NREQ, 2 * CAP, width // 4), ("req", "tp"), 0, 0, tiled=True
    )
    return combine(mixed, shares, returned.reshape(-1, width // 4))


def solution(mesh):
    placed = (
        P("req", None),
        P("req", "tp"),
        P("req", "tp"),
        P("req", "tp"),
        P("req"),
        P("req", None, None, "tp"),
        P("req", None),
        P("req", None),
        P("req", None),
        P("req", None),
        P("tp", None),
        P(),
        P("req", None, "tp"),
        P("req", None, "tp"),
        P("req", "tp", None),
    )
    return jax.shard_map(
        shards, mesh=mesh, in_specs=placed, out_specs=P("req", "tp"), check_vma=False
    )
```

```python
import math

import jax
import jax.numpy as jnp
import numpy as np
from jax import lax
from jax.experimental import pallas as pl
from jax.experimental.pallas import tpu as pltpu
from jax.sharding import PartitionSpec as P

HD = 128
TOP = 4
HEADS = 4
PAGE = 128
TOK = 128
CAP = 12
SLOTS = 6
ROWS = SLOTS * 16
STAT = HEADS * ROWS
BLOCK = STAT + 16
MERGE_PARTS = 2
NORM_EPS = 1e-06
SCALE = 1.0 / math.sqrt(HD)
LOG2E = math.log2(math.e)
NEG = -1e30
F32 = jnp.float32
BF16 = jnp.bfloat16

NY, NZ, NX, NC = 4, 4, 2, 2
NREQ = NY * NZ * NX * NC
NCHIP = NY * NZ * NX


def req_index(y, z, x, c):
    return ((y * NZ + z) * NX + x) * NC + c


def all_coords():
    return [
        (y, z, x, c) for y in range(NY) for z in range(NZ) for x in range(NX) for c in range(NC)
    ]


def perm_x():
    return [(req_index(y, z, x, c), req_index(y, z, 1 - x, c)) for y, z, x, c in all_coords()]


def perm_core():
    return [(req_index(y, z, x, c), req_index(y, z, x, 1 - c)) for y, z, x, c in all_coords()]


def perm_ring(stage, step):
    pairs = []
    for y, z, x, c in all_coords():
        if (c + stage) % 2 == 0:
            to = req_index((y + step) % NY, z, x, c)
        else:
            to = req_index(y, (z + step) % NZ, x, c)
        pairs.append((req_index(y, z, x, c), to))
    return pairs


PIECES = tuple((step, far) for step in (0, 1, 3, 2) for far in (0, 1))


def chip_table():
    table = np.zeros((NREQ, NCHIP), np.int32)
    for y, z, x, c in all_coords():
        row = []
        for d1, dx in PIECES:
            for d0 in range(4):
                dy, dz = (d0, d1) if c == 0 else (d1, d0)
                row.append(req_index((y - dy) % NY, (z - dz) % NZ, x ^ dx, 0) // NC)
        table[req_index(y, z, x, c)] = row
    return table


def core_groups():
    return [[chip * NC + core for chip in range(NCHIP)] for core in range(NC)]


def ring_line(block):
    return [block] + [lax.ppermute(block, "req", perm_ring(0, step)) for step in (1, 2, 3)]


def stack_kernel(*refs):
    out, sems = refs[-2:]
    copies = [
        pltpu.make_async_copy(block, out.at[i], sems.at[i]) for i, block in enumerate(refs[:-2])
    ]
    for copy in copies:
        copy.start()
    for copy in copies:
        copy.wait()


def stack_blocks(blocks):
    count = len(blocks)
    size = math.prod(blocks[0].shape) * 2
    return pl.pallas_call(
        stack_kernel,
        out_shape=jax.ShapeDtypeStruct((count, *blocks[0].shape), BF16),
        in_specs=[hbm()] + [pl.BlockSpec(memory_space=pl.ANY)] * (count - 1),
        out_specs=pl.BlockSpec(memory_space=pl.ANY),
        scratch_shapes=[pltpu.SemaphoreType.DMA((count,))],
        compiler_params=pltpu.CompilerParams(vmem_limit_bytes=8 << 20),
        cost_estimate=pl.CostEstimate(
            flops=0, bytes_accessed=2 * count * size, transcendentals=0
        ),
        name="stack_blocks",
    )(*blocks)


def ring_rest(line):
    return [lax.ppermute(line, "req", perm_ring(1, step)) for step in (1, 3, 2)]


def attend(query, key_t, value_1, shift):
    scores = jnp.dot(query, key_t, preferred_element_type=F32)
    scores = shift(scores)
    top = jnp.max(scores, axis=1, keepdims=True)
    probs = jnp.exp2((scores - top) * (SCALE * LOG2E)).astype(BF16)
    both = jnp.dot(probs, value_1, preferred_element_type=F32)
    total = both[:, HD:]
    return both[:, :HD] / total, top * SCALE + jnp.log(total)


def by_head(rows):
    head = lax.broadcasted_iota(jnp.int32, (8, 128), 0) % HEADS
    tile = jnp.where(head == 0, rows[0], rows[1])
    tile = jnp.where(head == 2, rows[2], tile)
    return jnp.where(head == 3, rows[3], tile)


def page_kernel(place, chip_of, page_a, page_b, pages_a_in, pages_b_in, *refs):
    out, blocks, pages_a, pages_b, held, notes, codes, sems, load_sems, note_sem = refs[-10:]
    count = held.shape[0]
    pieces = refs[: count // 8]
    loads = [
        pltpu.make_async_copy(source, target, load_sems.at[n])
        for n, (source, target) in enumerate(
            [(piece, blocks.at[pl.ds(8 * n, 8)]) for n, piece in enumerate(pieces)]
            + [(pages_a_in, pages_a), (pages_b_in, pages_b)]
        )
    ]
    for load in loads:
        load.start()
    row = lax.broadcasted_iota(jnp.int32, (16, 128), 0)
    offset = lax.broadcasted_iota(jnp.int32, (16, 128), 1) - row
    sub = lax.broadcasted_iota(jnp.int32, (8, 128), 0)
    ones = jnp.ones((PAGE, HD), BF16)
    for load in loads[: len(pieces)]:
        load.wait()
    lane = lax.broadcasted_iota(jnp.int32, (8, 128), 1)
    words = jnp.zeros((8, 128), F32)
    for i in range(count):
        sent = blocks[i, TOK : TOK + 8, :128].astype(F32)
        mine = jnp.sum(jnp.where(lane == place[0], sent, 0.0), axis=1, keepdims=True)
        words = jnp.where(lane == i, mine, words)
    notes[...] = words.astype(jnp.int32)
    note_copy = pltpu.make_async_copy(notes, codes, note_sem)
    note_copy.start()
    for load in loads[len(pieces) :]:
        load.wait()
    note_copy.wait()

    def copy(i):
        return pltpu.make_async_copy(held.at[i], out.at[chip_of[i]], sems.at[i])

    def step(i, carry):
        pa, pb = page_a[i], page_b[i]
        code = [codes[j, i] for j in range(SLOTS)]
        first = [pl.multiple_of((c & 7) * 16, 16) for c in code]
        bias = jnp.concatenate(
            [
                jnp.concatenate(
                    [
                        jnp.full((16, PAGE), jnp.where((c & bit) != 0, 0.0, NEG), F32)
                        for bit in (8, 16)
                    ],
                    axis=1,
                )
                for c in code
            ],
            axis=0,
        )
        mine = [offset == jnp.where(c >= 8, (c & 7) * 16, -1024) for c in code]
        scores = []
        for head in range(HEADS):
            cols = slice(head * HD, (head + 1) * HD)
            query = jnp.concatenate(
                [blocks[i, pl.ds(first[j], 16), cols] for j in range(SLOTS)], axis=0
            )
            key = jnp.concatenate([pages_a[pa, 0, :, cols], pages_b[pb, 0, :, cols]], axis=0)
            scores.append(
                lax.dot_general(
                    query, key, (((1,), (1,)), ((), ())), preferred_element_type=F32
                )
                + bias
            )
        tops = [jnp.max(s, axis=1, keepdims=True) for s in scores]
        probs = [
            jnp.exp2((s - t) * (SCALE * LOG2E)).astype(BF16) for s, t in zip(scores, tops)
        ]
        boths = []
        for head in range(HEADS):
            cols = slice(head * HD, (head + 1) * HD)
            value_1 = jnp.concatenate(
                [
                    jnp.concatenate([pages_a[pa, 1, :, cols], ones], axis=1),
                    jnp.concatenate([pages_b[pb, 1, :, cols], ones], axis=1),
                ],
                axis=0,
            )
            boths.append(jnp.dot(probs[head], value_1, preferred_element_type=F32))
        sums = []
        for head in range(HEADS):
            total = boths[head][:, HD:]
            got = boths[head][:, :HD] / total
            held[i, head * ROWS : (head + 1) * ROWS, :] = got.astype(BF16)
            total = tops[head] * SCALE + jnp.log(total)
            here = jnp.where(mine[0], total[:16], NEG)
            for j in range(1, SLOTS):
                here = jnp.maximum(here, jnp.where(mine[j], total[16 * j : 16 * j + 16], NEG))
            sums.append(jnp.max(here, axis=0, keepdims=True))
        tile = by_head(sums)
        high = tile.astype(BF16).astype(F32)
        rest = tile - high
        middle = rest.astype(BF16).astype(F32)
        upper = jnp.where(sub < HEADS, high, middle)
        lower = jnp.where(sub < HEADS, rest - middle, 0.0)
        held[i, STAT:BLOCK, :] = jnp.concatenate([upper, lower], axis=0).astype(BF16)
        copy(i).start()
        return carry

    lax.fori_loop(0, count, step, 0, unroll=4)
    lax.fori_loop(0, count, lambda i, carry: (copy(i).wait(), carry)[1], 0)


def page_attention(here, chip_of, page_a, page_b, pages_a, pages_b, pieces, last):
    count = 8 * len(pieces)
    before = [] if last is None else [last]
    return pl.pallas_call(
        page_kernel,
        out_shape=jax.ShapeDtypeStruct((NCHIP, BLOCK, HD), BF16),
        in_specs=[smem()] * 4 + [hbm()] * (2 + len(pieces) + len(before)),
        out_specs=hbm(),
        input_output_aliases={6 + len(pieces): 0} if before else {},
        scratch_shapes=[
            pltpu.VMEM((count, *pieces[0].shape[1:]), BF16),
            pltpu.VMEM(pages_a.shape, BF16),
            pltpu.VMEM(pages_b.shape, BF16),
            pltpu.VMEM((count, BLOCK, HD), BF16),
            pltpu.VMEM((8, 128), jnp.int32),
            pltpu.SMEM((8, 128), jnp.int32),
            pltpu.SemaphoreType.DMA((count,)),
            pltpu.SemaphoreType.DMA((2 + len(pieces),)),
            pltpu.SemaphoreType.DMA,
        ],
        compiler_params=pltpu.CompilerParams(vmem_limit_bytes=62 << 20),
        cost_estimate=pl.CostEstimate(
            flops=count * HEADS * 16 * ROWS * HD * HD,
            bytes_accessed=5 << 20,
            transcendentals=count * HEADS * ROWS * 2 * PAGE,
        ),
        name="page_attention",
    )(here, chip_of, page_a, page_b, pages_a, pages_b, *pieces, *before)


def smem():
    return pl.BlockSpec(memory_space=pltpu.SMEM)


def hbm():
    return pl.BlockSpec(memory_space=pltpu.HBM)


def vmem():
    return pl.BlockSpec(memory_space=pltpu.VMEM)


def own_kernel(request_col, request_row, queries, keys, values, out_hbm, total_hbm, out, total, sems):
    token = lax.broadcasted_iota(jnp.int32, (TOK, TOK), 0)
    key = lax.broadcasted_iota(jnp.int32, (TOK, TOK), 1)
    mask = (request_col[...] == request_row[...]) & (key <= token)
    ones = jnp.ones((TOK, HD), BF16)
    sums = []
    for head in range(HEADS):
        cols = slice(head * HD, (head + 1) * HD)
        got, low = attend(
            queries[:, cols],
            keys[:, cols].T,
            jnp.concatenate([values[:, cols], ones], axis=1),
            lambda s: jnp.where(mask, s, NEG),
        )
        out[head] = got
        sums.append(jnp.max(jnp.where(token == key, low, NEG), axis=0, keepdims=True))
    total[...] = by_head(sums)
    copies = [
        pltpu.make_async_copy(out, out_hbm, sems.at[0]),
        pltpu.make_async_copy(total, total_hbm, sems.at[1]),
    ]
    for copy in copies:
        copy.start()
    for copy in copies:
        copy.wait()


def own_attention(request_ids, queries, keys, values):
    return pl.pallas_call(
        own_kernel,
        out_shape=(
            jax.ShapeDtypeStruct((HEADS, TOK, HD), F32),
            jax.ShapeDtypeStruct((8, TOK), F32),
        ),
        in_specs=[vmem()] * 5,
        out_specs=(hbm(), hbm()),
        scratch_shapes=[
            pltpu.VMEM((HEADS, TOK, HD), F32),
            pltpu.VMEM((8, TOK), F32),
            pltpu.SemaphoreType.DMA((2,)),
        ],
        compiler_params=pltpu.CompilerParams(vmem_limit_bytes=62 << 20),
        cost_estimate=pl.CostEstimate(
            flops=64 << 20, bytes_accessed=1 << 20, transcendentals=HEADS * TOK * TOK
        ),
        name="own_attention",
    )(request_ids[:, None], request_ids[None, :], queries, keys, values)


def merge_kernel(
    here, codes, arrived_in, own_in, own_sums_in, out, acc, tiles, arrived, own, own_sums, sems
):
    part = NCHIP // MERGE_PARTS
    loads = [
        pltpu.make_async_copy(own_sums_in, own_sums, sems.at[0]),
        pltpu.make_async_copy(own_in, own, sems.at[1]),
    ] + [
        pltpu.make_async_copy(
            arrived_in.at[pl.ds(i * part, part)], arrived.at[pl.ds(i * part, part)], sems.at[2 + i]
        )
        for i in range(MERGE_PARTS)
    ]
    for load in loads:
        load.start()
    row = lax.broadcasted_iota(jnp.int32, (16, TOK), 0)
    offset = lax.broadcasted_iota(jnp.int32, (16, TOK), 1) - row

    def halves(tile):
        high = tile.astype(BF16).astype(F32)
        return high, tile - high

    def on_rows(parts, masks):
        blocks = []
        for head in range(HEADS):
            for mask in masks:
                blocks.append(
                    jnp.concatenate(
                        [
                            jnp.where(mask, jnp.broadcast_to(p[head : head + 1], (16, TOK)), 0.0)
                            for p in parts
                        ],
                        axis=1,
                    )
                )
        picked = jnp.concatenate(blocks, axis=0).astype(BF16)
        ones = jnp.ones((len(parts) * TOK, HD), BF16)
        return jnp.dot(picked, ones, preferred_element_type=F32)

    def collect(p, top):
        tile = arrived[p, STAT:BLOCK, :].astype(F32)
        tile = (tile[:8] + pltpu.roll(tile[:8], HEADS, 0)) + tile[8:]
        tiles[p] = tile
        return jnp.maximum(top, tile)

    loads[0].wait()
    top = own_sums[...]
    for i in range(MERGE_PARTS):
        loads[2 + i].wait()
        top = lax.fori_loop(i * part, (i + 1) * part, collect, top, unroll=4)
    loads[1].wait()
    whole = [offset == 16 * g for g in range(TOK // 16)]
    share = jnp.exp(own_sums[...] - top)
    acc[...] = own[...] * on_rows(halves(share), whole).reshape(HEADS, TOK, HD)

    def add(p, low):
        share = jnp.exp(tiles[p] - top).astype(BF16).astype(F32)
        code = [codes[j, p * NC + here[0] % NC] for j in range(SLOTS)]
        masks = [offset == jnp.where(c >= 8, (c & 7) * 16, -1024) for c in code]
        factor = on_rows((share,), masks)
        for j in range(SLOTS):
            at = pl.ds(pl.multiple_of((code[j] & 7) * 16, 16), 16)
            for head in range(HEADS):
                start = head * ROWS + 16 * j
                part = arrived[p, start : start + 16, :].astype(F32)
                acc[head, at, :] += part * factor[start : start + 16]
        return low + share

    low = lax.fori_loop(0, NCHIP, add, share, unroll=8)
    factor = on_rows(halves(1.0 / low), whole)
    for head in range(HEADS):
        out[:, head * HD : (head + 1) * HD] = (
            acc[head] * factor[head * TOK : (head + 1) * TOK]
        ).astype(BF16)


def merge_attention(here, codes, arrived, own, own_sums):
    return pl.pallas_call(
        merge_kernel,
        out_shape=jax.ShapeDtypeStruct((TOK, HEADS * HD), BF16),
        in_specs=[smem()] * 2 + [hbm()] * 3,
        out_specs=vmem(),
        scratch_shapes=[
            pltpu.VMEM((HEADS, TOK, HD), F32),
            pltpu.VMEM((NCHIP, 8, TOK), F32),
            pltpu.VMEM((NCHIP, BLOCK, HD), BF16),
            pltpu.VMEM((HEADS, TOK, HD), F32),
            pltpu.VMEM((8, TOK), F32),
            pltpu.SemaphoreType.DMA((2 + MERGE_PARTS,)),
        ],
        compiler_params=pltpu.CompilerParams(vmem_limit_bytes=62 << 20),
        cost_estimate=pl.CostEstimate(
            flops=64 << 20, bytes_accessed=4 << 20, transcendentals=1 << 18
        ),
        name="merge_attention",
    )(here, codes, arrived, own, own_sums)


def project_kernel(
    side,
    att,
    att_far,
    weight_in,
    weight_mine,
    weight_other,
    residual_in,
    gain,
    picks_in,
    mixed,
    sent,
    both,
    kept,
    rows,
    weight,
    weight_far,
    residual,
    picks,
    load_sems,
    sems,
):
    part = weight_mine.shape[0]
    loads = [
        pltpu.make_async_copy(source, target, load_sems.at[n])
        for n, (source, target) in enumerate(
            (
                (weight_in, weight),
                (residual_in, residual),
                (weight_mine, weight_far.at[pl.ds(pl.multiple_of(side[1] * part, part), part)]),
                (weight_other, weight_far.at[pl.ds(pl.multiple_of(side[2] * part, part), part)]),
                (picks_in, picks),
            )
        )
    ]
    for load in loads:
        load.start()
    half = residual.shape[1] // 2
    steps, step = rows.shape[0], rows.shape[1]
    loads[0].wait()
    total = jnp.dot(att[...], weight[...], preferred_element_type=F32)
    loads[1].wait()
    total += residual[...].astype(F32)
    loads[2].wait()
    loads[3].wait()
    total += jnp.dot(att_far[...], weight_far[...], preferred_element_type=F32)
    kept[...] = jnp.where(side[0] == 0, total[:, :half], total[:, half:])
    keep = pltpu.make_async_copy(kept, mixed, sems.at[steps])
    keep.start()
    scale = lax.rsqrt(jnp.mean(total * total, axis=1, keepdims=True) + NORM_EPS)
    normed = (total * scale * gain[...]).astype(BF16)
    both[:TOK] = normed[:, :half]
    both[TOK:] = normed[:, half:]
    copies = []
    loads[4].wait()
    for i in range(steps):
        rows[i] = jnp.dot(
            picks[i * step : (i + 1) * step], both[...], preferred_element_type=F32
        ).astype(BF16)
        copies.append(
            pltpu.make_async_copy(rows.at[i], sent.at[pl.ds(i * step, step)], sems.at[i])
        )
        copies[-1].start()
    keep.wait()
    for copy in copies:
        copy.wait()


def project(side, att, att_far, weight, weight_mine, weight_other, residual, gain, picks, steps=4):
    width = residual.shape[1]
    step = picks.shape[0] // steps
    return pl.pallas_call(
        project_kernel,
        out_shape=(
            jax.ShapeDtypeStruct((TOK, width // 2), F32),
            jax.ShapeDtypeStruct((picks.shape[0], width // 2), BF16),
        ),
        in_specs=[smem(), vmem(), vmem(), hbm(), hbm(), hbm(), hbm(), vmem(), hbm()],
        out_specs=(hbm(), hbm()),
        scratch_shapes=[
            pltpu.VMEM((2 * TOK, width // 2), BF16),
            pltpu.VMEM((TOK, width // 2), F32),
            pltpu.VMEM((steps, step, width // 2), BF16),
            pltpu.VMEM(weight.shape, BF16),
            pltpu.VMEM((2 * weight_mine.shape[0], width), BF16),
            pltpu.VMEM(residual.shape, BF16),
            pltpu.VMEM(picks.shape, BF16),
            pltpu.SemaphoreType.DMA((5,)),
            pltpu.SemaphoreType.DMA((steps + 1,)),
        ],
        compiler_params=pltpu.CompilerParams(vmem_limit_bytes=62 << 20),
        cost_estimate=pl.CostEstimate(
            flops=4 * TOK * 512 * width + 2 * picks.shape[0] * 256 * width // 2,
            bytes_accessed=10 << 20,
            transcendentals=TOK,
        ),
        name="project_dispatch",
    )(side, att, att_far, weight, weight_mine, weight_other, residual, gain, picks)


def expert_kernel(rows, gate, up, down, out, rows_v, gate_v, up_v, down_v, out_v, sems, back):
    steps, count = rows_v.shape[0], rows_v.shape[1]
    width = gate.shape[0]
    half, quarter = width // 2, width // 4

    def fetch(i):
        return pltpu.make_async_copy(rows.at[pl.ds(i * count, count)], rows_v.at[i], sems.at[i])

    def send(i):
        return pltpu.make_async_copy(out_v.at[i], out.at[pl.ds(i * count, count)], back.at[i])

    loads = [
        pltpu.make_async_copy(src, dst, sems.at[steps + n])
        for n, (src, dst) in enumerate(((gate, gate_v), (up, up_v), (down, down_v)))
    ]
    fetch(0).start()
    for load in loads:
        load.start()
    for i in range(1, steps):
        fetch(i).start()
    low_half = lax.broadcasted_iota(jnp.int32, (count // 2, 8, half), 1) < 4
    low_quarter = lax.broadcasted_iota(jnp.int32, (count // 2, 8, quarter), 1) < 4
    def step(i, carry):
        fetch(i).wait()
        wide = rows_v[i].astype(F32)
        tail = wide[:, 16:24].reshape(count // 2, 2, 8, half)
        even, odd = tail[:, 0], tail[:, 1]
        tail_0 = jnp.where(low_half, even, pltpu.roll(odd, 4, 1))
        tail_1 = jnp.where(low_half, pltpu.roll(even, 4, 1), odd)
        left = jnp.concatenate(
            [wide[:, 0:8].reshape(count * 8, half), tail_0.reshape(count * 4, half)], axis=0
        )
        right = jnp.concatenate(
            [wide[:, 8:16].reshape(count * 8, half), tail_1.reshape(count * 4, half)], axis=0
        )
        tokens = jnp.concatenate([left.astype(BF16), right.astype(BF16)], axis=1)
        if i == 0:
            loads[0].wait()
        gate_act = jnp.dot(tokens, gate_v[...], preferred_element_type=F32)
        if i == 0:
            loads[1].wait()
        up_act = jnp.dot(tokens, up_v[...], preferred_element_type=F32)
        hidden = (gate_act / (1.0 + jnp.exp(-gate_act)) * up_act).astype(BF16)
        if i == 0:
            loads[2].wait()
        result = jnp.dot(hidden, down_v[...], preferred_element_type=F32)
        for side in range(2):
            cols = [slice((2 * side + q) * quarter, (2 * side + q + 1) * quarter) for q in range(2)]
            main = [result[: count * 8, c].reshape(count, 8, quarter) for c in cols]
            tail = [result[count * 8 :, c].reshape(count // 2, 8, quarter) for c in cols]
            even = jnp.where(low_quarter, tail[0], pltpu.roll(tail[1], 4, 1))
            odd = jnp.where(low_quarter, pltpu.roll(tail[0], 4, 1), tail[1])
            last = jnp.stack([even, odd], axis=1).reshape(count, 8, quarter)
            out_v[i, :, side] = jnp.concatenate(main + [last], axis=1).astype(BF16)
        send(i).start()
        return carry

    for i in range(steps):
        step(i, 0)
    for i in range(steps):
        send(i).wait()


def run_expert(rows, gate, up, down, steps=4):
    count = rows.shape[0] // steps
    width, hidden = gate.shape
    return pl.pallas_call(
        expert_kernel,
        out_shape=jax.ShapeDtypeStruct((rows.shape[0], 2, 2 * CAP, width // 4), BF16),
        in_specs=[hbm()] * 4,
        out_specs=hbm(),
        scratch_shapes=[
            pltpu.VMEM((steps, count, 2 * CAP, width // 2), BF16),
            pltpu.VMEM((width, hidden), BF16),
            pltpu.VMEM((width, hidden), BF16),
            pltpu.VMEM((hidden, width), BF16),
            pltpu.VMEM((steps, count, 2, 2 * CAP, width // 4), BF16),
            pltpu.SemaphoreType.DMA((steps + 3,)),
            pltpu.SemaphoreType.DMA((steps,)),
        ],
        compiler_params=pltpu.CompilerParams(vmem_limit_bytes=62 << 20),
        cost_estimate=pl.CostEstimate(
            flops=6 * rows.shape[0] * CAP * width * hidden,
            bytes_accessed=15 << 20,
            transcendentals=rows.shape[0] * CAP * hidden,
        ),
        name="expert",
    )(rows, gate, up, down)


def combine_kernel(mixed, shares, rows, out, mixed_v, shares_v, rows_v, sems):
    parts, depth, width = rows_v.shape
    loads = [
        pltpu.make_async_copy(rows.at[pl.ds(i * depth, depth)], rows_v.at[i], sems.at[i])
        for i in range(parts)
    ]
    share_load = pltpu.make_async_copy(shares, shares_v, sems.at[parts])
    mixed_load = pltpu.make_async_copy(mixed, mixed_v, sems.at[parts + 1])
    share_load.start()
    for load in loads:
        load.start()
    mixed_load.start()
    share_load.wait()
    total = jnp.zeros((shares_v.shape[0], width), F32)
    for i in range(parts):
        loads[i].wait()
        total += jnp.dot(
            shares_v[:, i * depth : (i + 1) * depth], rows_v[i], preferred_element_type=F32
        )
    mixed_load.wait()
    out[:, :width] = (mixed_v[:, :width] + total[:TOK]).astype(BF16)
    out[:, width:] = (mixed_v[:, width:] + total[TOK:]).astype(BF16)


def combine(mixed, shares, rows, parts=4):
    return pl.pallas_call(
        combine_kernel,
        out_shape=jax.ShapeDtypeStruct(mixed.shape, BF16),
        in_specs=[hbm()] * 3,
        out_specs=vmem(),
        scratch_shapes=[
            pltpu.VMEM(mixed.shape, F32),
            pltpu.VMEM(shares.shape, BF16),
            pltpu.VMEM((parts, rows.shape[0] // parts, rows.shape[1]), BF16),
            pltpu.SemaphoreType.DMA((parts + 2,)),
        ],
        compiler_params=pltpu.CompilerParams(vmem_limit_bytes=62 << 20),
        cost_estimate=pl.CostEstimate(
            flops=2 * shares.shape[0] * rows.shape[0] * rows.shape[1],
            bytes_accessed=6 << 20,
            transcendentals=0,
        ),
        name="combine",
    )(mixed, shares, rows)


def slot_rows():
    slot = np.array(list(range(8)) * 2 + list(range(8, 12)) * 2, np.int32)
    part = np.array([0] * 8 + [1] * 8 + [0] * 4 + [1] * 4, np.int32)
    return slot, part


def routing(expert_ids, expert_weights):
    flat = expert_ids.reshape(-1)
    count = flat.shape[0]
    onehot = (flat[:, None] == jnp.arange(NREQ, dtype=jnp.int32)[None, :]).astype(BF16)
    earlier = (
        jnp.arange(count, dtype=jnp.int32)[None, :] < jnp.arange(count, dtype=jnp.int32)[:, None]
    ).astype(BF16)
    before = jnp.dot(earlier, onehot, preferred_element_type=F32)
    slot = jnp.sum(before * onehot.astype(F32), axis=1).astype(jnp.int32)
    place = (flat * CAP + slot).reshape(TOK, TOP)

    slot_at, part_at = slot_rows()
    row_place = (np.arange(NREQ, dtype=np.int32)[:, None] * CAP + slot_at[None, :]).reshape(-1)
    row_part = np.tile(part_at, NREQ)
    col_place = jnp.concatenate([place, place], axis=0)
    col_part = np.repeat(np.arange(2, dtype=np.int32), TOK)
    hit = jnp.zeros((row_place.shape[0], 2 * TOK), jnp.bool_)
    for k in range(TOP):
        hit = hit | (col_place[None, :, k] == row_place[:, None])
    picks = (hit & (row_part[:, None] == col_part[None, :])).astype(BF16)

    back_place = np.repeat(row_place.reshape(NREQ, 1, -1), 2, axis=1).reshape(-1)
    back_part = np.tile(part_at, 2 * NREQ)
    col_weight = jnp.concatenate([expert_weights, expert_weights], axis=0)
    shares = jnp.zeros((2 * TOK, back_place.shape[0]), F32)
    for k in range(TOP):
        shares = shares + jnp.where(
            col_place[:, k, None] == back_place[None, :], col_weight[:, k, None], 0.0
        )
    shares = jnp.where(back_part[None, :] == col_part[:, None], shares, 0.0)
    return picks, shares.astype(BF16)


def note_kernel(ids, users, queries, block, codes, wide):
    lane = lax.broadcasted_iota(jnp.int32, (8, 128), 1)
    slot = lax.broadcasted_iota(jnp.int32, (8, 128), 0)
    wide[...] = jnp.full((8, 128), -1, jnp.int32)
    wide[:1, : users.shape[1]] = users[...]
    user = jnp.broadcast_to(wide[:1], (8, 128))
    other = jnp.where(lane % 2 == 0, pltpu.roll(user, 127, 1), pltpu.roll(user, 1, 1))
    rank = jnp.zeros((8, 128), jnp.int32)
    total = jnp.zeros((8, 128), jnp.int32)
    for group in range(TOK // 16):
        mine = user == ids[group * 16]
        theirs = other == ids[group * 16]
        value = group + jnp.where(mine, 8, 0) + jnp.where(theirs, 16, 0)
        needed = mine | theirs
        total = jnp.where(needed & (rank == slot), value, total)
        rank = rank + jnp.where(needed, 1, 0)
    codes[...] = total
    block[:TOK] = queries[...]
    block[TOK:] = jnp.zeros((8, block.shape[1]), BF16)
    block[TOK:, :128] = total.astype(F32).astype(BF16)


def make_block(ids, users, queries):
    return pl.pallas_call(
        note_kernel,
        out_shape=(
            jax.ShapeDtypeStruct((TOK + 8, queries.shape[1]), BF16),
            jax.ShapeDtypeStruct((8, 128), jnp.int32),
        ),
        in_specs=[smem(), vmem(), vmem()],
        out_specs=(vmem(), vmem()),
        scratch_shapes=[pltpu.VMEM((8, 128), jnp.int32)],
        compiler_params=pltpu.CompilerParams(vmem_limit_bytes=62 << 20),
        cost_estimate=pl.CostEstimate(flops=1 << 16, bytes_accessed=1 << 18, transcendentals=0),
        name="make_block",
    )(ids, users, queries)


def shards(
    residual,
    queries,
    new_keys,
    new_values,
    request_ids,
    page_store,
    page_sends,
    page_users,
    expert_ids,
    expert_weights,
    output_weight,
    norm_gain,
    gate_weight,
    up_weight,
    down_weight,
):
    me = lax.axis_index("req")
    width = residual.shape[1]
    half = width // 2
    swap = [(0, 1), (1, 0)]

    core = me % NC
    pages_far = lax.ppermute(page_store, "req", perm_core())
    sends_far = lax.ppermute(page_sends, "req", perm_core())
    block, codes = make_block(request_ids, page_users, queries)
    near = lax.ppermute(block, "req", perm_x())
    line_a = ring_line(block)
    near, line_a, pages_far, sends_far, weight = lax.optimization_barrier(
        (near, line_a, pages_far, sends_far, output_weight)
    )
    line = stack_blocks(line_a + ring_line(near))
    far_rows = weight.shape[0] // NC
    far_part = lax.dynamic_slice_in_dim(weight, core * far_rows, far_rows, 0)
    weight_mine = lax.ppermute(far_part, "tp", swap)

    chips = lax.dynamic_index_in_dim(jnp.asarray(chip_table()), me, 0, keepdims=False)
    page_a = page_sends[0][chips * NC + core]
    page_b = sends_far[0][chips * NC + core]
    line, chips, page_a, page_b = lax.optimization_barrier((line, chips, page_a, page_b))
    pieces = [line] + ring_rest(line)
    own, own_sums = own_attention(request_ids, queries, new_keys, new_values)
    picks, shares = routing(expert_ids, expert_weights)

    parts = None
    for first, last in ((0, 1), (1, 4)):
        group = pieces[first:last]
        if first:
            group, parts = lax.optimization_barrier((group, parts))
        rows = slice(8 * first, 8 * last)
        parts = page_attention(
            me[None], chips[rows], page_a[rows], page_b[rows], page_store, pages_far, group, parts
        )
    parts, weight_mine = lax.optimization_barrier((parts, weight_mine))
    weight_other = lax.ppermute(weight_mine, "req", perm_core())
    arrived = lax.all_to_all(
        parts, "req", 0, 0, tiled=True, axis_index_groups=core_groups()
    )
    own, picks, weight_other = lax.optimization_barrier((own, picks, weight_other))
    attended = merge_attention(me[None], codes, arrived, own, own_sums)
    attended_far = lax.ppermute(attended, "tp", swap)
    mixed, sent = project(
        jnp.stack([lax.axis_index("tp"), core, 1 - core]),
        attended,
        attended_far,
        output_weight,
        weight_mine,
        weight_other,
        residual,
        norm_gain[None, :],
        picks,
    )
    rows = lax.all_to_all(sent.reshape(NREQ, 2 * CAP, half), "req", 0, 0, tiled=True)
    result = run_expert(rows, gate_weight[0], up_weight[0], down_weight[0])
    returned = lax.all_to_all(
        result.reshape(2 * NREQ, 2 * CAP, width // 4), ("req", "tp"), 0, 0, tiled=True
    )
    return combine(mixed, shares, returned.reshape(-1, width // 4))


def solution(mesh):
    placed = (
        P("req", None),
        P("req", "tp"),
        P("req", "tp"),
        P("req", "tp"),
        P("req"),
        P("req", None, None, "tp"),
        P("req", None),
        P("req", None),
        P("req", None),
        P("req", None),
        P("tp", None),
        P(),
        P("req", None, "tp"),
        P("req", None, "tp"),
        P("req", "tp", None),
    )
    return jax.shard_map(
        shards, mesh=mesh, in_specs=placed, out_specs=P("req", "tp"), check_vma=False
    )
```

```python
import math

import jax
import jax.numpy as jnp
import numpy as np
from jax import lax
from jax.experimental import pallas as pl
from jax.experimental.pallas import tpu as pltpu
from jax.sharding import PartitionSpec as P

HD = 128
TOP = 4
HEADS = 4
PAGE = 128
TOK = 128
CAP = 12
SLOTS = 6
ROWS = SLOTS * 16
STAT = HEADS * ROWS
BLOCK = STAT + 16
MERGE_PARTS = 2
NORM_EPS = 1e-06
SCALE = 1.0 / math.sqrt(HD)
LOG2E = math.log2(math.e)
NEG = -1e30
F32 = jnp.float32
BF16 = jnp.bfloat16

NY, NZ, NX, NC = 4, 4, 2, 2
NREQ = NY * NZ * NX * NC
NCHIP = NY * NZ * NX


def req_index(y, z, x, c):
    return ((y * NZ + z) * NX + x) * NC + c


def all_coords():
    return [
        (y, z, x, c) for y in range(NY) for z in range(NZ) for x in range(NX) for c in range(NC)
    ]


def perm_x():
    return [(req_index(y, z, x, c), req_index(y, z, 1 - x, c)) for y, z, x, c in all_coords()]


def perm_core():
    return [(req_index(y, z, x, c), req_index(y, z, x, 1 - c)) for y, z, x, c in all_coords()]


def perm_ring(stage, step):
    pairs = []
    for y, z, x, c in all_coords():
        if (c + stage) % 2 == 0:
            to = req_index((y + step) % NY, z, x, c)
        else:
            to = req_index(y, (z + step) % NZ, x, c)
        pairs.append((req_index(y, z, x, c), to))
    return pairs


PIECES = tuple((step, far) for step in (0, 2, 1, 3) for far in (0, 1))


def chip_table():
    table = np.zeros((NREQ, NCHIP), np.int32)
    for y, z, x, c in all_coords():
        row = []
        for d1, dx in PIECES:
            for d0 in range(4):
                dy, dz = (d0, d1) if c == 0 else (d1, d0)
                row.append(req_index((y - dy) % NY, (z - dz) % NZ, x ^ dx, 0) // NC)
        table[req_index(y, z, x, c)] = row
    return table


def core_groups():
    return [[chip * NC + core for chip in range(NCHIP)] for core in range(NC)]


def ring_line(block):
    return [block] + [lax.ppermute(block, "req", perm_ring(0, step)) for step in (1, 2, 3)]


def stack_kernel(*refs):
    out, sems = refs[-2:]
    copies = [
        pltpu.make_async_copy(block, out.at[i], sems.at[i]) for i, block in enumerate(refs[:-2])
    ]
    for copy in copies:
        copy.start()
    for copy in copies:
        copy.wait()


def stack_blocks(blocks):
    count = len(blocks)
    size = math.prod(blocks[0].shape) * 2
    return pl.pallas_call(
        stack_kernel,
        out_shape=jax.ShapeDtypeStruct((count, *blocks[0].shape), BF16),
        in_specs=[hbm()] + [pl.BlockSpec(memory_space=pl.ANY)] * (count - 1),
        out_specs=pl.BlockSpec(memory_space=pl.ANY),
        scratch_shapes=[pltpu.SemaphoreType.DMA((count,))],
        compiler_params=pltpu.CompilerParams(vmem_limit_bytes=8 << 20),
        cost_estimate=pl.CostEstimate(
            flops=0, bytes_accessed=2 * count * size, transcendentals=0
        ),
        name="stack_blocks",
    )(*blocks)


def ring_rest(line):
    return [lax.ppermute(line, "req", perm_ring(1, step)) for step in (2, 1, 3)]


def attend(query, key_t, value_1, shift):
    scores = jnp.dot(query, key_t, preferred_element_type=F32)
    scores = shift(scores)
    top = jnp.max(scores, axis=1, keepdims=True)
    probs = jnp.exp2((scores - top) * (SCALE * LOG2E)).astype(BF16)
    both = jnp.dot(probs, value_1, preferred_element_type=F32)
    total = both[:, HD:]
    return both[:, :HD] / total, top * SCALE + jnp.log(total)


def by_head(rows):
    head = lax.broadcasted_iota(jnp.int32, (8, 128), 0) % HEADS
    tile = jnp.where(head == 0, rows[0], rows[1])
    tile = jnp.where(head == 2, rows[2], tile)
    return jnp.where(head == 3, rows[3], tile)


def page_kernel(place, chip_of, page_a, page_b, pages_a_in, pages_b_in, *refs):
    out, blocks, pages_a, pages_b, held, notes, codes, sems, load_sems, note_sem = refs[-10:]
    count = held.shape[0]
    pieces = refs[: count // 8]
    loads = [
        pltpu.make_async_copy(source, target, load_sems.at[n])
        for n, (source, target) in enumerate(
            [(piece, blocks.at[pl.ds(8 * n, 8)]) for n, piece in enumerate(pieces)]
            + [(pages_a_in, pages_a), (pages_b_in, pages_b)]
        )
    ]
    for load in loads:
        load.start()
    row = lax.broadcasted_iota(jnp.int32, (16, 128), 0)
    offset = lax.broadcasted_iota(jnp.int32, (16, 128), 1) - row
    sub = lax.broadcasted_iota(jnp.int32, (8, 128), 0)
    ones = jnp.ones((PAGE, HD), BF16)
    for load in loads[: len(pieces)]:
        load.wait()
    lane = lax.broadcasted_iota(jnp.int32, (8, 128), 1)
    words = jnp.zeros((8, 128), F32)
    for i in range(count):
        sent = blocks[i, TOK : TOK + 8, :128].astype(F32)
        mine = jnp.sum(jnp.where(lane == place[0], sent, 0.0), axis=1, keepdims=True)
        words = jnp.where(lane == i, mine, words)
    notes[...] = words.astype(jnp.int32)
    note_copy = pltpu.make_async_copy(notes, codes, note_sem)
    note_copy.start()
    for load in loads[len(pieces) :]:
        load.wait()
    note_copy.wait()

    def copy(i):
        return pltpu.make_async_copy(held.at[i], out.at[chip_of[i]], sems.at[i])

    def step(i, carry):
        pa, pb = page_a[i], page_b[i]
        code = [codes[j, i] for j in range(SLOTS)]
        first = [pl.multiple_of((c & 7) * 16, 16) for c in code]
        bias = jnp.concatenate(
            [
                jnp.concatenate(
                    [
                        jnp.full((16, PAGE), jnp.where((c & bit) != 0, 0.0, NEG), F32)
                        for bit in (8, 16)
                    ],
                    axis=1,
                )
                for c in code
            ],
            axis=0,
        )
        mine = [offset == jnp.where(c >= 8, (c & 7) * 16, -1024) for c in code]
        scores = []
        for head in range(HEADS):
            cols = slice(head * HD, (head + 1) * HD)
            query = jnp.concatenate(
                [blocks[i, pl.ds(first[j], 16), cols] for j in range(SLOTS)], axis=0
            )
            key = jnp.concatenate([pages_a[pa, 0, :, cols], pages_b[pb, 0, :, cols]], axis=0)
            scores.append(
                lax.dot_general(
                    query, key, (((1,), (1,)), ((), ())), preferred_element_type=F32
                )
                + bias
            )
        tops = [jnp.max(s, axis=1, keepdims=True) for s in scores]
        probs = [
            jnp.exp2((s - t) * (SCALE * LOG2E)).astype(BF16) for s, t in zip(scores, tops)
        ]
        boths = []
        for head in range(HEADS):
            cols = slice(head * HD, (head + 1) * HD)
            value_1 = jnp.concatenate(
                [
                    jnp.concatenate([pages_a[pa, 1, :, cols], ones], axis=1),
                    jnp.concatenate([pages_b[pb, 1, :, cols], ones], axis=1),
                ],
                axis=0,
            )
            boths.append(jnp.dot(probs[head], value_1, preferred_element_type=F32))
        sums = []
        for head in range(HEADS):
            total = boths[head][:, HD:]
            got = boths[head][:, :HD] / total
            held[i, head * ROWS : (head + 1) * ROWS, :] = got.astype(BF16)
            total = tops[head] * SCALE + jnp.log(total)
            here = jnp.where(mine[0], total[:16], NEG)
            for j in range(1, SLOTS):
                here = jnp.maximum(here, jnp.where(mine[j], total[16 * j : 16 * j + 16], NEG))
            sums.append(jnp.max(here, axis=0, keepdims=True))
        tile = by_head(sums)
        high = tile.astype(BF16).astype(F32)
        rest = tile - high
        middle = rest.astype(BF16).astype(F32)
        upper = jnp.where(sub < HEADS, high, middle)
        lower = jnp.where(sub < HEADS, rest - middle, 0.0)
        held[i, STAT:BLOCK, :] = jnp.concatenate([upper, lower], axis=0).astype(BF16)
        copy(i).start()
        return carry

    lax.fori_loop(0, count, step, 0, unroll=4)
    lax.fori_loop(0, count, lambda i, carry: (copy(i).wait(), carry)[1], 0)


def page_attention(here, chip_of, page_a, page_b, pages_a, pages_b, pieces, last):
    count = 8 * len(pieces)
    before = [] if last is None else [last]
    return pl.pallas_call(
        page_kernel,
        out_shape=jax.ShapeDtypeStruct((NCHIP, BLOCK, HD), BF16),
        in_specs=[smem()] * 4 + [hbm()] * (2 + len(pieces) + len(before)),
        out_specs=hbm(),
        input_output_aliases={6 + len(pieces): 0} if before else {},
        scratch_shapes=[
            pltpu.VMEM((count, *pieces[0].shape[1:]), BF16),
            pltpu.VMEM(pages_a.shape, BF16),
            pltpu.VMEM(pages_b.shape, BF16),
            pltpu.VMEM((count, BLOCK, HD), BF16),
            pltpu.VMEM((8, 128), jnp.int32),
            pltpu.SMEM((8, 128), jnp.int32),
            pltpu.SemaphoreType.DMA((count,)),
            pltpu.SemaphoreType.DMA((2 + len(pieces),)),
            pltpu.SemaphoreType.DMA,
        ],
        compiler_params=pltpu.CompilerParams(vmem_limit_bytes=62 << 20),
        cost_estimate=pl.CostEstimate(
            flops=count * HEADS * 16 * ROWS * HD * HD,
            bytes_accessed=5 << 20,
            transcendentals=count * HEADS * ROWS * 2 * PAGE,
        ),
        name="page_attention",
    )(here, chip_of, page_a, page_b, pages_a, pages_b, *pieces, *before)


def smem():
    return pl.BlockSpec(memory_space=pltpu.SMEM)


def hbm():
    return pl.BlockSpec(memory_space=pltpu.HBM)


def vmem():
    return pl.BlockSpec(memory_space=pltpu.VMEM)


def own_kernel(request_col, request_row, queries, keys, values, out_hbm, total_hbm, out, total, sems):
    token = lax.broadcasted_iota(jnp.int32, (TOK, TOK), 0)
    key = lax.broadcasted_iota(jnp.int32, (TOK, TOK), 1)
    mask = (request_col[...] == request_row[...]) & (key <= token)
    ones = jnp.ones((TOK, HD), BF16)
    sums = []
    for head in range(HEADS):
        cols = slice(head * HD, (head + 1) * HD)
        got, low = attend(
            queries[:, cols],
            keys[:, cols].T,
            jnp.concatenate([values[:, cols], ones], axis=1),
            lambda s: jnp.where(mask, s, NEG),
        )
        out[head] = got
        sums.append(jnp.max(jnp.where(token == key, low, NEG), axis=0, keepdims=True))
    total[...] = by_head(sums)
    copies = [
        pltpu.make_async_copy(out, out_hbm, sems.at[0]),
        pltpu.make_async_copy(total, total_hbm, sems.at[1]),
    ]
    for copy in copies:
        copy.start()
    for copy in copies:
        copy.wait()


def own_attention(request_ids, queries, keys, values):
    return pl.pallas_call(
        own_kernel,
        out_shape=(
            jax.ShapeDtypeStruct((HEADS, TOK, HD), F32),
            jax.ShapeDtypeStruct((8, TOK), F32),
        ),
        in_specs=[vmem()] * 5,
        out_specs=(hbm(), hbm()),
        scratch_shapes=[
            pltpu.VMEM((HEADS, TOK, HD), F32),
            pltpu.VMEM((8, TOK), F32),
            pltpu.SemaphoreType.DMA((2,)),
        ],
        compiler_params=pltpu.CompilerParams(vmem_limit_bytes=62 << 20),
        cost_estimate=pl.CostEstimate(
            flops=64 << 20, bytes_accessed=1 << 20, transcendentals=HEADS * TOK * TOK
        ),
        name="own_attention",
    )(request_ids[:, None], request_ids[None, :], queries, keys, values)


def merge_kernel(
    here, codes, arrived_in, own_in, own_sums_in, out, acc, tiles, arrived, own, own_sums, sems
):
    part = NCHIP // MERGE_PARTS
    loads = [
        pltpu.make_async_copy(own_sums_in, own_sums, sems.at[0]),
        pltpu.make_async_copy(own_in, own, sems.at[1]),
    ] + [
        pltpu.make_async_copy(
            arrived_in.at[pl.ds(i * part, part)], arrived.at[pl.ds(i * part, part)], sems.at[2 + i]
        )
        for i in range(MERGE_PARTS)
    ]
    for load in loads:
        load.start()
    row = lax.broadcasted_iota(jnp.int32, (16, TOK), 0)
    offset = lax.broadcasted_iota(jnp.int32, (16, TOK), 1) - row

    def halves(tile):
        high = tile.astype(BF16).astype(F32)
        return high, tile - high

    def on_rows(parts, masks):
        blocks = []
        for head in range(HEADS):
            for mask in masks:
                blocks.append(
                    jnp.concatenate(
                        [
                            jnp.where(mask, jnp.broadcast_to(p[head : head + 1], (16, TOK)), 0.0)
                            for p in parts
                        ],
                        axis=1,
                    )
                )
        picked = jnp.concatenate(blocks, axis=0).astype(BF16)
        ones = jnp.ones((len(parts) * TOK, HD), BF16)
        return jnp.dot(picked, ones, preferred_element_type=F32)

    def collect(p, top):
        tile = arrived[p, STAT:BLOCK, :].astype(F32)
        tile = (tile[:8] + pltpu.roll(tile[:8], HEADS, 0)) + tile[8:]
        tiles[p] = tile
        return jnp.maximum(top, tile)

    loads[0].wait()
    top = own_sums[...]
    for i in range(MERGE_PARTS):
        loads[2 + i].wait()
        top = lax.fori_loop(i * part, (i + 1) * part, collect, top, unroll=4)
    loads[1].wait()
    whole = [offset == 16 * g for g in range(TOK // 16)]
    share = jnp.exp(own_sums[...] - top)
    acc[...] = own[...] * on_rows(halves(share), whole).reshape(HEADS, TOK, HD)

    def add(p, low):
        share = jnp.exp(tiles[p] - top).astype(BF16).astype(F32)
        code = [codes[j, p * NC + here[0] % NC] for j in range(SLOTS)]
        masks = [offset == jnp.where(c >= 8, (c & 7) * 16, -1024) for c in code]
        factor = on_rows((share,), masks)
        for j in range(SLOTS):
            at = pl.ds(pl.multiple_of((code[j] & 7) * 16, 16), 16)
            for head in range(HEADS):
                start = head * ROWS + 16 * j
                part = arrived[p, start : start + 16, :].astype(F32)
                acc[head, at, :] += part * factor[start : start + 16]
        return low + share

    low = lax.fori_loop(0, NCHIP, add, share, unroll=8)
    factor = on_rows(halves(1.0 / low), whole)
    for head in range(HEADS):
        out[:, head * HD : (head + 1) * HD] = (
            acc[head] * factor[head * TOK : (head + 1) * TOK]
        ).astype(BF16)


def merge_attention(here, codes, arrived, own, own_sums):
    return pl.pallas_call(
        merge_kernel,
        out_shape=jax.ShapeDtypeStruct((TOK, HEADS * HD), BF16),
        in_specs=[smem()] * 2 + [hbm()] * 3,
        out_specs=vmem(),
        scratch_shapes=[
            pltpu.VMEM((HEADS, TOK, HD), F32),
            pltpu.VMEM((NCHIP, 8, TOK), F32),
            pltpu.VMEM((NCHIP, BLOCK, HD), BF16),
            pltpu.VMEM((HEADS, TOK, HD), F32),
            pltpu.VMEM((8, TOK), F32),
            pltpu.SemaphoreType.DMA((2 + MERGE_PARTS,)),
        ],
        compiler_params=pltpu.CompilerParams(vmem_limit_bytes=62 << 20),
        cost_estimate=pl.CostEstimate(
            flops=64 << 20, bytes_accessed=4 << 20, transcendentals=1 << 18
        ),
        name="merge_attention",
    )(here, codes, arrived, own, own_sums)


def project_kernel(
    side,
    att,
    att_far,
    weight_in,
    weight_mine,
    weight_other,
    residual_in,
    gain,
    picks_in,
    mixed,
    sent,
    both,
    kept,
    rows,
    weight,
    weight_far,
    residual,
    picks,
    load_sems,
    sems,
):
    part = weight_mine.shape[0]
    loads = [
        pltpu.make_async_copy(source, target, load_sems.at[n])
        for n, (source, target) in enumerate(
            (
                (weight_in, weight),
                (residual_in, residual),
                (weight_mine, weight_far.at[pl.ds(pl.multiple_of(side[1] * part, part), part)]),
                (weight_other, weight_far.at[pl.ds(pl.multiple_of(side[2] * part, part), part)]),
                (picks_in, picks),
            )
        )
    ]
    for load in loads:
        load.start()
    half = residual.shape[1] // 2
    steps, step = rows.shape[0], rows.shape[1]
    loads[0].wait()
    total = jnp.dot(att[...], weight[...], preferred_element_type=F32)
    loads[1].wait()
    total += residual[...].astype(F32)
    loads[2].wait()
    loads[3].wait()
    total += jnp.dot(att_far[...], weight_far[...], preferred_element_type=F32)
    kept[...] = jnp.where(side[0] == 0, total[:, :half], total[:, half:])
    keep = pltpu.make_async_copy(kept, mixed, sems.at[steps])
    keep.start()
    scale = lax.rsqrt(jnp.mean(total * total, axis=1, keepdims=True) + NORM_EPS)
    normed = (total * scale * gain[...]).astype(BF16)
    both[:TOK] = normed[:, :half]
    both[TOK:] = normed[:, half:]
    copies = []
    loads[4].wait()
    for i in range(steps):
        rows[i] = jnp.dot(
            picks[i * step : (i + 1) * step], both[...], preferred_element_type=F32
        ).astype(BF16)
        copies.append(
            pltpu.make_async_copy(rows.at[i], sent.at[pl.ds(i * step, step)], sems.at[i])
        )
        copies[-1].start()
    keep.wait()
    for copy in copies:
        copy.wait()


def project(side, att, att_far, weight, weight_mine, weight_other, residual, gain, picks, steps=4):
    width = residual.shape[1]
    step = picks.shape[0] // steps
    return pl.pallas_call(
        project_kernel,
        out_shape=(
            jax.ShapeDtypeStruct((TOK, width // 2), F32),
            jax.ShapeDtypeStruct((picks.shape[0], width // 2), BF16),
        ),
        in_specs=[smem(), vmem(), vmem(), hbm(), hbm(), hbm(), hbm(), vmem(), hbm()],
        out_specs=(hbm(), hbm()),
        scratch_shapes=[
            pltpu.VMEM((2 * TOK, width // 2), BF16),
            pltpu.VMEM((TOK, width // 2), F32),
            pltpu.VMEM((steps, step, width // 2), BF16),
            pltpu.VMEM(weight.shape, BF16),
            pltpu.VMEM((2 * weight_mine.shape[0], width), BF16),
            pltpu.VMEM(residual.shape, BF16),
            pltpu.VMEM(picks.shape, BF16),
            pltpu.SemaphoreType.DMA((5,)),
            pltpu.SemaphoreType.DMA((steps + 1,)),
        ],
        compiler_params=pltpu.CompilerParams(vmem_limit_bytes=62 << 20),
        cost_estimate=pl.CostEstimate(
            flops=4 * TOK * 512 * width + 2 * picks.shape[0] * 256 * width // 2,
            bytes_accessed=10 << 20,
            transcendentals=TOK,
        ),
        name="project_dispatch",
    )(side, att, att_far, weight, weight_mine, weight_other, residual, gain, picks)


def expert_kernel(rows, gate, up, down, out, rows_v, gate_v, up_v, down_v, out_v, sems, back):
    steps, count = rows_v.shape[0], rows_v.shape[1]
    width = gate.shape[0]
    half, quarter = width // 2, width // 4

    def fetch(i):
        return pltpu.make_async_copy(rows.at[pl.ds(i * count, count)], rows_v.at[i], sems.at[i])

    def send(i):
        return pltpu.make_async_copy(out_v.at[i], out.at[pl.ds(i * count, count)], back.at[i])

    loads = [
        pltpu.make_async_copy(src, dst, sems.at[steps + n])
        for n, (src, dst) in enumerate(((gate, gate_v), (up, up_v), (down, down_v)))
    ]
    fetch(0).start()
    for load in loads:
        load.start()
    for i in range(1, steps):
        fetch(i).start()
    low_half = lax.broadcasted_iota(jnp.int32, (count // 2, 8, half), 1) < 4
    low_quarter = lax.broadcasted_iota(jnp.int32, (count // 2, 8, quarter), 1) < 4
    def step(i, carry):
        fetch(i).wait()
        wide = rows_v[i].astype(F32)
        tail = wide[:, 16:24].reshape(count // 2, 2, 8, half)
        even, odd = tail[:, 0], tail[:, 1]
        tail_0 = jnp.where(low_half, even, pltpu.roll(odd, 4, 1))
        tail_1 = jnp.where(low_half, pltpu.roll(even, 4, 1), odd)
        left = jnp.concatenate(
            [wide[:, 0:8].reshape(count * 8, half), tail_0.reshape(count * 4, half)], axis=0
        )
        right = jnp.concatenate(
            [wide[:, 8:16].reshape(count * 8, half), tail_1.reshape(count * 4, half)], axis=0
        )
        tokens = jnp.concatenate([left.astype(BF16), right.astype(BF16)], axis=1)
        if i == 0:
            loads[0].wait()
        gate_act = jnp.dot(tokens, gate_v[...], preferred_element_type=F32)
        if i == 0:
            loads[1].wait()
        up_act = jnp.dot(tokens, up_v[...], preferred_element_type=F32)
        hidden = (gate_act / (1.0 + jnp.exp(-gate_act)) * up_act).astype(BF16)
        if i == 0:
            loads[2].wait()
        result = jnp.dot(hidden, down_v[...], preferred_element_type=F32)
        for side in range(2):
            cols = [slice((2 * side + q) * quarter, (2 * side + q + 1) * quarter) for q in range(2)]
            main = [result[: count * 8, c].reshape(count, 8, quarter) for c in cols]
            tail = [result[count * 8 :, c].reshape(count // 2, 8, quarter) for c in cols]
            even = jnp.where(low_quarter, tail[0], pltpu.roll(tail[1], 4, 1))
            odd = jnp.where(low_quarter, pltpu.roll(tail[0], 4, 1), tail[1])
            last = jnp.stack([even, odd], axis=1).reshape(count, 8, quarter)
            out_v[i, :, side] = jnp.concatenate(main + [last], axis=1).astype(BF16)
        send(i).start()
        return carry

    for i in range(steps):
        step(i, 0)
    for i in range(steps):
        send(i).wait()


def run_expert(rows, gate, up, down, steps=4):
    count = rows.shape[0] // steps
    width, hidden = gate.shape
    return pl.pallas_call(
        expert_kernel,
        out_shape=jax.ShapeDtypeStruct((rows.shape[0], 2, 2 * CAP, width // 4), BF16),
        in_specs=[hbm()] * 4,
        out_specs=hbm(),
        scratch_shapes=[
            pltpu.VMEM((steps, count, 2 * CAP, width // 2), BF16),
            pltpu.VMEM((width, hidden), BF16),
            pltpu.VMEM((width, hidden), BF16),
            pltpu.VMEM((hidden, width), BF16),
            pltpu.VMEM((steps, count, 2, 2 * CAP, width // 4), BF16),
            pltpu.SemaphoreType.DMA((steps + 3,)),
            pltpu.SemaphoreType.DMA((steps,)),
        ],
        compiler_params=pltpu.CompilerParams(vmem_limit_bytes=62 << 20),
        cost_estimate=pl.CostEstimate(
            flops=6 * rows.shape[0] * CAP * width * hidden,
            bytes_accessed=15 << 20,
            transcendentals=rows.shape[0] * CAP * hidden,
        ),
        name="expert",
    )(rows, gate, up, down)


def combine_kernel(mixed, shares, rows, out, mixed_v, shares_v, rows_v, sems):
    parts, depth, width = rows_v.shape
    loads = [
        pltpu.make_async_copy(rows.at[pl.ds(i * depth, depth)], rows_v.at[i], sems.at[i])
        for i in range(parts)
    ]
    share_load = pltpu.make_async_copy(shares, shares_v, sems.at[parts])
    mixed_load = pltpu.make_async_copy(mixed, mixed_v, sems.at[parts + 1])
    share_load.start()
    for load in loads:
        load.start()
    mixed_load.start()
    share_load.wait()
    total = jnp.zeros((shares_v.shape[0], width), F32)
    for i in range(parts):
        loads[i].wait()
        total += jnp.dot(
            shares_v[:, i * depth : (i + 1) * depth], rows_v[i], preferred_element_type=F32
        )
    mixed_load.wait()
    out[:, :width] = (mixed_v[:, :width] + total[:TOK]).astype(BF16)
    out[:, width:] = (mixed_v[:, width:] + total[TOK:]).astype(BF16)


def combine(mixed, shares, rows, parts=4):
    return pl.pallas_call(
        combine_kernel,
        out_shape=jax.ShapeDtypeStruct(mixed.shape, BF16),
        in_specs=[hbm()] * 3,
        out_specs=vmem(),
        scratch_shapes=[
            pltpu.VMEM(mixed.shape, F32),
            pltpu.VMEM(shares.shape, BF16),
            pltpu.VMEM((parts, rows.shape[0] // parts, rows.shape[1]), BF16),
            pltpu.SemaphoreType.DMA((parts + 2,)),
        ],
        compiler_params=pltpu.CompilerParams(vmem_limit_bytes=62 << 20),
        cost_estimate=pl.CostEstimate(
            flops=2 * shares.shape[0] * rows.shape[0] * rows.shape[1],
            bytes_accessed=6 << 20,
            transcendentals=0,
        ),
        name="combine",
    )(mixed, shares, rows)


def slot_rows():
    slot = np.array(list(range(8)) * 2 + list(range(8, 12)) * 2, np.int32)
    part = np.array([0] * 8 + [1] * 8 + [0] * 4 + [1] * 4, np.int32)
    return slot, part


def routing(expert_ids, expert_weights):
    flat = expert_ids.reshape(-1)
    count = flat.shape[0]
    onehot = (flat[:, None] == jnp.arange(NREQ, dtype=jnp.int32)[None, :]).astype(BF16)
    earlier = (
        jnp.arange(count, dtype=jnp.int32)[None, :] < jnp.arange(count, dtype=jnp.int32)[:, None]
    ).astype(BF16)
    before = jnp.dot(earlier, onehot, preferred_element_type=F32)
    slot = jnp.sum(before * onehot.astype(F32), axis=1).astype(jnp.int32)
    place = (flat * CAP + slot).reshape(TOK, TOP)

    slot_at, part_at = slot_rows()
    row_place = (np.arange(NREQ, dtype=np.int32)[:, None] * CAP + slot_at[None, :]).reshape(-1)
    row_part = np.tile(part_at, NREQ)
    col_place = jnp.concatenate([place, place], axis=0)
    col_part = np.repeat(np.arange(2, dtype=np.int32), TOK)
    hit = jnp.zeros((row_place.shape[0], 2 * TOK), jnp.bool_)
    for k in range(TOP):
        hit = hit | (col_place[None, :, k] == row_place[:, None])
    picks = (hit & (row_part[:, None] == col_part[None, :])).astype(BF16)

    back_place = np.repeat(row_place.reshape(NREQ, 1, -1), 2, axis=1).reshape(-1)
    back_part = np.tile(part_at, 2 * NREQ)
    col_weight = jnp.concatenate([expert_weights, expert_weights], axis=0)
    shares = jnp.zeros((2 * TOK, back_place.shape[0]), F32)
    for k in range(TOP):
        shares = shares + jnp.where(
            col_place[:, k, None] == back_place[None, :], col_weight[:, k, None], 0.0
        )
    shares = jnp.where(back_part[None, :] == col_part[:, None], shares, 0.0)
    return picks, shares.astype(BF16)


def note_kernel(ids, users, queries, block, codes, wide):
    lane = lax.broadcasted_iota(jnp.int32, (8, 128), 1)
    slot = lax.broadcasted_iota(jnp.int32, (8, 128), 0)
    wide[...] = jnp.full((8, 128), -1, jnp.int32)
    wide[:1, : users.shape[1]] = users[...]
    user = jnp.broadcast_to(wide[:1], (8, 128))
    other = jnp.where(lane % 2 == 0, pltpu.roll(user, 127, 1), pltpu.roll(user, 1, 1))
    rank = jnp.zeros((8, 128), jnp.int32)
    total = jnp.zeros((8, 128), jnp.int32)
    for group in range(TOK // 16):
        mine = user == ids[group * 16]
        theirs = other == ids[group * 16]
        value = group + jnp.where(mine, 8, 0) + jnp.where(theirs, 16, 0)
        needed = mine | theirs
        total = jnp.where(needed & (rank == slot), value, total)
        rank = rank + jnp.where(needed, 1, 0)
    codes[...] = total
    block[:TOK] = queries[...]
    block[TOK:] = jnp.zeros((8, block.shape[1]), BF16)
    block[TOK:, :128] = total.astype(F32).astype(BF16)


def make_block(ids, users, queries):
    return pl.pallas_call(
        note_kernel,
        out_shape=(
            jax.ShapeDtypeStruct((TOK + 8, queries.shape[1]), BF16),
            jax.ShapeDtypeStruct((8, 128), jnp.int32),
        ),
        in_specs=[smem(), vmem(), vmem()],
        out_specs=(vmem(), vmem()),
        scratch_shapes=[pltpu.VMEM((8, 128), jnp.int32)],
        compiler_params=pltpu.CompilerParams(vmem_limit_bytes=62 << 20),
        cost_estimate=pl.CostEstimate(flops=1 << 16, bytes_accessed=1 << 18, transcendentals=0),
        name="make_block",
    )(ids, users, queries)


def shards(
    residual,
    queries,
    new_keys,
    new_values,
    request_ids,
    page_store,
    page_sends,
    page_users,
    expert_ids,
    expert_weights,
    output_weight,
    norm_gain,
    gate_weight,
    up_weight,
    down_weight,
):
    me = lax.axis_index("req")
    width = residual.shape[1]
    half = width // 2
    swap = [(0, 1), (1, 0)]

    core = me % NC
    pages_far = lax.ppermute(page_store, "req", perm_core())
    sends_far = lax.ppermute(page_sends, "req", perm_core())
    block, codes = make_block(request_ids, page_users, queries)
    near = lax.ppermute(block, "req", perm_x())
    line_a = ring_line(block)
    near, line_a, pages_far, sends_far, weight = lax.optimization_barrier(
        (near, line_a, pages_far, sends_far, output_weight)
    )
    line = stack_blocks(line_a + ring_line(near))
    far_rows = weight.shape[0] // NC
    far_part = lax.dynamic_slice_in_dim(weight, core * far_rows, far_rows, 0)
    weight_mine = lax.ppermute(far_part, "tp", swap)

    chips = lax.dynamic_index_in_dim(jnp.asarray(chip_table()), me, 0, keepdims=False)
    page_a = page_sends[0][chips * NC + core]
    page_b = sends_far[0][chips * NC + core]
    line, chips, page_a, page_b = lax.optimization_barrier((line, chips, page_a, page_b))
    pieces = [line] + ring_rest(line)
    own, own_sums = own_attention(request_ids, queries, new_keys, new_values)
    picks, shares = routing(expert_ids, expert_weights)

    parts = None
    for first, last in ((0, 1), (1, 4)):
        group = pieces[first:last]
        if first:
            group, parts = lax.optimization_barrier((group, parts))
        rows = slice(8 * first, 8 * last)
        parts = page_attention(
            me[None], chips[rows], page_a[rows], page_b[rows], page_store, pages_far, group, parts
        )
    parts, weight_mine = lax.optimization_barrier((parts, weight_mine))
    weight_other = lax.ppermute(weight_mine, "req", perm_core())
    arrived = lax.all_to_all(
        parts, "req", 0, 0, tiled=True, axis_index_groups=core_groups()
    )
    own, picks, weight_other = lax.optimization_barrier((own, picks, weight_other))
    attended = merge_attention(me[None], codes, arrived, own, own_sums)
    attended_far = lax.ppermute(attended, "tp", swap)
    mixed, sent = project(
        jnp.stack([lax.axis_index("tp"), core, 1 - core]),
        attended,
        attended_far,
        output_weight,
        weight_mine,
        weight_other,
        residual,
        norm_gain[None, :],
        picks,
    )
    rows = lax.all_to_all(sent.reshape(NREQ, 2 * CAP, half), "req", 0, 0, tiled=True)
    result = run_expert(rows, gate_weight[0], up_weight[0], down_weight[0])
    returned = lax.all_to_all(
        result.reshape(2 * NREQ, 2 * CAP, width // 4), ("req", "tp"), 0, 0, tiled=True
    )
    return combine(mixed, shares, returned.reshape(-1, width // 4))


def solution(mesh):
    placed = (
        P("req", None),
        P("req", "tp"),
        P("req", "tp"),
        P("req", "tp"),
        P("req"),
        P("req", None, None, "tp"),
        P("req", None),
        P("req", None),
        P("req", None),
        P("req", None),
        P("tp", None),
        P(),
        P("req", None, "tp"),
        P("req", None, "tp"),
        P("req", "tp", None),
    )
    return jax.shard_map(
        shards, mesh=mesh, in_specs=placed, out_specs=P("req", "tp"), check_vma=False
    )
```
